32 devices in a mesh: dp: 8 (over y, x, core), seq: 4 (over z).
Axes of the slice: x: 2, y: 2, z: 4, core: 2. Of those that a mesh axis runs over, the one named last changes fastest.
Arguments:
- layer_input: bfloat16 [16, 512, 768], P('dp', 'seq'), may hold values from -6 to 6
- segment_ids: int32 [16, 512], P('dp', 'seq'), may hold values from 0 to 2, as said below
- w_query: bfloat16 [768, 768], replicated, may hold values from -0.21875 to 0.21875
- b_query: float32 [768], replicated, may hold values from -1.5 to 1.5
- w_key: bfloat16 [768, 768], replicated, may hold values from -0.21875 to 0.21875
- w_value: bfloat16 [768, 768], replicated, may hold values from -0.21875 to 0.21875
- b_value: float32 [768], replicated, may hold values from -1.5 to 1.5
- w_out: bfloat16 [768, 768], replicated, may hold values from -1.75 to 1.75
- b_out: float32 [768], replicated, may hold values from -1.5 to 1.5
- gain_one: float32 [768], replicated, may hold values from 0.5 to 1.5
- shift_one: float32 [768], replicated, may hold values from -1.5 to 1.5
- w_inner: bfloat16 [768, 3072], replicated, may hold values from -0.21875 to 0.21875
- b_inner: float32 [3072], replicated, may hold values from -1.5 to 1.5
- w_outer: bfloat16 [3072, 768], replicated, may hold values from -0.109375 to 0.109375
- b_outer: float32 [768], replicated, may hold values from -1.5 to 1.5
- gain_two: float32 [768], replicated, may hold values from 0.5 to 1.5
- shift_two: float32 [768], replicated, may hold values from -1.5 to 1.5
- cotangent: bfloat16 [16, 512, 768], P('dp', 'seq'), may hold values from -6 to 6
Outputs:
- output: bfloat16 [16, 512, 768], P('dp', 'seq')
- d_input: bfloat16 [16, 512, 768], P('dp', 'seq')
- d_w_query: float32 [768, 768], replicated
- d_b_query: float32 [768], replicated
- d_w_key: float32 [768, 768], replicated
- d_w_value: float32 [768, 768], replicated
- d_b_value: float32 [768], replicated
- d_w_out: float32 [768, 768], replicated
- d_b_out: float32 [768], replicated
- d_gain_one: float32 [768], replicated
- d_shift_one: float32 [768], replicated
- d_w_inner: float32 [768, 3072], replicated
- d_b_inner: float32 [3072], replicated
- d_w_outer: float32 [3072, 768], replicated
- d_b_outer: float32 [768], replicated
- d_gain_two: float32 [768], replicated
- d_shift_two: float32 [768], replicated
The draws below stay inside these ranges and needn't reach their ends.
Inputs may be any that keep to these rules, and one draw needn't show every extreme that they name: `segment_ids`: each row holds either one pair (ids 1, then 0 for padding at its end) of more than 256 tokens, or two pairs packed in halves of 256 positions (ids 1 in the first half, 2 in the second, each followed by padding 0 in its half), each of 128 tokens or more. Some row is a single pair without padding, some row is packed with padding.
All inputs are finite; a program needn't handle non-finite values.
Results may differ from the reference program's by a relative error of at most 0.015.
Values may be sent and summed in bfloat16 or wider, within the bound.
A program may use at most 192 MiB of HBM per device.

```python
import math
import jax
import jax.numpy as jnp
from jax import lax

D = 768
H = 12
HD = 64
FF = 3072
LENGTH = 512
ROWS = 16


def draw_segment_ids(key, part):
    half_len = LENGTH // 2
    key_one, key_two, key_three, key_four = jax.random.split(jax.random.fold_in(key, 17), 4)
    packed = jax.random.randint(key_one, (ROWS,), 0, 2)
    packed = packed.at[0].set(0).at[ROWS - 1].set(1)
    single_len = jax.random.randint(key_two, (ROWS,), half_len + 1, LENGTH + 1)
    single_len = single_len.at[0].set(LENGTH)
    first_len = jax.random.randint(key_three, (ROWS,), half_len // 2, half_len + 1)
    first_len = first_len.at[ROWS - 1].set(half_len // 2)
    second_len = jax.random.randint(key_four, (ROWS,), half_len // 2, half_len + 1)
    places = jnp.arange(LENGTH, dtype=jnp.int32)[None, :]
    single_ids = jnp.where(places < single_len[:, None], 1, 0)
    first_ids = jnp.where(places < first_len[:, None], 1, 0)
    second_ids = jnp.where(places - half_len < second_len[:, None], 2, 0)
    packed_ids = jnp.where(places < half_len, first_ids, second_ids)
    return jnp.where(packed[:, None] == 1, packed_ids, single_ids).astype(jnp.int32)


def block_scale(key, dims, cuts, low, top_value):
    loudness = 1.0
    for axis_at, shards_of in cuts:
        draws = jax.random.uniform(jax.random.fold_in(jax.random.fold_in(key, 6), axis_at), (shards_of,), jnp.float32, low / len(cuts), top_value / len(cuts))
        loudness = loudness * jnp.repeat(jnp.exp(draws), dims[axis_at] // shards_of).reshape((-1,) + (1,) * (len(dims) - 1 - axis_at))
    return loudness


def noise(stream_key, dims, scale, bound, pieces=(), held_as=jnp.bfloat16):
    array = jax.random.normal(stream_key, dims, jnp.float32) * scale
    if len(pieces) > 0:
        array = block_scale(stream_key, dims, pieces, -0.22, 0.18) * array
    return jnp.clip(array, min=-bound, max=bound).astype(held_as)


def setup_inputs(seed: int = 0) -> dict:
    splits = jax.random.split(jax.random.key(seed), 19)
    layer_input = noise(splits[0], (ROWS, LENGTH, D), 1.0, 6.0, ((0, 8), (1, 4)))
    segment_ids = draw_segment_ids(jax.random.fold_in(splits[18], 71), 0)
    w_query = noise(splits[2], (D, D), D ** -0.5, 0.21875)
    b_query = noise(splits[3], (D,), 0.3, 1.5, (), jnp.float32)
    w_key = noise(splits[4], (D, D), D ** -0.5, 0.21875)
    w_value = noise(splits[5], (D, D), D ** -0.5, 0.21875)
    b_value = noise(splits[6], (D,), 0.3, 1.5, (), jnp.float32)
    w_out = noise(splits[7], (D, D), (D // 64) ** -0.5, 1.75)
    b_out = noise(splits[8], (D,), 0.3, 1.5, (), jnp.float32)
    gain_one = jnp.clip(1.0 + 0.1 * jax.random.normal(splits[9], (D,), jnp.float32), 0.5, 1.5)
    shift_one = noise(splits[10], (D,), 0.3, 1.5, (), jnp.float32)
    w_inner = noise(splits[11], (D, FF), D ** -0.5, 0.21875)
    b_inner = noise(splits[12], (FF,), 0.3, 1.5, (), jnp.float32)
    w_outer = noise(splits[13], (FF, D), FF ** -0.5, 0.109375)
    b_outer = noise(splits[14], (D,), 0.3, 1.5, (), jnp.float32)
    gain_two = jnp.clip(1.0 + 0.1 * jax.random.normal(splits[15], (D,), jnp.float32), 0.5, 1.5)
    shift_two = noise(splits[16], (D,), 0.3, 1.5, (), jnp.float32)
    cotangent = noise(splits[17], (ROWS, LENGTH, D), 1.0, 6.0, ((0, 8), (1, 4)))
    return dict(layer_input=layer_input, segment_ids=segment_ids, w_query=w_query, b_query=b_query, w_key=w_key, w_value=w_value, b_value=b_value, w_out=w_out, b_out=b_out, gain_one=gain_one, shift_one=shift_one, w_inner=w_inner, b_inner=b_inner, w_outer=w_outer, b_outer=b_outer, gain_two=gain_two, shift_two=shift_two, cotangent=cotangent)


@jax.custom_vjp
def low(v):
    return lax.optimization_barrier(v.astype(jnp.bfloat16)).astype(jnp.float32)

@jax.custom_vjp
def low_back(v):
    return v

def low_keep(v):
    return (low(v), None)

def low_pass(kept, grad):
    return (grad,)

def back_keep(v):
    return (v, None)

def back_low(kept, grad):
    return (low(grad),)
low.defvjp(low_keep, low_pass)
low_back.defvjp(back_keep, back_low)
EPSILON = 1e-12
MASKED = -1000000000.0
HIGHEST = lax.Precision.HIGHEST
INV_ROOT_TWO = 0.7071067811865476

def product(left, right):
    return jnp.dot(left, right, precision=HIGHEST, preferred_element_type=jnp.float32)

def layer_norm(values, scale_gain, offset):
    centre = values - lax.optimization_barrier(jnp.mean(values, axis=-1, keepdims=True))
    spread = lax.optimization_barrier(jnp.mean(centre * centre, axis=-1, keepdims=True))
    return centre * lax.rsqrt(spread + EPSILON) * scale_gain + offset

def gelu_exact(values):
    return values * 0.5 * (1.0 + lax.erf(values * INV_ROOT_TWO))

def row_block(weights, inputs, segments):
    w_query, b_query, w_key, w_value, b_value, w_out, b_out, gain_one, shift_one, w_inner, b_inner, w_outer, b_outer, gain_two, shift_two = weights
    row_count = inputs.shape[0]
    flat_rows = inputs.reshape(row_count * LENGTH, D)
    query_rows = low(low_back(product(flat_rows, w_query) + b_query)).reshape(row_count, LENGTH, H, HD)
    key_rows = low(low_back(product(flat_rows, w_key))).reshape(row_count, LENGTH, H, HD)
    value_rows = low(low_back(product(flat_rows, w_value) + b_value)).reshape(row_count, LENGTH, H, HD)
    scores = jnp.einsum('bqhd,bkhd->bhqk', query_rows, key_rows, precision=HIGHEST) * 0.125
    same_pair = segments[:, None, :, None] == segments[:, None, None, :]
    scores = low_back(jnp.where(same_pair, scores, MASKED))
    row_max = lax.optimization_barrier(jnp.max(scores, axis=-1, keepdims=True))
    powers = jnp.exp(scores - row_max)
    soft_probs = powers / lax.optimization_barrier(jnp.sum(powers, axis=-1, keepdims=True))
    attended = jnp.einsum('bhqk,bkhd->bqhd', low(soft_probs), value_rows, precision=HIGHEST)
    attended = low(low_back(attended.reshape(row_count * LENGTH, D)))
    branch = low_back(product(attended, w_out) + b_out)
    hidden_one = layer_norm(flat_rows + branch, gain_one, shift_one)
    inner_pre = low_back(product(low(hidden_one), w_inner) + b_inner)
    active = low(gelu_exact(inner_pre))
    outer_out = low_back(product(active, w_outer) + b_outer)
    return layer_norm(hidden_one + outer_out, gain_two, shift_two).reshape(row_count, LENGTH, D)

def reference(layer_input, segment_ids, w_query, b_query, w_key, w_value, b_value, w_out, b_out, gain_one, shift_one, w_inner, b_inner, w_outer, b_outer, gain_two, shift_two, cotangent):
    params = tuple((tensor.astype(jnp.float32) for tensor in (w_query, b_query, w_key, w_value, b_value, w_out, b_out, gain_one, shift_one, w_inner, b_inner, w_outer, b_outer, gain_two, shift_two)))
    inputs_full = layer_input.astype(jnp.float32)
    group = math.gcd(ROWS, max(1, 4096 // LENGTH))
    seg_blocks = segment_ids.reshape(ROWS // group, group, LENGTH)

    def forward(inputs, weights):
        blocks = inputs.reshape(ROWS // group, group, LENGTH, D)
        runner = jax.checkpoint(row_block)

        def one_block(packed_item):
            return runner(weights, packed_item[0], packed_item[1])
        result_rows = lax.map(one_block, (blocks, seg_blocks))
        return result_rows.reshape(ROWS, LENGTH, D)
    result, pull = jax.vjp(forward, inputs_full, params)
    grad_input, grads = pull(cotangent.astype(jnp.float32))
    return (result.astype(jnp.bfloat16), grad_input.astype(jnp.bfloat16), grads[0], grads[1], grads[2], grads[3], grads[4], grads[5], grads[6], grads[7], grads[8], grads[9], grads[10], grads[11], grads[12], grads[13], grads[14])
```

```python
import functools

import jax
import jax.numpy as jnp
from jax import lax
from jax.experimental import pallas as pl
from jax.experimental.pallas import tpu as pltpu
from jax.sharding import PartitionSpec as P

HD = 64
EPSILON = 1e-12
MASKED = -1000000000.0
INV_ROOT_TWO = 0.7071067811865476
DENSITY = 0.3989422804014327
MESH = pl.DeviceIdType.MESH
BF16 = jnp.bfloat16
F32 = jnp.float32


def product(left, right):
    return jnp.dot(left, right, preferred_element_type=F32)


def product_tn(left, right):
    return lax.dot_general(left, right, (((0,), (0,)), ((), ())), preferred_element_type=F32)


def product_nt(left, right):
    return lax.dot_general(left, right, (((1,), (1,)), ((), ())), preferred_element_type=F32)


def place(seq_size):
    dp, sq = lax.axis_index("dp"), lax.axis_index("seq")
    side = dp % 2
    return dp, sq, side, dp - side


def gather_kernel(seq_size, x_ref, cot_ref, seg_ref, xf_ref, ct_ref, sg_ref, ss, rs, ls):
    rows, length = x_ref.shape[0], x_ref.shape[1]
    spread = seq_size // 2
    dp, sq, side, pair = place(seq_size)
    half, spot = sq // spread, sq % spread
    own = side * spread * length
    sibling = (dp + 1 - 2 * side, sq)

    def x_copy(r, b, tgt, row0):
        return pltpu.make_async_remote_copy(
            x_ref.at[r], xf_ref.at[pl.ds(row0, length)], ss.at[0, r], rs.at[0, b], tgt, MESH
        )

    def c_copy(r, b, tgt):
        return pltpu.make_async_remote_copy(
            cot_ref.at[r], ct_ref.at[pl.ds(pl.multiple_of(b * length, length), length)],
            ss.at[1, r], rs.at[1, b], tgt, MESH,
        )

    def s_copy(r, c, at, tgt):
        return pltpu.make_async_remote_copy(
            seg_ref.at[r], sg_ref.at[at], ss.at[2 + c, r], rs.at[2, at], tgt, MESH
        )

    def forward(b):
        row0 = pl.multiple_of(own + b * length, length)
        return pltpu.make_async_remote_copy(
            xf_ref.at[pl.ds(row0, length)], xf_ref.at[pl.ds(row0, length)],
            ss.at[4, b], rs.at[3, b], sibling, MESH,
        )

    for r in range(rows):
        to_seq = rows * side + r
        local = jnp.logical_and(half == side, sq == to_seq)
        row0 = pl.multiple_of((half * spread + spot) * length, length)

        @pl.when(local)
        def _():
            pltpu.make_async_copy(x_ref.at[r], xf_ref.at[pl.ds(row0, length)], ls.at[0, r]).start()
            pltpu.make_async_copy(
                cot_ref.at[r], ct_ref.at[pl.ds(pl.multiple_of(spot * length, length), length)], ls.at[1, r]
            ).start()

        @pl.when(jnp.logical_not(local))
        def _():
            x_copy(r, spot, (pair + half, to_seq), row0).start()

        for c in range(2):
            mine = jnp.logical_and(side == c, sq == to_seq)

            @pl.when(mine)
            def _():
                pltpu.make_async_copy(seg_ref.at[r], sg_ref.at[sq], ls.at[2, r]).start()

            @pl.when(jnp.logical_not(mine))
            def _():
                s_copy(r, c, sq, (pair + c, to_seq)).start()

    for r in range(rows):
        to_seq = rows * side + r
        local = jnp.logical_and(half == side, sq == to_seq)

        @pl.when(jnp.logical_not(local))
        def _():
            c_copy(r, spot, (pair + half, to_seq)).start()

    for b in range(spread):
        local = jnp.logical_and(sq // rows == side, side * spread + b == sq)

        @pl.when(local)
        def _():
            row0 = pl.multiple_of(own + b * length, length)
            pltpu.make_async_copy(x_ref.at[b], xf_ref.at[pl.ds(row0, length)], ls.at[0, sq % rows]).wait()

        @pl.when(jnp.logical_not(local))
        def _():
            x_copy(0, b, sibling, pl.multiple_of(own + b * length, length)).wait_recv()

        forward(b).start()

    for b in range(spread):
        local = jnp.logical_and(sq // rows == side, side * spread + b == sq)

        @pl.when(local)
        def _():
            pltpu.make_async_copy(
                cot_ref.at[b], ct_ref.at[pl.ds(pl.multiple_of(b * length, length), length)], ls.at[1, sq % rows]
            ).wait()

        @pl.when(jnp.logical_not(local))
        def _():
            c_copy(0, b, sibling).wait_recv()

        other = pl.multiple_of((1 - side) * spread * length + b * length, length)
        pltpu.make_async_remote_copy(
            xf_ref.at[pl.ds(other, length)], xf_ref.at[pl.ds(other, length)], ss.at[4, b], rs.at[3, b], sibling, MESH
        ).wait_recv()
        forward(b).wait_send()

    for p in range(seq_size):
        mine = jnp.logical_and(sq // rows == side, p == sq)

        @pl.when(mine)
        def _():
            pltpu.make_async_copy(seg_ref.at[0], sg_ref.at[sq], ls.at[2, sq % rows]).wait()

        @pl.when(jnp.logical_not(mine))
        def _():
            s_copy(0, 0, p, sibling).wait_recv()

    for r in range(rows):
        to_seq = rows * side + r
        local = jnp.logical_and(half == side, sq == to_seq)

        @pl.when(jnp.logical_not(local))
        def _():
            x_copy(r, spot, sibling, 0).wait_send()
            c_copy(r, spot, sibling).wait_send()

        for c in range(2):

            @pl.when(jnp.logical_not(jnp.logical_and(side == c, sq == to_seq)))
            def _():
                s_copy(r, c, sq, sibling).wait_send()


def gather_rows(layer_input, cotangent, segment_ids, seq_size):
    rows, length, width = layer_input.shape
    tokens = seq_size * length
    seg = jnp.broadcast_to(segment_ids[:, None, :], (rows, 8, length))
    vmem = pl.BlockSpec(memory_space=pltpu.VMEM)
    return pl.pallas_call(
        functools.partial(gather_kernel, seq_size),
        out_shape=(
            jax.ShapeDtypeStruct((tokens, width), BF16),
            jax.ShapeDtypeStruct((tokens // 2, width), BF16),
            jax.ShapeDtypeStruct((seq_size, 8, length), jnp.int32),
        ),
        in_specs=[vmem] * 3,
        out_specs=(vmem,) * 3,
        scratch_shapes=[
            pltpu.SemaphoreType.DMA((5, 2)),
            pltpu.SemaphoreType.DMA((4, seq_size)),
            pltpu.SemaphoreType.DMA((3, 2)),
        ],
        compiler_params=pltpu.CompilerParams(has_side_effects=True),
        name="gather_rows",
    )(layer_input, cotangent, seg)


GROUP = 3072
PIECE = 1024
ORDERS = (("x", "y", "z"), ("y", "z", "x"), ("z", "x", "y"))
SUBS = 2


class Exchange:
    def __init__(self, dp_size, seq_size, groups):
        self.dp_size, self.seq_size, self.groups = dp_size, seq_size, groups
        self.extra = []
        bit = 8
        while bit < dp_size:
            self.extra.append(bit)
            bit *= 2
        self.sems = 0
        self.slots = 0
        self.pieces = []
        for g in range(groups):
            for cls in range(3):
                self.pieces.append(self.plan(g * GROUP + cls * PIECE, ORDERS[cls]))

    def sem(self):
        self.sems += 1
        return self.sems - 1

    def slot(self, rows):
        self.slots += rows
        return self.slots - rows

    def plan(self, base, order):
        stages, rows, ends = [], PIECE, False
        for axis in ("c",) + order:
            half = rows // 2
            st = dict(axis=axis, rows=half, ends=ends)
            if axis == "z":
                n = half // SUBS
                st["down"] = [dict(rs=self.sem(), ag=self.sem(), slot=self.slot(n), rows=n, at=i * n) for i in range(SUBS)]
                st["up"] = [dict(rs=self.sem(), ag=self.sem(), slot=self.slot(n), rows=n, at=i * n) for i in range(SUBS)]
                ends = True
            else:
                st.update(rs=self.sem(), ag=self.sem(), slot=self.slot(half))
            stages.append(st)
            rows = half
        more = [dict(bit=b, rs=self.sem(), slot=self.slot(rows)) for b in self.extra]
        return dict(base=base, stages=stages, more=more, rows=rows)

    def bind(self, total, slots, final, send_sem, recv_sem):
        self.total, self.landing, self.final = total, slots, final
        self.ss, self.rs = send_sem, recv_sem
        dp, sq = lax.axis_index("dp"), lax.axis_index("seq")
        self.dp, self.sq = dp, sq
        self.bits = {"c": (1, dp % 2), "x": (2, (dp // 2) % 2), "y": (4, (dp // 4) % 2)}
        self.last = self.seq_size - 1
        self.edge = jnp.logical_or(sq == 0, sq == self.last)
        self.side = sq // self.last
        self.sent = []
        for p in self.pieces:
            off = p["base"]
            for st in p["stages"]:
                half = st["rows"]
                st["off"] = off
                value = self.side if st["axis"] == "z" else self.bits[st["axis"]][1]
                st["keep"] = off + value * half
                st["give"] = off + (1 - value) * half
                off = st["keep"]
            p["own"] = off

    def view(self, off, rows):
        return self.total.at[pl.ds(pl.multiple_of(off, 16), rows)]

    def partner(self, axis):
        bit, value = self.bits[axis]
        return (self.dp + bit * (1 - 2 * value), self.sq)

    def copy(self, src, dst, sem, tgt):
        return pltpu.make_async_remote_copy(src, dst, self.ss.at[sem], self.rs.at[sem], tgt, MESH)

    def send(self, make, when):
        self.sent.append((make, when))
        make().start()

    def gated(self, when, f):
        if when is None:
            f()
        else:
            pl.when(when)(f)

    def done(self, off, rows):
        return self.final.at[pl.ds(pl.multiple_of(off, 16), rows)]

    def add(self, off, slot, rows, into=None):
        into = self.total if into is None else into
        step = 32 if rows % 32 == 0 else 16

        def body(i, _):
            at = pl.multiple_of(off + i * step, 16)
            frm = pl.multiple_of(slot + i * step, 16)
            into[pl.ds(at, step)] = self.total[pl.ds(at, step)] + self.landing[pl.ds(frm, step)]
            return 0

        lax.fori_loop(0, rows // step, body, 0)


    def rs_start(self, p, i):
        st = p["stages"][i]
        if st["axis"] == "z":
            for way, at, to, base in (("down", self.last, -1, 0), ("up", 0, 1, st["rows"])):
                when = self.sq == at

                def f(way=way, to=to, base=base, when=when):
                    for s in st[way]:
                        self.send(lambda s=s: self.rs_copy(st, s, base, to), when)
                self.gated(when, f)
        else:
            when = self.edge if st["ends"] else None

            def f():
                self.send(
                    lambda: self.copy(
                        self.view(st["give"], st["rows"]), self.landing.at[pl.ds(st["slot"], st["rows"])],
                        st["rs"], self.partner(st["axis"]),
                    ),
                    when,
                )
            self.gated(when, f)

    def rs_hyper(self, p, i):
        st = p["stages"][i]

        def f():
            self.copy(
                self.view(st["give"], st["rows"]), self.landing.at[pl.ds(st["slot"], st["rows"])],
                st["rs"], self.partner(st["axis"]),
            ).wait_recv()
            self.add(st["keep"], st["slot"], st["rows"], self.final if i + 1 == len(p["stages"]) else None)
        self.gated(self.edge if st["ends"] else None, f)

    def rs_hop(self, p, i, hop):
        st = p["stages"][i]
        for way, at, to, base in (("down", self.last - hop, -1, 0), ("up", hop, 1, st["rows"])):
            when = self.sq == at

            def f(way=way, to=to, base=base, when=when):
                for s in st[way]:
                    self.rs_copy(st, s, base, -to).wait_recv()
                    ended = hop == self.last and i + 1 == len(p["stages"])
                    self.add(st["off"] + base + s["at"], s["slot"], s["rows"], self.final if ended else None)
                    if hop < self.last:
                        self.send(lambda s=s: self.rs_copy(st, s, base, to), when)
            self.gated(when, f)

    def rs_copy(self, st, s, base, to):
        return self.copy(
            self.view(st["off"] + base + s["at"], s["rows"]), self.landing.at[pl.ds(s["slot"], s["rows"])],
            s["rs"], (self.dp, self.sq + to),
        )

    def more(self, p):
        for m in p["more"]:
            bit = m["bit"]
            value = (self.dp // bit) % 2
            tgt = (self.dp + bit * (1 - 2 * value), self.sq)

            def f():
                c = self.copy(
                    self.done(p["own"], p["rows"]), self.landing.at[pl.ds(m["slot"], p["rows"])], m["rs"], tgt
                )
                c.start()
                c.wait()
                part = pl.ds(pl.multiple_of(p["own"], 16), p["rows"])
                self.final[part] = self.final[part] + self.landing[pl.ds(m["slot"], p["rows"])]
            self.gated(self.edge, f)


    def ag_start(self, p, i):
        st = p["stages"][i]
        if st["axis"] == "z":
            for way, at, to, base in (("down", self.last, -1, st["rows"]), ("up", 0, 1, 0)):
                when = self.sq == at

                def f(way=way, to=to, base=base, when=when):
                    for s in st[way]:
                        self.send(lambda s=s: self.ag_copy(st, s, base, to), when)
                self.gated(when, f)
        else:
            when = self.edge if st["ends"] else None

            def f():
                self.send(
                    lambda: self.copy(
                        self.done(st["keep"], st["rows"]), self.done(st["keep"], st["rows"]),
                        st["ag"], self.partner(st["axis"]),
                    ),
                    when,
                )
            self.gated(when, f)

    def ag_copy(self, st, s, base, to):
        part = self.done(st["off"] + base + s["at"], s["rows"])
        return self.copy(part, part, s["ag"], (self.dp, self.sq + to))

    def ag_hyper(self, p, i):
        st = p["stages"][i]

        def f():
            part = self.done(st["give"], st["rows"])
            self.copy(part, part, st["ag"], self.partner(st["axis"])).wait_recv()
        self.gated(self.edge if st["ends"] else None, f)

    def ag_hop(self, p, i, hop):
        st = p["stages"][i]
        for way, at, to, base in (("down", self.last - hop, -1, st["rows"]), ("up", hop, 1, 0)):
            when = self.sq == at

            def f(way=way, to=to, base=base, when=when):
                for s in st[way]:
                    self.ag_copy(st, s, base, -to).wait_recv()
                    if hop < self.last:
                        self.send(lambda s=s: self.ag_copy(st, s, base, to), when)
            self.gated(when, f)

    def script(self, p):
        steps, n = [], len(p["stages"])
        for i, st in enumerate(p["stages"]):
            after = (lambda i=i: self.rs_start(p, i + 1)) if i + 1 < n else (lambda: (self.more(p), self.ag_start(p, n - 1)))
            if st["axis"] == "z":
                for hop in range(1, self.last + 1):
                    def step(i=i, hop=hop, after=after):
                        self.rs_hop(p, i, hop)
                        if hop == self.last:
                            after()
                    steps.append((f"rz{hop}", step))
            else:
                def step(i=i, after=after):
                    self.rs_hyper(p, i)
                    after()
                steps.append(("r" + st["axis"], step))
        for i in reversed(range(n)):
            st = p["stages"][i]
            after = (lambda i=i: self.ag_start(p, i - 1)) if i > 0 else (lambda: None)
            if st["axis"] == "z":
                for hop in range(1, self.last + 1):
                    def step(i=i, hop=hop, after=after):
                        self.ag_hop(p, i, hop)
                        if hop == self.last:
                            after()
                    steps.append((f"gz{hop}", step))
            else:
                def step(i=i, after=after):
                    self.ag_hyper(p, i)
                    after()
                steps.append(("g" + st["axis"], step))
        return steps

    def finish(self):
        for make, when in self.sent:
            self.gated(when, lambda make=make: make().wait_send())


def small_bits(dp_size, seq_size):
    out, bit = [], 1
    while bit < dp_size:
        out.append(("dp", bit))
        bit *= 2
    bit = 1
    while bit < seq_size:
        out.append(("seq", bit))
        bit *= 2
    return out


def blocks_of(refs, g):
    outer, inner, proj = refs
    out = []
    for i in range(GROUP // 256):
        at = i * 256
        block, row = at // 768, at % 768
        if g == 0:
            view = outer.at[pl.ds(at, 256)]
        elif g == 1:
            view = inner.at[pl.ds(row, 256), pl.ds(block * 768, 768)]
        else:
            view = proj[block].at[pl.ds(row, 256)]
        out.append((g * GROUP + at, view))
    return out


def sums_kernel(
    plan, seq_size,
    outer_in, inner_in, o_in, q_in, k_in, v_in, small_in, y_in, dx_in, dxs_in,
    outer_out, inner_out, o_out, q_out, k_out, v_out, small_out, y_out, dx_out,
    total, landing, final, small, dx_far, dx_near, ss, rs, ls, ms, mr, ys, yr, xs,
):
    plan.bind(total, landing, final, ss, rs)
    dp, sq, side, pair = place(seq_size)
    sibling = (dp + 1 - 2 * side, sq)
    rows, length = y_out.shape[0], y_out.shape[1]
    spread = seq_size // 2

    loads = []
    for g in range(plan.groups):
        part = []
        for i, (at, view) in enumerate(blocks_of((outer_in, inner_in, (o_in, q_in, k_in, v_in)), g)):
            c = pltpu.make_async_copy(view, total.at[pl.ds(at, 256)], ls.at[g, i])
            c.start()
            part.append(c)
        loads.append(part)

    dx_send = pltpu.make_async_remote_copy(dxs_in, dx_far, xs.at[0], xs.at[1], sibling, MESH)
    dx_send.start()

    def back(src, dst, b, lane, tgt):
        return pltpu.make_async_remote_copy(
            src.at[pl.ds(b * length, length)], dst.at[tgt[2]], ys.at[lane, b], yr.at[lane, tgt[2]], tgt[:2], MESH
        )

    def each_back(src, dst, lane, remote, local):
        for b in range(spread):
            home = (pair + sq // rows, side * spread + b, sq % rows)
            mine = jnp.logical_and(home[0] == dp, home[1] == sq)

            @pl.when(mine)
            def _():
                local(pltpu.make_async_copy(src.at[pl.ds(b * length, length)], dst.at[home[2]], xs.at[2 + lane]))

            @pl.when(jnp.logical_not(mine))
            def _():
                remote(back(src, dst, b, lane, home))

    def all_arrived(src, dst, lane):
        for r in range(rows):
            mine = jnp.logical_and(sq // spread == side, sq == rows * side + r)

            @pl.when(jnp.logical_not(mine))
            def _():
                back(src, dst, 0, lane, (sibling[0], sibling[1], r)).wait_recv()

    each_back(y_in, y_out, 0, lambda c: c.start(), lambda c: c.start())

    steps = [plan.script(p) for p in plan.pieces]
    for g in range(plan.groups):
        for c in loads[g]:
            c.wait()
        for p in plan.pieces[3 * g : 3 * g + 3]:
            plan.rs_start(p, 0)

    small[0] = small_in[...]
    bits = small_bits(plan.dp_size, seq_size)

    def small_copy(i):
        axis, bit = bits[i]
        if axis == "dp":
            tgt = (dp + bit * (1 - 2 * ((dp // bit) % 2)), sq)
        else:
            tgt = (dp, sq + bit * (1 - 2 * ((sq // bit) % 2)))
        return pltpu.make_async_remote_copy(small.at[i], small.at[len(bits) + 1 + i], ms.at[i], mr.at[i], tgt, MESH)

    small_copy(0).start()

    dx_send.wait_recv()

    def dx_body(i, _):
        at = pl.ds(pl.multiple_of(i * 32, 32), 32)
        dx_near[at] = (dx_in[at] + dx_far[at].astype(F32)).astype(BF16)
        return 0

    lax.fori_loop(0, dx_in.shape[0] // 32, dx_body, 0)
    each_back(dx_near, dx_out, 1, lambda c: c.start(), lambda c: c.start())

    stores = []
    for t in range(len(steps[0])):
        for g in range(plan.groups):
            for cls in range(3):
                steps[3 * g + cls][t][1]()
        if t < len(bits):
            small_copy(t).wait_recv()
            small[t + 1] = small[t] + small[len(bits) + 1 + t]
            if t + 1 < len(bits):
                small_copy(t + 1).start()
    for g in range(plan.groups):
        for i, (at, view) in enumerate(blocks_of((outer_out, inner_out, (o_out, q_out, k_out, v_out)), g)):
            c = pltpu.make_async_copy(final.at[pl.ds(at, 256)], view, ls.at[g, i])
            c.start()
            stores.append(c)
    small_out[...] = small[len(bits)]
    for i in range(len(bits)):
        small_copy(i).wait_send()
    dx_send.wait_send()
    each_back(y_in, y_out, 0, lambda c: c.wait_send(), lambda c: c.wait())
    each_back(dx_near, dx_out, 1, lambda c: c.wait_send(), lambda c: c.wait())
    all_arrived(y_in, y_out, 0)
    all_arrived(dx_near, dx_out, 1)
    plan.finish()
    for c in stores:
        c.wait()


def all_sums(outer, inner, w_o, w_q, w_k, w_v, small, y, dx, dx_far, dp_size, seq_size, rows):
    plan = Exchange(dp_size, seq_size, 3)
    tokens, width = dx.shape
    length = 2 * tokens // seq_size
    vmem, anyw = pl.BlockSpec(memory_space=pltpu.VMEM), pl.BlockSpec(memory_space=pl.ANY)
    nbits = len(small_bits(dp_size, seq_size))
    back = jax.ShapeDtypeStruct((rows, length, width), BF16)
    like = lambda a: jax.ShapeDtypeStruct(a.shape, a.dtype)
    return pl.pallas_call(
        functools.partial(sums_kernel, plan, seq_size),
        out_shape=(like(outer), like(inner), like(w_o), like(w_q), like(w_k), like(w_v), like(small), back, back),
        in_specs=[anyw] * 6 + [vmem, anyw, vmem, anyw],
        out_specs=(anyw,) * 6 + (vmem, anyw, anyw),
        scratch_shapes=[
            pltpu.VMEM((3 * GROUP, width), BF16),
            pltpu.VMEM((plan.slots, width), BF16),
            pltpu.VMEM((3 * GROUP, width), BF16),
            pltpu.VMEM((2 * nbits + 1,) + small.shape, F32),
            pltpu.VMEM((tokens, width), BF16),
            pltpu.VMEM((tokens, width), BF16),
            pltpu.SemaphoreType.DMA((plan.sems,)),
            pltpu.SemaphoreType.DMA((plan.sems,)),
            pltpu.SemaphoreType.DMA((3, GROUP // 256)),
            pltpu.SemaphoreType.DMA((nbits,)),
            pltpu.SemaphoreType.DMA((nbits,)),
            pltpu.SemaphoreType.DMA((2, 2)),
            pltpu.SemaphoreType.DMA((2, 2)),
            pltpu.SemaphoreType.DMA((4,)),
        ],
        compiler_params=pltpu.CompilerParams(has_side_effects=True, vmem_limit_bytes=56 << 20),
        name="all_sums",
    )(outer, inner, w_o, w_q, w_k, w_v, small, y, dx, dx_far)


def layer_norm(values, scale_gain, offset):
    centre = values - jnp.mean(values, axis=-1, keepdims=True)
    inverse_std = lax.rsqrt(jnp.mean(centre * centre, axis=-1, keepdims=True) + EPSILON)
    normed = centre * inverse_std
    return (normed * scale_gain + offset, normed, inverse_std)


def norm_back(grad_out, normed, inverse_std, scale_gain):
    scaled = grad_out * scale_gain
    return inverse_std * (
        scaled
        - jnp.mean(scaled, axis=-1, keepdims=True)
        - normed * jnp.mean(scaled * normed, axis=-1, keepdims=True)
    )


def heads(t):
    return t.reshape(t.shape[0], t.shape[1] // HD, HD)


def local_layer(x_full, cot, segs, side, w):
    (w_query, b_query, w_key, w_value, b_value, w_out, b_out, gain_one, shift_one,
     w_inner, b_inner, w_outer, b_outer, gain_two, shift_two) = w
    tokens = cot.shape[0]
    x_own = lax.dynamic_slice_in_dim(x_full, side * tokens, tokens, 0)
    seg_own = lax.dynamic_slice_in_dim(segs, side * tokens, tokens, 0)
    query = (product(x_own, w_query) + b_query).astype(BF16)
    key = product(x_full, w_key).astype(BF16)
    value = (product(x_full, w_value) + b_value).astype(BF16)
    scores = jnp.einsum("qhd,khd->hqk", heads(query), heads(key), preferred_element_type=F32) * 0.125
    scores = jnp.where(seg_own[None, :, None] == segs[None, None, :], scores, MASKED)
    row_max = jnp.max(scores, axis=-1, keepdims=True)
    powers = jnp.exp(scores - row_max)
    totals = jnp.sum(powers, axis=-1, keepdims=True)
    probs = powers / totals
    probs_low = probs.astype(BF16)
    attended = jnp.einsum("hqk,khd->qhd", probs_low, heads(value), preferred_element_type=F32)
    attn_low = attended.reshape(tokens, -1).astype(BF16)
    hidden_one, normed_one, inverse_one = layer_norm(
        x_own.astype(F32) + product(attn_low, w_out) + b_out, gain_one, shift_one
    )
    hidden_low = hidden_one.astype(BF16)
    inner = product(hidden_low, w_inner) + b_inner
    cdf = 0.5 * (1.0 + lax.erf(inner * INV_ROOT_TWO))
    active = (inner * cdf).astype(BF16)
    result, normed_two, inverse_two = layer_norm(hidden_one + product(active, w_outer) + b_outer, gain_two, shift_two)
    g = cot.astype(F32)
    d_gain_two, d_shift_two = jnp.sum(g * normed_two, 0), jnp.sum(g, 0)
    grad_two = norm_back(g, normed_two, inverse_two, gain_two)
    grad_outer = grad_two.astype(BF16)
    d_outer = product_tn(active, grad_outer).astype(BF16)
    d_b_outer = jnp.sum(grad_outer.astype(F32), 0)
    slope = cdf + inner * DENSITY * jnp.exp(-0.5 * inner * inner)
    grad_inner = (product_nt(grad_outer, w_outer) * slope).astype(BF16)
    d_inner = product_tn(hidden_low, grad_inner).astype(BF16)
    d_b_inner = jnp.sum(grad_inner.astype(F32), 0)
    grad_hidden = grad_two + product_nt(grad_inner, w_inner)
    d_gain_one, d_shift_one = jnp.sum(grad_hidden * normed_one, 0), jnp.sum(grad_hidden, 0)
    grad_one = norm_back(grad_hidden, normed_one, inverse_one, gain_one)
    grad_branch = grad_one.astype(BF16)
    d_out = product_tn(attn_low, grad_branch).astype(BF16)
    d_b_out = jnp.sum(grad_branch.astype(F32), 0)
    grad_attn = product_nt(grad_branch, w_out).astype(BF16)
    delta = jnp.sum(heads(grad_attn).astype(F32) * heads(attended.reshape(tokens, -1)), -1)
    grad_prob = jnp.einsum("qhd,khd->hqk", heads(grad_attn), heads(value), preferred_element_type=F32)
    grad_scores = (probs * (grad_prob - delta.T[:, :, None])).astype(BF16)
    grad_query = (jnp.einsum("hqk,khd->qhd", grad_scores, heads(key), preferred_element_type=F32) * 0.125)
    grad_query = grad_query.reshape(tokens, -1).astype(BF16)
    grad_key = (jnp.einsum("hqk,qhd->khd", grad_scores, heads(query), preferred_element_type=F32) * 0.125)
    grad_key = grad_key.reshape(2 * tokens, -1).astype(BF16)
    grad_value = jnp.einsum("hqk,qhd->khd", probs_low, heads(grad_attn), preferred_element_type=F32)
    grad_value = grad_value.reshape(2 * tokens, -1).astype(BF16)
    d_query = product_tn(x_own, grad_query).astype(BF16)
    d_key = product_tn(x_full, grad_key).astype(BF16)
    d_value = product_tn(x_full, grad_value).astype(BF16)
    d_b_query = jnp.sum(grad_query.astype(F32), 0)
    d_b_value = jnp.sum(grad_value.astype(F32), 0)
    both = product_nt(grad_key, w_key) + product_nt(grad_value, w_value)
    dx = grad_one + product_nt(grad_query, w_query) + lax.dynamic_slice_in_dim(both, side * tokens, tokens, 0)
    dx_far = lax.dynamic_slice_in_dim(both, (1 - side) * tokens, tokens, 0).astype(BF16)
    small = jnp.concatenate(
        [
            jnp.stack([d_b_query, d_b_value, d_b_out, d_gain_one, d_shift_one, d_b_outer, d_gain_two, d_shift_two]),
            d_b_inner.reshape(-1, 768),
            jnp.zeros((4, 768), F32),
        ]
    )
    return result.astype(BF16), dx, dx_far, d_outer, d_inner, d_out, d_query, d_key, d_value, small


def on_device(
    dp_size, seq_size, layer_input, segment_ids, w_query, b_query, w_key, w_value, b_value, w_out, b_out, gain_one,
    shift_one, w_inner, b_inner, w_outer, b_outer, gain_two, shift_two, cotangent,
):
    rows = layer_input.shape[0]
    x_full, cot, sg = gather_rows(layer_input, cotangent, segment_ids, seq_size)
    side = lax.axis_index("dp") % 2
    y, dx, dx_far, d_outer, d_inner, d_out, d_query, d_key, d_value, small = local_layer(
        x_full, cot, sg[:, 0, :].reshape(-1), side,
        (w_query, b_query, w_key, w_value, b_value, w_out, b_out, gain_one, shift_one, w_inner, b_inner, w_outer,
         b_outer, gain_two, shift_two),
    )
    d_outer, d_inner, d_out, d_query, d_key, d_value, small, y, dx = all_sums(
        d_outer, d_inner, d_out, d_query, d_key, d_value, small, y, dx, dx_far, dp_size, seq_size, rows
    )
    up = lambda a: a.astype(F32)
    return (
        y, dx, up(d_query), small[0], up(d_key), up(d_value), small[1], up(d_out), small[2], small[3], small[4],
        up(d_inner), small[8:12].reshape(-1), up(d_outer), small[5], small[6], small[7],
    )


def solution(mesh):
    sizes = (mesh.shape["dp"], mesh.shape["seq"])
    tokens = P("dp", "seq", None)
    return jax.shard_map(
        functools.partial(on_device, *sizes),
        mesh=mesh,
        in_specs=(tokens, P("dp", "seq")) + (P(),) * 15 + (tokens,),
        out_specs=(tokens, tokens) + (P(),) * 15,
        check_vma=False,
    )
```

```python
import functools

import jax
import jax.numpy as jnp
from jax import lax
from jax.experimental import pallas as pl
from jax.experimental.pallas import tpu as pltpu
from jax.sharding import PartitionSpec as P

HD = 64
EPSILON = 1e-12
MASKED = -1000000000.0
INV_ROOT_TWO = 0.7071067811865476
DENSITY = 0.3989422804014327
MESH = pl.DeviceIdType.MESH
BF16 = jnp.bfloat16
F32 = jnp.float32


def product(left, right):
    return jnp.dot(left, right, preferred_element_type=F32)


def product_tn(left, right):
    return lax.dot_general(left, right, (((0,), (0,)), ((), ())), preferred_element_type=F32)


def product_nt(left, right):
    return lax.dot_general(left, right, (((1,), (1,)), ((), ())), preferred_element_type=F32)


def place(seq_size):
    dp, sq = lax.axis_index("dp"), lax.axis_index("seq")
    side = dp % 2
    return dp, sq, side, dp - side


GROUP = 1536
PIECE = 512
ORDERS = (("x", "y", "z"), ("y", "z", "x"), ("z", "x", "y"))
SUBS = 1


class Exchange:
    def __init__(self, dp_size, seq_size, groups):
        self.dp_size, self.seq_size, self.groups = dp_size, seq_size, groups
        self.extra = []
        bit = 8
        while bit < dp_size:
            self.extra.append(bit)
            bit *= 2
        self.sems = 0
        self.slots = 0
        self.pieces = []
        for g in range(groups):
            for cls in range(3):
                self.pieces.append(self.plan(g * GROUP + cls * PIECE, ORDERS[cls]))

    def sem(self):
        self.sems += 1
        return self.sems - 1

    def slot(self, rows):
        self.slots += rows
        return self.slots - rows

    def plan(self, base, order):
        stages, rows, ends = [], PIECE, False
        for axis in ("c",) + order:
            half = rows // 2
            st = dict(axis=axis, rows=half, ends=ends)
            if axis == "z":
                n = half // SUBS
                st["down"] = [dict(rs=self.sem(), ag=self.sem(), slot=self.slot(n), rows=n, at=i * n) for i in range(SUBS)]
                st["up"] = [dict(rs=self.sem(), ag=self.sem(), slot=self.slot(n), rows=n, at=i * n) for i in range(SUBS)]
                ends = True
            else:
                st.update(rs=self.sem(), ag=self.sem(), slot=None if axis == "c" else self.slot(half))
            stages.append(st)
            rows = half
        more = [dict(bit=b, rs=self.sem(), slot=self.slot(rows)) for b in self.extra]
        return dict(base=base, stages=stages, more=more, rows=rows)

    def bind(self, total, slots, final, send_sem, recv_sem):
        self.total, self.landing, self.final = total, slots, final
        self.ss, self.rs = send_sem, recv_sem
        dp, sq = lax.axis_index("dp"), lax.axis_index("seq")
        self.dp, self.sq = dp, sq
        self.bits = {"c": (1, dp % 2), "x": (2, (dp // 2) % 2), "y": (4, (dp // 4) % 2)}
        self.last = self.seq_size - 1
        self.edge = jnp.logical_or(sq == 0, sq == self.last)
        self.side = sq // self.last
        self.sent = []
        for p in self.pieces:
            off = p["base"]
            for st in p["stages"]:
                half = st["rows"]
                st["off"] = off
                value = self.side if st["axis"] == "z" else self.bits[st["axis"]][1]
                st["keep"] = off + value * half
                st["give"] = off + (1 - value) * half
                off = st["keep"]
            p["own"] = off

    def view(self, off, rows):
        return self.total.at[pl.ds(pl.multiple_of(off, 16), rows)]

    def partner(self, axis):
        bit, value = self.bits[axis]
        return (self.dp + bit * (1 - 2 * value), self.sq)

    def copy(self, src, dst, sem, tgt):
        return pltpu.make_async_remote_copy(src, dst, self.ss.at[sem], self.rs.at[sem], tgt, MESH)

    def send(self, make, when):
        self.sent.append((make, when))
        make().start()

    def gated(self, when, f):
        if when is None:
            f()
        else:
            pl.when(when)(f)

    def done(self, off, rows):
        return self.final.at[pl.ds(pl.multiple_of(off, 16), rows)]

    def landed(self, st):
        if st["slot"] is None:
            return self.done(st["give"], st["rows"])
        return self.landing.at[pl.ds(st["slot"], st["rows"])]

    def add(self, off, slot, rows, into=None):
        into = self.total if into is None else into
        source = self.final if slot is None else self.landing
        slot = off if slot is None else slot
        step = 32 if rows % 32 == 0 else 16

        def body(i, _):
            at = pl.multiple_of(off + i * step, 16)
            frm = pl.multiple_of(slot + i * step, 16)
            into[pl.ds(at, step)] = self.total[pl.ds(at, step)] + source[pl.ds(frm, step)]
            return 0

        lax.fori_loop(0, rows // step, body, 0)


    def rs_start(self, p, i):
        st = p["stages"][i]
        if st["axis"] == "z":
            for way, at, to, base in (("down", self.last, -1, 0), ("up", 0, 1, st["rows"])):
                when = self.sq == at

                def f(way=way, to=to, base=base, when=when):
                    for s in st[way]:
                        self.send(lambda s=s: self.rs_copy(st, s, base, to), when)
                self.gated(when, f)
        else:
            when = self.edge if st["ends"] else None

            def f():
                self.send(
                    lambda: self.copy(
                        self.view(st["give"], st["rows"]), self.landed(st), st["rs"], self.partner(st["axis"]),
                    ),
                    when,
                )
            self.gated(when, f)

    def rs_hyper(self, p, i):
        st = p["stages"][i]

        def f():
            self.copy(
                self.view(st["give"], st["rows"]), self.landed(st), st["rs"], self.partner(st["axis"]),
            ).wait_recv()
            self.add(st["keep"], st["slot"], st["rows"], self.final if i + 1 == len(p["stages"]) else None)
        self.gated(self.edge if st["ends"] else None, f)

    def rs_hop(self, p, i, hop):
        st = p["stages"][i]
        for way, at, to, base in (("down", self.last - hop, -1, 0), ("up", hop, 1, st["rows"])):
            when = self.sq == at

            def f(way=way, to=to, base=base, when=when):
                for s in st[way]:
                    self.rs_copy(st, s, base, -to).wait_recv()
                    ended = hop == self.last and i + 1 == len(p["stages"])
                    self.add(st["off"] + base + s["at"], s["slot"], s["rows"], self.final if ended else None)
                    if hop < self.last:
                        self.send(lambda s=s: self.rs_copy(st, s, base, to), when)
            self.gated(when, f)

    def rs_copy(self, st, s, base, to):
        return self.copy(
            self.view(st["off"] + base + s["at"], s["rows"]), self.landing.at[pl.ds(s["slot"], s["rows"])],
            s["rs"], (self.dp, self.sq + to),
        )

    def more(self, p):
        for m in p["more"]:
            bit = m["bit"]
            value = (self.dp // bit) % 2
            tgt = (self.dp + bit * (1 - 2 * value), self.sq)

            def f():
                c = self.copy(
                    self.done(p["own"], p["rows"]), self.landing.at[pl.ds(m["slot"], p["rows"])], m["rs"], tgt
                )
                c.start()
                c.wait()
                part = pl.ds(pl.multiple_of(p["own"], 16), p["rows"])
                self.final[part] = self.final[part] + self.landing[pl.ds(m["slot"], p["rows"])]
            self.gated(self.edge, f)


    def ag_start(self, p, i):
        st = p["stages"][i]
        if st["axis"] == "z":
            for way, at, to, base in (("down", self.last, -1, st["rows"]), ("up", 0, 1, 0)):
                when = self.sq == at

                def f(way=way, to=to, base=base, when=when):
                    for s in st[way]:
                        self.send(lambda s=s: self.ag_copy(st, s, base, to), when)
                self.gated(when, f)
        else:
            when = self.edge if st["ends"] else None

            def f():
                self.send(
                    lambda: self.copy(
                        self.done(st["keep"], st["rows"]), self.done(st["keep"], st["rows"]),
                        st["ag"], self.partner(st["axis"]),
                    ),
                    when,
                )
            self.gated(when, f)

    def ag_copy(self, st, s, base, to):
        part = self.done(st["off"] + base + s["at"], s["rows"])
        return self.copy(part, part, s["ag"], (self.dp, self.sq + to))

    def ag_hyper(self, p, i):
        st = p["stages"][i]

        def f():
            part = self.done(st["give"], st["rows"])
            self.copy(part, part, st["ag"], self.partner(st["axis"])).wait_recv()
        self.gated(self.edge if st["ends"] else None, f)

    def ag_hop(self, p, i, hop):
        st = p["stages"][i]
        for way, at, to, base in (("down", self.last - hop, -1, st["rows"]), ("up", hop, 1, 0)):
            when = self.sq == at

            def f(way=way, to=to, base=base, when=when):
                for s in st[way]:
                    self.ag_copy(st, s, base, -to).wait_recv()
                    if hop < self.last:
                        self.send(lambda s=s: self.ag_copy(st, s, base, to), when)
            self.gated(when, f)

    def script(self, p):
        steps, n = [], len(p["stages"])
        for i, st in enumerate(p["stages"]):
            after = (lambda i=i: self.rs_start(p, i + 1)) if i + 1 < n else (lambda: (self.more(p), self.ag_start(p, n - 1)))
            if st["axis"] == "z":
                for hop in range(1, self.last + 1):
                    def step(i=i, hop=hop, after=after):
                        self.rs_hop(p, i, hop)
                        if hop == self.last:
                            after()
                    steps.append((f"rz{hop}", step))
            else:
                def step(i=i, after=after):
                    self.rs_hyper(p, i)
                    after()
                steps.append(("r" + st["axis"], step))
        for i in reversed(range(n)):
            st = p["stages"][i]
            after = (lambda i=i: self.ag_start(p, i - 1)) if i > 0 else (lambda: None)
            if st["axis"] == "z":
                for hop in range(1, self.last + 1):
                    def step(i=i, hop=hop, after=after):
                        self.ag_hop(p, i, hop)
                        if hop == self.last:
                            after()
                    steps.append((f"gz{hop}", step))
            else:
                def step(i=i, after=after):
                    self.ag_hyper(p, i)
                    after()
                steps.append(("g" + st["axis"], step))
        return steps

    def finish(self):
        for make, when in self.sent:
            self.gated(when, lambda make=make: make().wait_send())


def small_bits(dp_size, seq_size):
    out, bit = [], 1
    while bit < dp_size:
        out.append(("dp", bit))
        bit *= 2
    bit = 1
    while bit < seq_size:
        out.append(("seq", bit))
        bit *= 2
    return out


D = 768
FF = 3072
OUTER, INNER, PROJ = 0, 3072, 6144
ORDER = (
    -1, -2, -3, 0, 1, 2, 3, 4, -4, 5, -5, 0, 6, 1, 2, 7, 8, -6, 3, 4, 5, -7, 9, 0,
    1, 10, 2, 6, 11, -8, 7, 8, 5, -9, 3, 4, 9, 1, 0, 2, 10, 8, -10, 11, 5, 2, 6, 4,
    7, 0, 1, 9, 3, 2, -11, 10, 5, 6, 8, 1, 9, 2, 4, 11, 0, -12, 7, 5, -13, 3, 8, 0,
    12, 1, 13, 5, 10, 14, 11, 6, 15, 2, 9, 16, 8, 4, 7, 0, 17, 3, 1, -14, -15, 10, 12, 13,
    6, 1, 9, 14, 5, 0, 11, 16, 1, -16, 8, 2, 14, 12, 15, 4, 0, 17, 7, 11, 3, 2, -17, 10,
    14, 13, 8, 6, 1, 9, 17, 1, 3, 15, 2, -18, 0, 11, 13, 2, 7, 5, 0, 6, 10, 9, 17, 16,
    -19, 14, 3, 12, 11, 13, 14, 4, 5, 6, 17, 9, 3, -20, 16, 13, 14, 12, 8, 6, 15, 4, 5, 17,
    7, 3, 5, 16, 9, 13, 12, 17, 3, 10, 8, 14, 15, 4, 7, 11, 6, 10, 8, 13, 16, 15, 6, 4,
    12, 8, 7, 4, 11, 9, 10, 14, 13, 9, 15, 17, 12, 16, 7, 11, 7, 14, 11, 13, 15, 17, 12, 10,
    16, 10, 14, 13, 15, 17, 14, 12, 13, 16, 15, 17, 12, 17, 16, 12, 15, 15, 16, 16,
)


SMALL_PARTS = 5


def fold(values):
    return jnp.sum(values.reshape(values.shape[0] // 8, 8, values.shape[1]), axis=0)


def layer_kernel(
    plan, seq_size,
    x_ref, cot_ref, seg_ref, wq_hbm, wk_hbm, wv_hbm, wo_hbm, win_hbm, wout_hbm,
    bq, bv, bo, g1, s1, bi, b2, g2, s2,
    final, small_out, y_out, dx_out,
    total, landing, wproj, xf, qs, key, val, probs, attn, normed, inv1, hid, hid_t, active, slope, cot, ybuf, gout, acc,
    mask, sg, dx_far, small,
    ss, rs, gs_, gr, gl, ws, ms, mr, ys, yr, xs,
):
    plan.bind(total, landing, final, ss, rs)
    dp, sq, side, pair = place(seq_size)
    sibling = (dp + 1 - 2 * side, sq)
    rows, length = x_ref.shape[0], x_ref.shape[1]
    spread = seq_size // 2
    tokens = spread * length
    own, far = side * tokens, (1 - side) * tokens

    loads = {}

    def load(name, src, dst, i):
        loads.setdefault(name, []).append(pltpu.make_async_copy(src, dst, ws.at[i]))
        loads[name][-1].start()

    for i, (name, src) in enumerate((("q", wq_hbm), ("k", wk_hbm), ("v", wv_hbm), ("o", wo_hbm))):
        load(name, src, wproj.at[i], i)
    for j in range(4):
        load("in", win_hbm.at[:, pl.ds(j * D, D)], total.at[pl.ds(INNER + j * D, D)], 4 + j)
    load("out", wout_hbm, total.at[pl.ds(PROJ, FF)], 8)

    def loaded(name):
        for c in loads[name]:
            c.wait()

    half, spot = sq // spread, sq % spread

    def block(i):
        return pl.ds(pl.multiple_of(i * length, length), length)

    def x_copy(r, b, tgt, at):
        return pltpu.make_async_remote_copy(x_ref.at[r], xf.at[block(at)], gs_.at[0, r], gr.at[0, b], tgt, MESH)

    def c_copy(r, b, tgt):
        return pltpu.make_async_remote_copy(cot_ref.at[r], cot.at[block(b)], gs_.at[1, r], gr.at[1, b], tgt, MESH)

    def s_copy(r, c, at, tgt):
        return pltpu.make_async_remote_copy(seg_ref.at[r], sg.at[at], gs_.at[2 + c, r], gr.at[2, at], tgt, MESH)

    def forward(b, base):
        part = xf.at[block(base + b)]
        return pltpu.make_async_remote_copy(part, part, gs_.at[4, b], gr.at[3, b], sibling, MESH)

    def split(local, near, remote):
        pl.when(local)(near)
        pl.when(jnp.logical_not(local))(remote)

    stays = [jnp.logical_and(half == side, sq == rows * side + r) for r in range(rows)]
    comes = [jnp.logical_and(sq // rows == side, side * spread + b == sq) for b in range(spread)]

    def x_local(r, at):
        return pltpu.make_async_copy(x_ref.at[r], xf.at[block(at)], gl.at[0])

    def c_local(r, at):
        return pltpu.make_async_copy(cot_ref.at[r], cot.at[block(at)], gl.at[1])

    def s_local(r):
        return pltpu.make_async_copy(seg_ref.at[r], sg.at[sq], gl.at[2])

    for r in range(rows):
        at = half * spread + spot
        split(
            stays[r],
            lambda r=r, at=at: x_local(r, at).start(),
            lambda r=r, at=at: x_copy(r, spot, (pair + half, rows * side + r), at).start(),
        )
    mine = [[jnp.logical_and(side == c, sq == rows * side + r) for c in range(2)] for r in range(rows)]
    for r in range(rows):
        for c in range(2):
            split(
                mine[r][c],
                lambda r=r: s_local(r).start(),
                lambda r=r, c=c: s_copy(r, c, sq, (pair + c, rows * side + r)).start(),
            )
    for r in range(rows):
        split(
            stays[r],
            lambda r=r: c_local(r, spot).start(),
            lambda r=r: c_copy(r, spot, (pair + half, rows * side + r)).start(),
        )

    for b in range(spread):
        split(
            comes[b],
            lambda b=b: x_local(b, side * spread + b).wait(),
            lambda b=b: x_copy(0, b, sibling, side * spread + b).wait_recv(),
        )
        forward(b, side * spread).start()

    def token_block(which):
        return pl.ds(pl.multiple_of(which, tokens), tokens)

    def cols(i, n=256):
        return pl.ds(pl.multiple_of(i * n, 128), n)

    loaded("q")
    loaded("k")
    loaded("v")

    def project(which, also_query):
        def body(i, _):
            xb = xf[token_block(which)]
            c = cols(i)
            if also_query:
                qs[:, c] = (product(xb, wproj[0, :, c]) + bq[:, c]).astype(BF16) * BF16(0.125)
            key[token_block(which), c] = product(xb, wproj[1, :, c]).astype(BF16)
            val[token_block(which), c] = (product(xb, wproj[2, :, c]) + bv[:, c]).astype(BF16)
            return 0

        lax.fori_loop(0, D // 256, body, 0)

    project(own, True)

    for p in range(seq_size):
        split(
            jnp.logical_and(sq // rows == side, p == sq),
            lambda: s_local(0).wait(),
            lambda p=p: s_copy(0, 0, p, sibling).wait_recv(),
        )
    diagonal = lax.broadcasted_iota(jnp.int32, (length, length), 0) == lax.broadcasted_iota(
        jnp.int32, (length, length), 1
    )
    for b in range(spread):
        mine_seg = jnp.broadcast_to(sg[side * spread + b], (length, length))
        column = jnp.sum(jnp.where(diagonal, mine_seg, 0), axis=1, keepdims=True)
        for p in range(seq_size):
            seen = jnp.broadcast_to(column, (length, length)) == jnp.broadcast_to(sg[p], (length, length))
            mask[b * length : (b + 1) * length, p * length : (p + 1) * length] = jnp.where(seen, 0.0, MASKED)

    for b in range(spread):
        forward(b, (1 - side) * spread).wait_recv()
    project(far, False)

    lane = lax.broadcasted_iota(jnp.int32, (1, 128), 1)
    first = (lane < HD).astype(BF16)
    picks = (first, BF16(1.0) - first)
    low_lanes = lane < HD

    def attend(i, _):
        c = cols(i, 128)
        qp, kp, vp = qs[:, c], key[:, c], val[:, c]
        outs = []
        for n in range(2):
            s = product_nt(qp * picks[n], kp) + mask[...]
            e = jnp.exp(s - jnp.max(s, axis=-1, keepdims=True))
            p = (e * (1.0 / jnp.sum(e, axis=-1, keepdims=True))).astype(BF16)
            probs[2 * i + n] = p
            outs.append(product(p, vp))
        attn[:, c] = jnp.where(low_lanes, outs[0], outs[1]).astype(BF16)
        return 0

    lax.fori_loop(0, D // 128, attend, 0)

    loaded("o")

    def branch(i, _):
        c = cols(i)
        acc[:, c] = product(attn[...], wproj[3, :, c]) + bo[:, c] + xf[token_block(own), c].astype(F32)
        return 0

    lax.fori_loop(0, D // 256, branch, 0)
    step = 32

    def chunk(i):
        return pl.ds(pl.multiple_of(i * step, step), step)

    def norm_one(i, _):
        r = chunk(i)
        v = acc[r]
        centre = v - jnp.mean(v, axis=-1, keepdims=True)
        inv = lax.rsqrt(jnp.mean(centre * centre, axis=-1, keepdims=True) + EPSILON)
        n = centre * inv
        normed[r] = n
        inv1[r] = jnp.broadcast_to(inv, (step, 128))
        hid[r] = (n * g1[...] + s1[...]).astype(BF16)
        return 0

    lax.fori_loop(0, tokens // step, norm_one, 0)

    loaded("in")
    loaded("out")

    def inner_cols(j, i):
        return total.at[pl.ds(INNER + j * D, D), cols(i)]

    for j in range(4):

        def expand(i, _, j=j):
            c = cols(j * 3 + i)
            v = product(hid[...], inner_cols(j, i)[...]) + bi[:, c]
            cdf = 0.5 * (1.0 + lax.erf(v * INV_ROOT_TWO))
            active[:, c] = (v * cdf).astype(BF16)
            slope[:, c] = cdf + v * DENSITY * jnp.exp(-0.5 * v * v)
            return 0

        lax.fori_loop(0, 3, expand, 0)

    def contract(i, _):
        c = cols(i)
        acc[:, c] = product(active[...], total[pl.ds(PROJ, FF), c]) + b2[:, c]
        return 0

    lax.fori_loop(0, D // 256, contract, 0)
    for b in range(spread):
        split(comes[b], lambda b=b: c_local(b, b).wait(), lambda b=b: c_copy(0, b, sibling).wait_recv())

    small[0] = jnp.zeros((16, D), F32)

    def norm_two(i, carry):
        d_gain, d_shift, d_bias = carry
        r = chunk(i)
        v = normed[r] * g1[...] + s1[...] + acc[r]
        centre = v - jnp.mean(v, axis=-1, keepdims=True)
        inv = lax.rsqrt(jnp.mean(centre * centre, axis=-1, keepdims=True) + EPSILON)
        n = centre * inv
        ybuf[r] = (n * g2[...] + s2[...]).astype(BF16)
        g = cot[r].astype(F32)
        scaled = g * g2[...]
        grad = inv * (
            scaled - jnp.mean(scaled, axis=-1, keepdims=True) - n * jnp.mean(scaled * n, axis=-1, keepdims=True)
        )
        grad_low = grad.astype(BF16)
        gout[r] = grad_low
        acc[r] = grad
        return d_gain + fold(g * n), d_shift + fold(g), d_bias + fold(grad_low.astype(F32))

    zero = jnp.zeros((8, D), F32)
    sums = lax.fori_loop(0, tokens // step, norm_two, (zero, zero, zero))
    for at, v in zip((6, 7, 5), sums):
        small[0, at : at + 1] = jnp.sum(v, axis=0, keepdims=True)

    homes = [(pair + sq // rows, side * spread + b) for b in range(spread)]
    at_home = [jnp.logical_and(h[0] == dp, h[1] == sq) for h in homes]

    def back(src, dst, b, lane_, to, slot):
        return pltpu.make_async_remote_copy(
            src.at[pl.ds(b * length, length)], dst.at[slot], ys.at[lane_, b], yr.at[lane_, slot], to, MESH
        )

    def home_local(src, dst, b, lane_):
        return pltpu.make_async_copy(src.at[pl.ds(b * length, length)], dst.at[sq % rows], xs.at[2 + lane_])

    def send_home(src, dst, lane_):
        for b in range(spread):
            split(
                at_home[b],
                lambda b=b: home_local(src, dst, b, lane_).start(),
                lambda b=b: back(src, dst, b, lane_, homes[b], sq % rows).start(),
            )

    def sent_home(src, dst, lane_):
        for b in range(spread):
            split(
                at_home[b],
                lambda b=b: home_local(src, dst, b, lane_).wait(),
                lambda b=b: back(src, dst, b, lane_, homes[b], sq % rows).wait_send(),
            )
        for r in range(rows):
            pl.when(jnp.logical_not(jnp.logical_and(half == side, sq == rows * side + r)))(
                lambda r=r: back(src, dst, 0, lane_, sibling, r).wait_recv()
            )

    send_home(ybuf, y_out, 0)


    def outer_part(n):
        def body(i, _):
            t = n * 6 + i
            total[pl.ds(pl.multiple_of(OUTER + t * 256, 256), 256)] = product(
                active[:, cols(t)].T, gout[...]
            ).astype(BF16)
            return 0

        lax.fori_loop(0, 6, body, 0)

    def inner_part(j):
        if j == 0:
            for i in range(3):
                hid_t[i * 256 : (i + 1) * 256] = hid[:, i * 256 : (i + 1) * 256].T

        def body(i, _):
            t = j * 3 + i
            up = product_nt(gout[...], total[pl.ds(pl.multiple_of(PROJ + t * 256, 256), 256)])
            gi = (up * slope[:, cols(t)]).astype(BF16)
            small[0, 8 + j : 9 + j, cols(i)] = jnp.sum(fold(gi.astype(F32)), axis=0, keepdims=True)
            view = inner_cols(j, i)
            acc[...] += product_nt(gi, view[...])
            view[...] = product(hid_t[...], gi).astype(BF16)
            return 0

        lax.fori_loop(0, 3, body, 0)

    def norm_one_part():
        def body(i, carry):
            d_gain, d_shift, d_bias = carry
            r = chunk(i)
            g, n = acc[r], normed[r]
            scaled = g * g1[...]
            grad = inv1[r][:, :1] * (
                scaled - jnp.mean(scaled, axis=-1, keepdims=True) - n * jnp.mean(scaled * n, axis=-1, keepdims=True)
            )
            grad_low = grad.astype(BF16)
            gout[r] = grad_low
            acc[r] = grad
            return d_gain + fold(g * n), d_shift + fold(g), d_bias + fold(grad_low.astype(F32))

        out = lax.fori_loop(0, tokens // step, body, (zero, zero, zero))
        for at, v in zip((3, 4, 2), out):
            small[0, at : at + 1] = jnp.sum(v, axis=0, keepdims=True)

    def branch_part():
        def body(i, _):
            total[pl.ds(pl.multiple_of(PROJ + i * 256, 256), 256)] = product(attn[:, cols(i)].T, gout[...]).astype(BF16)
            cot[:, cols(i)] = product_nt(gout[...], wproj[3, pl.ds(pl.multiple_of(i * 256, 256), 256)]).astype(BF16)
            return 0

        lax.fori_loop(0, D // 256, body, 0)

    def attention_part(n):
        def body(m, _):
            i = n * 2 + m
            c = cols(i, 128)
            qp, kp, vp, gp = qs[:, c], key[:, c], val[:, c], cot[:, c]
            dq, dk, dv = [], [], []
            for h in range(2):
                p = probs[2 * i + h]
                pf = p.astype(F32)
                weighted = pf * product_nt(gp * picks[h], vp)
                delta = jnp.sum(weighted, axis=-1, keepdims=True)
                gs = (weighted - pf * delta).astype(BF16)
                dq.append(product(gs, kp))
                dk.append(product_tn(gs, qp))
                dv.append(product_tn(p, gp))
            gq = (jnp.where(low_lanes, dq[0], dq[1]) * 0.125).astype(BF16)
            gk = jnp.where(low_lanes, dk[0], dk[1]).astype(BF16)
            gv = jnp.where(low_lanes, dv[0], dv[1]).astype(BF16)
            qs[:, c] = gq
            small[0, 0:1, c] = jnp.sum(fold(gq.astype(F32)), axis=0, keepdims=True)
            small[0, 1:2, c] = jnp.sum(fold(gv.astype(F32)), axis=0, keepdims=True)
            for b in range(2):
                active[:, cols(b * 6 + i, 128)] = gk[b * tokens : (b + 1) * tokens]
                active[:, cols(12 + b * 6 + i, 128)] = gv[b * tokens : (b + 1) * tokens]
            return 0

        lax.fori_loop(0, 2, body, 0)

    def query_part():
        def body(i, _):
            total[pl.ds(pl.multiple_of(PROJ + D + i * 256, 256), 256)] = product(
                xf[token_block(own), cols(i)].T, qs[...]
            ).astype(BF16)
            return 0

        lax.fori_loop(0, D // 256, body, 0)

    def key_part():
        def body(i, _):
            left = xf[pl.ds(0, tokens), cols(i)].T
            right = xf[pl.ds(tokens, tokens), cols(i)].T
            for n in range(2):
                base = n * 2 * D
                total[pl.ds(pl.multiple_of(PROJ + (2 + n) * D + i * 256, 256), 256)] = (
                    product(left, active[:, base : base + D]) + product(right, active[:, base + D : base + 2 * D])
                ).astype(BF16)
            return 0

        lax.fori_loop(0, D // 256, body, 0)

    dx_send = pltpu.make_async_remote_copy(hid, dx_far, xs.at[0], xs.at[1], sibling, MESH)

    def input_part():
        def both(s, w):
            return product_nt(active[:, pl.ds(pl.multiple_of(s * D, 128), D)], wproj[1, w]) + product_nt(
                active[:, pl.ds(pl.multiple_of((2 + s) * D, 128), D)], wproj[2, w]
            )

        def body(i, _):
            w = pl.ds(pl.multiple_of(i * 256, 256), 256)
            hid[:, cols(i)] = both(1 - side, w).astype(BF16)
            acc[:, cols(i)] += product_nt(qs[...], wproj[0, w]) + both(side, w)
            return 0

        lax.fori_loop(0, D // 256, body, 0)
        dx_send.start()

    bits = small_bits(plan.dp_size, seq_size)

    def small_copy(i):
        axis, bit = bits[i]
        if axis == "dp":
            tgt = (dp + bit * (1 - 2 * ((dp // bit) % 2)), sq)
        else:
            tgt = (dp, sq + bit * (1 - 2 * ((sq // bit) % 2)))
        return pltpu.make_async_remote_copy(small.at[i], small.at[len(bits) + 1 + i], ms.at[i], mr.at[i], tgt, MESH)

    def input_end():
        dx_send.wait_recv()

        def body(i, _):
            r = chunk(i)
            gout[r] = (acc[r] + dx_far[r].astype(F32)).astype(BF16)
            return 0

        lax.fori_loop(0, tokens // step, body, 0)
        send_home(gout, dx_out, 1)
        small_copy(0).start()

    def small_part(n):
        for i in range(n, n + 1 if n < SMALL_PARTS - 1 else len(bits)):
            small_copy(i).wait_recv()
            small[i + 1] = small[i] + small[len(bits) + 1 + i]
            if i + 1 < len(bits):
                small_copy(i + 1).start()

    parts = (
        [functools.partial(outer_part, n) for n in range(2)]
        + [functools.partial(inner_part, j) for j in range(4)]
        + [norm_one_part, branch_part]
        + [functools.partial(attention_part, n) for n in range(3)]
        + [query_part, key_part, input_part, input_end]
        + [functools.partial(small_part, n) for n in range(SMALL_PARTS)]
    )
    ready = {0: (0,), 1: (1,), 3: (2,), 5: (3,), 11: (4,), 12: (5,)}
    scripts = [iter(plan.script(p)) for p in plan.pieces]
    for entry in ORDER:
        if entry >= 0:
            next(scripts[entry])[1]()
            continue
        parts[-entry - 1]()
        for g in ready.get(-entry - 1, ()):
            for p in plan.pieces[3 * g : 3 * g + 3]:
                plan.rs_start(p, 0)
    small_out[...] = small[len(bits)]
    for i in range(len(bits)):
        small_copy(i).wait_send()
    dx_send.wait_send()
    sent_home(ybuf, y_out, 0)
    sent_home(gout, dx_out, 1)
    for r in range(rows):
        for c in range(2):
            pl.when(jnp.logical_not(mine[r][c]))(lambda r=r, c=c: s_copy(r, c, sq, sibling).wait_send())
        pl.when(jnp.logical_not(stays[r]))(lambda r=r: x_copy(r, spot, sibling, 0).wait_send())
        pl.when(jnp.logical_not(stays[r]))(lambda r=r: c_copy(r, spot, sibling).wait_send())
    for b in range(spread):
        forward(b, side * spread).wait_send()
    plan.finish()


def whole_layer(args, dp_size, seq_size):
    (layer_input, segment_ids, w_query, b_query, w_key, w_value, b_value, w_out, b_out, gain_one, shift_one,
     w_inner, b_inner, w_outer, b_outer, gain_two, shift_two, cotangent) = args
    plan = Exchange(dp_size, seq_size, 6)
    rows, length, width = layer_input.shape
    tokens = seq_size * length // 2
    vmem, anyw = pl.BlockSpec(memory_space=pltpu.VMEM), pl.BlockSpec(memory_space=pl.ANY)
    nbits = len(small_bits(dp_size, seq_size))
    back = jax.ShapeDtypeStruct((rows, length, width), BF16)
    vector = lambda v: v.reshape(1, -1)
    dma = pltpu.SemaphoreType.DMA
    return pl.pallas_call(
        functools.partial(layer_kernel, plan, seq_size),
        out_shape=(pltpu.VMEM((3 * FF, D), BF16), jax.ShapeDtypeStruct((16, D), F32), back, back),
        in_specs=[anyw] * 9 + [vmem] * 9,
        out_specs=(vmem, vmem, anyw, anyw),
        scratch_shapes=[
            pltpu.VMEM((3 * FF, D), BF16),
            pltpu.VMEM((plan.slots, D), BF16),
            pltpu.VMEM((4, D, D), BF16),
            pltpu.VMEM((2 * tokens, D), BF16),
            pltpu.VMEM((tokens, D), BF16),
            pltpu.VMEM((2 * tokens, D), BF16),
            pltpu.VMEM((2 * tokens, D), BF16),
            pltpu.VMEM((D // HD, tokens, 2 * tokens), BF16),
            pltpu.VMEM((tokens, D), BF16),
            pltpu.VMEM((tokens, D), F32),
            pltpu.VMEM((tokens, 128), F32),
            pltpu.VMEM((tokens, D), BF16),
            pltpu.VMEM((D, tokens), BF16),
            pltpu.VMEM((tokens, FF), BF16),
            pltpu.VMEM((tokens, FF), F32),
            pltpu.VMEM((tokens, D), BF16),
            pltpu.VMEM((tokens, D), BF16),
            pltpu.VMEM((tokens, D), BF16),
            pltpu.VMEM((tokens, D), F32),
            pltpu.VMEM((tokens, 2 * tokens), F32),
            pltpu.VMEM((seq_size, 1, length), jnp.int32),
            pltpu.VMEM((tokens, D), BF16),
            pltpu.VMEM((2 * nbits + 1, 16, D), F32),
            dma((plan.sems,)), dma((plan.sems,)),
            dma((5, 2)), dma((4, seq_size)), dma((3,)), dma((9,)),
            dma((nbits,)), dma((nbits,)), dma((2, 2)), dma((2, 2)), dma((4,)),
        ],
        compiler_params=pltpu.CompilerParams(has_side_effects=True, vmem_limit_bytes=VMEM_LIMIT),
        name="layer",
    )(
        layer_input, cotangent, segment_ids.reshape(rows, 1, length), w_query, w_key, w_value, w_out, w_inner, w_outer,
        vector(b_query), vector(b_value), vector(b_out), vector(gain_one), vector(shift_one), vector(b_inner),
        vector(b_outer), vector(gain_two), vector(shift_two),
    )


VMEM_LIMIT = 48 << 20


def on_device(dp_size, seq_size, *args):
    sums, small, y, dx = whole_layer(args, dp_size, seq_size)
    up = sums.astype(F32)
    d_inner = jnp.concatenate([up[INNER + j * D : INNER + (j + 1) * D] for j in range(4)], axis=1)
    d_out, d_query, d_key, d_value = (up[PROJ + j * D : PROJ + (j + 1) * D] for j in range(4))
    return (
        y, dx, d_query, small[0], d_key, d_value, small[1], d_out, small[2], small[3], small[4],
        d_inner, small[8:12].reshape(-1), up[:FF], small[5], small[6], small[7],
    )


def solution(mesh):
    sizes = (mesh.shape["dp"], mesh.shape["seq"])
    tokens = P("dp", "seq", None)
    return jax.shard_map(
        functools.partial(on_device, *sizes),
        mesh=mesh,
        in_specs=(tokens, P("dp", "seq")) + (P(),) * 15 + (tokens,),
        out_specs=(tokens, tokens) + (P(),) * 15,
        check_vma=False,
    )
```

```python
import functools

import jax
import jax.numpy as jnp
from jax import lax
from jax.experimental import pallas as pl
from jax.experimental.pallas import tpu as pltpu
from jax.sharding import PartitionSpec as P

HD = 64
EPSILON = 1e-12
MASKED = -1000000000.0
INV_ROOT_TWO = 0.7071067811865476
DENSITY = 0.3989422804014327
MESH = pl.DeviceIdType.MESH
BF16 = jnp.bfloat16
F32 = jnp.float32


def product(left, right):
    return jnp.dot(left, right, preferred_element_type=F32)


def product_tn(left, right):
    return lax.dot_general(left, right, (((0,), (0,)), ((), ())), preferred_element_type=F32)


def product_nt(left, right):
    return lax.dot_general(left, right, (((1,), (1,)), ((), ())), preferred_element_type=F32)


def place(seq_size):
    dp, sq = lax.axis_index("dp"), lax.axis_index("seq")
    side = dp % 2
    return dp, sq, side, dp - side


GROUP = 1536
PIECE = 512
ORDERS = (("xyz", "yxz", "zxy"), ("xyz", "yxz", "zyx"))
SUBS = 1


class Exchange:
    def __init__(self, dp_size, seq_size, groups):
        self.dp_size, self.seq_size, self.groups = dp_size, seq_size, groups
        self.extra = []
        bit = 8
        while bit < dp_size:
            self.extra.append(bit)
            bit *= 2
        self.sems = 0
        self.slots = 0
        self.pieces = []
        for g in range(groups):
            for cls in range(3):
                self.pieces.append(self.plan(g * GROUP + cls * PIECE, ORDERS[g % len(ORDERS)][cls]))

    def sem(self):
        self.sems += 1
        return self.sems - 1

    def slot(self, rows):
        self.slots += rows
        return self.slots - rows

    def plan(self, base, order):
        stages, rows, ends = [], PIECE, False
        for axis in "c" + order:
            half = rows // 2
            st = dict(axis=axis, rows=half, ends=ends)
            if axis == "z":
                n = half // SUBS
                st["down"] = [dict(rs=self.sem(), ag=self.sem(), slot=self.slot(n), rows=n, at=i * n) for i in range(SUBS)]
                st["up"] = [dict(rs=self.sem(), ag=self.sem(), slot=self.slot(n), rows=n, at=i * n) for i in range(SUBS)]
                ends = True
            else:
                st.update(rs=self.sem(), ag=self.sem(), slot=None if axis == "c" else self.slot(half))
            stages.append(st)
            rows = half
        more = [dict(bit=b, rs=self.sem(), slot=self.slot(rows)) for b in self.extra]
        return dict(base=base, stages=stages, more=more, rows=rows)

    def bind(self, total, slots, final, send_sem, recv_sem):
        self.total, self.landing, self.final = total, slots, final
        self.ss, self.rs = send_sem, recv_sem
        dp, sq = lax.axis_index("dp"), lax.axis_index("seq")
        self.dp, self.sq = dp, sq
        self.bits = {"c": (1, dp % 2), "x": (2, (dp // 2) % 2), "y": (4, (dp // 4) % 2)}
        self.last = self.seq_size - 1
        self.edge = jnp.logical_or(sq == 0, sq == self.last)
        self.side = sq // self.last
        self.sent = []
        for p in self.pieces:
            off = p["base"]
            for st in p["stages"]:
                half = st["rows"]
                st["off"] = off
                value = self.side if st["axis"] == "z" else self.bits[st["axis"]][1]
                st["keep"] = off + value * half
                st["give"] = off + (1 - value) * half
                off = st["keep"]
            p["own"] = off

    def view(self, off, rows):
        return self.total.at[pl.ds(pl.multiple_of(off, 16), rows)]

    def partner(self, axis):
        bit, value = self.bits[axis]
        return (self.dp + bit * (1 - 2 * value), self.sq)

    def copy(self, src, dst, sem, tgt):
        return pltpu.make_async_remote_copy(src, dst, self.ss.at[sem], self.rs.at[sem], tgt, MESH)

    def send(self, make, when):
        self.sent.append((make, when))
        make().start()

    def gated(self, when, f):
        if when is None:
            f()
        else:
            pl.when(when)(f)

    def done(self, off, rows):
        return self.final.at[pl.ds(pl.multiple_of(off, 16), rows)]

    def landed(self, st):
        if st["slot"] is None:
            return self.done(st["give"], st["rows"])
        return self.landing.at[pl.ds(st["slot"], st["rows"])]

    def add(self, off, slot, rows, into=None):
        into = self.total if into is None else into
        source = self.final if slot is None else self.landing
        slot = off if slot is None else slot
        step = 32 if rows % 32 == 0 else 16

        def body(i, _):
            at = pl.multiple_of(off + i * step, 16)
            frm = pl.multiple_of(slot + i * step, 16)
            into[pl.ds(at, step)] = self.total[pl.ds(at, step)] + source[pl.ds(frm, step)]
            return 0

        lax.fori_loop(0, rows // step, body, 0)


    def rs_start(self, p, i):
        st = p["stages"][i]
        if st["axis"] == "z":
            for way, at, to, base in (("down", self.last, -1, 0), ("up", 0, 1, st["rows"])):
                when = self.sq == at

                def f(way=way, to=to, base=base, when=when):
                    for s in st[way]:
                        self.send(lambda s=s: self.rs_copy(st, s, base, to), when)
                self.gated(when, f)
        else:
            when = self.edge if st["ends"] else None

            def f():
                self.send(
                    lambda: self.copy(
                        self.view(st["give"], st["rows"]), self.landed(st), st["rs"], self.partner(st["axis"]),
                    ),
                    when,
                )
            self.gated(when, f)

    def rs_hyper(self, p, i):
        st = p["stages"][i]

        def f():
            self.copy(
                self.view(st["give"], st["rows"]), self.landed(st), st["rs"], self.partner(st["axis"]),
            ).wait_recv()
            self.add(st["keep"], st["slot"], st["rows"], self.final if i + 1 == len(p["stages"]) else None)
        self.gated(self.edge if st["ends"] else None, f)

    def rs_hop(self, p, i, hop):
        st = p["stages"][i]
        for way, at, to, base in (("down", self.last - hop, -1, 0), ("up", hop, 1, st["rows"])):
            when = self.sq == at

            def f(way=way, to=to, base=base, when=when):
                for s in st[way]:
                    self.rs_copy(st, s, base, -to).wait_recv()
                    ended = hop == self.last and i + 1 == len(p["stages"])
                    self.add(st["off"] + base + s["at"], s["slot"], s["rows"], self.final if ended else None)
                    if hop < self.last:
                        self.send(lambda s=s: self.rs_copy(st, s, base, to), when)
            self.gated(when, f)

    def rs_copy(self, st, s, base, to):
        return self.copy(
            self.view(st["off"] + base + s["at"], s["rows"]), self.landing.at[pl.ds(s["slot"], s["rows"])],
            s["rs"], (self.dp, self.sq + to),
        )

    def more(self, p):
        for m in p["more"]:
            bit = m["bit"]
            value = (self.dp // bit) % 2
            tgt = (self.dp + bit * (1 - 2 * value), self.sq)

            def f():
                c = self.copy(
                    self.done(p["own"], p["rows"]), self.landing.at[pl.ds(m["slot"], p["rows"])], m["rs"], tgt
                )
                c.start()
                c.wait()
                part = pl.ds(pl.multiple_of(p["own"], 16), p["rows"])
                self.final[part] = self.final[part] + self.landing[pl.ds(m["slot"], p["rows"])]
            self.gated(self.edge, f)


    def ag_start(self, p, i):
        st = p["stages"][i]
        if st["axis"] == "z":
            for way, at, to, base in (("down", self.last, -1, st["rows"]), ("up", 0, 1, 0)):
                when = self.sq == at

                def f(way=way, to=to, base=base, when=when):
                    for s in st[way]:
                        self.send(lambda s=s: self.ag_copy(st, s, base, to), when)
                self.gated(when, f)
        else:
            when = self.edge if st["ends"] else None

            def f():
                self.send(
                    lambda: self.copy(
                        self.done(st["keep"], st["rows"]), self.done(st["keep"], st["rows"]),
                        st["ag"], self.partner(st["axis"]),
                    ),
                    when,
                )
            self.gated(when, f)

    def ag_copy(self, st, s, base, to):
        part = self.done(st["off"] + base + s["at"], s["rows"])
        return self.copy(part, part, s["ag"], (self.dp, self.sq + to))

    def ag_hyper(self, p, i):
        st = p["stages"][i]

        def f():
            part = self.done(st["give"], st["rows"])
            self.copy(part, part, st["ag"], self.partner(st["axis"])).wait_recv()
        self.gated(self.edge if st["ends"] else None, f)

    def ag_hop(self, p, i, hop):
        st = p["stages"][i]
        for way, at, to, base in (("down", self.last - hop, -1, st["rows"]), ("up", hop, 1, 0)):
            when = self.sq == at

            def f(way=way, to=to, base=base, when=when):
                for s in st[way]:
                    self.ag_copy(st, s, base, -to).wait_recv()
                    if hop < self.last:
                        self.send(lambda s=s: self.ag_copy(st, s, base, to), when)
            self.gated(when, f)

    def script(self, p):
        steps, n = [], len(p["stages"])
        for i, st in enumerate(p["stages"]):
            after = (lambda i=i: self.rs_start(p, i + 1)) if i + 1 < n else (lambda: (self.more(p), self.ag_start(p, n - 1)))
            if st["axis"] == "z":
                for hop in range(1, self.last + 1):
                    def step(i=i, hop=hop, after=after):
                        self.rs_hop(p, i, hop)
                        if hop == self.last:
                            after()
                    steps.append((f"rz{hop}", step))
            else:
                def step(i=i, after=after):
                    self.rs_hyper(p, i)
                    after()
                steps.append(("r" + st["axis"], step))
        for i in reversed(range(n)):
            st = p["stages"][i]
            after = (lambda i=i: self.ag_start(p, i - 1)) if i > 0 else (lambda: None)
            if st["axis"] == "z":
                for hop in range(1, self.last + 1):
                    def step(i=i, hop=hop, after=after):
                        self.ag_hop(p, i, hop)
                        if hop == self.last:
                            after()
                    steps.append((f"gz{hop}", step))
            else:
                def step(i=i, after=after):
                    self.ag_hyper(p, i)
                    after()
                steps.append(("g" + st["axis"], step))
        return steps

    def finish(self):
        for make, when in self.sent:
            self.gated(when, lambda make=make: make().wait_send())


def small_bits(dp_size, seq_size):
    out, bit = [], 1
    while bit < dp_size:
        out.append(("dp", bit))
        bit *= 2
    bit = 1
    while bit < seq_size:
        out.append(("seq", bit))
        bit *= 2
    return out


D = 768
FF = 3072
OUTER, INNER, PROJ = 0, 3072, 6144
ORDER = (
    -1, -2, 0, -3, 1, 2, 3, 4, -4, 5, 0, -5, 6, 7, 1, 8, 2, -6, 3, -7, 4, 5, -8, 9,
    10, 6, 0, 11, 2, -9, 8, 7, 1, 4, 0, -10, 3, 5, 2, -11, 9, 10, 11, 7, 8, 1, 3, 4,
    0, -12, 6, 2, -13, 12, 9, 13, 10, 5, 6, 14, 7, 11, 2, 15, -14, -15, 16, 17, 8, 9, 10, 1,
    -16, 3, 12, 4, 6, 13, 7, -17, 0, 11, 14, 5, 2, 15, -18, 8, 16, 13, 1, 5, 12, -19, 9, 3,
    10, 4, 2, 11, -20, 6, 17, 7, 16, 0, 15, 9, 5, 13, 8, 14, 10, 11, 1, 12, 3, 5, 4, 11,
    17, 8, 0, 13, 14, 1, 2, 11, 12, 8, 6, 3, 7, 4, 17, 14, 16, 0, 15, 13, 9, 1, 10, 2,
    12, 17, 6, 3, 14, 7, 4, 16, 1, 0, 5, 15, 17, 9, 3, 10, 2, 14, 4, 6, 11, 2, 7, 16,
    5, 15, 0, 1, 9, 17, 8, 10, 0, 13, 1, 12, 11, 4, 16, 3, 15, 5, 6, 4, 3, 14, 8, 5,
    9, 13, 7, 12, 11, 17, 16, 10, 15, 11, 14, 8, 13, 6, 7, 8, 12, 16, 6, 17, 7, 15, 9, 10,
    14, 9, 12, 13, 10, 16, 15, 17, 14, 12, 13, 14, 12, 17, 13, 15, 16, 17, 15, 16,
)


SMALL_PARTS = 5


class Row:
    def __init__(self, ref):
        self.ref = ref

    def __getitem__(self, at):
        return (self.ref[...] if at is Ellipsis else self.ref[at[1]]).reshape(1, -1)


def fold(values):
    return jnp.sum(values.reshape(values.shape[0] // 8, 8, values.shape[1]), axis=0)


def layer_kernel(
    plan, seq_size,
    x_ref, cot_ref, seg_ref, wq_hbm, wk_hbm, wv_hbm, wo_hbm, win_hbm, wout_hbm,
    bq, bv, bo, g1, s1, bi, b2, g2, s2,
    final, small_out, y_out, dx_out,
    total, landing, wproj, xf, qs, key, val, probs, attn, normed, inv1, hid, hid_t, active, slope, cot, ybuf, gout, acc,
    mask, sg, dx_far, small,
    ss, rs, gs_, gr, gl, ws, ms, mr, ys, yr, xs,
):
    plan.bind(total, landing, final, ss, rs)
    bq, bv, bo, g1, s1, bi, b2, g2, s2 = (Row(v) for v in (bq, bv, bo, g1, s1, bi, b2, g2, s2))
    dp, sq, side, pair = place(seq_size)
    sibling = (dp + 1 - 2 * side, sq)
    rows, length = x_ref.shape[0], x_ref.shape[1]
    spread = seq_size // 2
    tokens = spread * length
    own, far = side * tokens, (1 - side) * tokens

    barrier = pltpu.get_barrier_semaphore()
    column = [(pair + c, p) for p in range(seq_size) for c in range(2)]
    for to in column:
        pl.when(jnp.logical_not(jnp.logical_and(to[0] == dp, to[1] == sq)))(
            lambda to=to: pl.semaphore_signal(barrier, inc=1, device_id=to, device_id_type=MESH)
        )
    across = [bit for axis, bit in small_bits(plan.dp_size, seq_size) if axis == "dp" and bit > 1]
    for bit in across:
        to = (dp + bit * (1 - 2 * ((dp // bit) % 2)), sq)
        pl.semaphore_signal(barrier, inc=1, device_id=to, device_id_type=MESH)

    loads = {}

    def load(name, src, dst, i):
        loads.setdefault(name, []).append(pltpu.make_async_copy(src, dst, ws.at[i]))
        loads[name][-1].start()

    for i, (name, src) in enumerate((("q", wq_hbm), ("k", wk_hbm), ("v", wv_hbm), ("o", wo_hbm))):
        load(name, src, wproj.at[i], i)
    for j in range(4):
        load("in", win_hbm.at[:, pl.ds(j * D, D)], total.at[pl.ds(INNER + j * D, D)], 4 + j)
    load("out", wout_hbm, total.at[pl.ds(PROJ, FF)], 8)

    def loaded(name):
        for c in loads[name]:
            c.wait()

    pl.semaphore_wait(barrier, len(column) - 1 + len(across))

    half, spot = sq // spread, sq % spread

    def block(i):
        return pl.ds(pl.multiple_of(i * length, length), length)

    def x_copy(r, b, tgt, at):
        return pltpu.make_async_remote_copy(x_ref.at[r], xf.at[block(at)], gs_.at[0, r], gr.at[0, b], tgt, MESH)

    def c_copy(r, b, tgt):
        return pltpu.make_async_remote_copy(cot_ref.at[r], cot.at[block(b)], gs_.at[1, r], gr.at[1, b], tgt, MESH)

    def s_copy(r, c, at, tgt):
        return pltpu.make_async_remote_copy(seg_ref.at[r], sg.at[at], gs_.at[2 + c, r], gr.at[2, at], tgt, MESH)

    def forward(b, base):
        part = xf.at[block(base + b)]
        return pltpu.make_async_remote_copy(part, part, gs_.at[4, b], gr.at[3, b], sibling, MESH)

    def split(local, near, remote):
        pl.when(local)(near)
        pl.when(jnp.logical_not(local))(remote)

    stays = [jnp.logical_and(half == side, sq == rows * side + r) for r in range(rows)]
    comes = [jnp.logical_and(sq // rows == side, side * spread + b == sq) for b in range(spread)]

    def x_local(r, at):
        return pltpu.make_async_copy(x_ref.at[r], xf.at[block(at)], gl.at[0])

    def c_local(r, at):
        return pltpu.make_async_copy(cot_ref.at[r], cot.at[block(at)], gl.at[1])

    def s_local(r):
        return pltpu.make_async_copy(seg_ref.at[r], sg.at[sq], gl.at[2])

    for r in range(rows):
        at = half * spread + spot
        split(
            stays[r],
            lambda r=r, at=at: x_local(r, at).start(),
            lambda r=r, at=at: x_copy(r, spot, (pair + half, rows * side + r), at).start(),
        )
    mine = [[jnp.logical_and(side == c, sq == rows * side + r) for c in range(2)] for r in range(rows)]
    for r in range(rows):
        for c in range(2):
            split(
                mine[r][c],
                lambda r=r: s_local(r).start(),
                lambda r=r, c=c: s_copy(r, c, sq, (pair + c, rows * side + r)).start(),
            )
    for r in range(rows):
        split(
            stays[r],
            lambda r=r: c_local(r, spot).start(),
            lambda r=r: c_copy(r, spot, (pair + half, rows * side + r)).start(),
        )

    for b in range(spread):
        split(
            comes[b],
            lambda b=b: x_local(b, side * spread + b).wait(),
            lambda b=b: x_copy(0, b, sibling, side * spread + b).wait_recv(),
        )
        forward(b, side * spread).start()

    def token_block(which):
        return pl.ds(pl.multiple_of(which, tokens), tokens)

    def cols(i, n=256):
        return pl.ds(pl.multiple_of(i * n, 128), n)

    loaded("q")
    loaded("k")
    loaded("v")

    def project(which, also_query):
        def body(i, _):
            xb = xf[token_block(which)]
            c = cols(i)
            if also_query:
                qs[:, c] = (product(xb, wproj[0, :, c]) + bq[:, c]).astype(BF16) * BF16(0.125)
            key[token_block(which), c] = product(xb, wproj[1, :, c]).astype(BF16)
            val[token_block(which), c] = (product(xb, wproj[2, :, c]) + bv[:, c]).astype(BF16)
            return 0

        lax.fori_loop(0, D // 256, body, 0)

    project(own, True)

    for p in range(seq_size):
        split(
            jnp.logical_and(sq // rows == side, p == sq),
            lambda: s_local(0).wait(),
            lambda p=p: s_copy(0, 0, p, sibling).wait_recv(),
        )
    diagonal = lax.broadcasted_iota(jnp.int32, (length, length), 0) == lax.broadcasted_iota(
        jnp.int32, (length, length), 1
    )
    for b in range(spread):
        mine_seg = jnp.broadcast_to(sg[side * spread + b], (length, length))
        column = jnp.sum(jnp.where(diagonal, mine_seg, 0), axis=1, keepdims=True)
        for p in range(seq_size):
            seen = jnp.broadcast_to(column, (length, length)) == jnp.broadcast_to(sg[p], (length, length))
            mask[b * length : (b + 1) * length, p * length : (p + 1) * length] = jnp.where(seen, 0.0, MASKED)

    for b in range(spread):
        forward(b, (1 - side) * spread).wait_recv()
    project(far, False)

    lane = lax.broadcasted_iota(jnp.int32, (1, 128), 1)
    first = (lane < HD).astype(BF16)
    picks = (first, BF16(1.0) - first)
    low_lanes = lane < HD

    def attend(i, _):
        c = cols(i, 128)
        qp, kp, vp = qs[:, c], key[:, c], val[:, c]
        outs = []
        for n in range(2):
            s = product_nt(qp * picks[n], kp) + mask[...]
            e = jnp.exp(s - jnp.max(s, axis=-1, keepdims=True))
            p = (e * (1.0 / jnp.sum(e, axis=-1, keepdims=True))).astype(BF16)
            probs[2 * i + n] = p
            outs.append(product(p, vp))
        attn[:, c] = jnp.where(low_lanes, outs[0], outs[1]).astype(BF16)
        return 0

    lax.fori_loop(0, D // 128, attend, 0)

    loaded("o")

    def branch(i, _):
        c = cols(i)
        acc[:, c] = product(attn[...], wproj[3, :, c]) + bo[:, c] + xf[token_block(own), c].astype(F32)
        return 0

    lax.fori_loop(0, D // 256, branch, 0)
    step = 32

    def chunk(i):
        return pl.ds(pl.multiple_of(i * step, step), step)

    def norm_one(i, _):
        r = chunk(i)
        v = acc[r]
        centre = v - jnp.mean(v, axis=-1, keepdims=True)
        inv = lax.rsqrt(jnp.mean(centre * centre, axis=-1, keepdims=True) + EPSILON)
        n = centre * inv
        normed[r] = n
        inv1[r] = jnp.broadcast_to(inv, (step, 128))
        hid[r] = (n * g1[...] + s1[...]).astype(BF16)
        return 0

    lax.fori_loop(0, tokens // step, norm_one, 0)

    loaded("in")
    loaded("out")

    def inner_cols(j, i):
        return total.at[pl.ds(INNER + j * D, D), cols(i)]

    for j in range(4):

        def expand(i, _, j=j):
            c = cols(j * 3 + i)
            v = product(hid[...], inner_cols(j, i)[...]) + bi[:, c]
            cdf = 0.5 * (1.0 + lax.erf(v * INV_ROOT_TWO))
            active[:, c] = (v * cdf).astype(BF16)
            slope[:, c] = cdf + v * DENSITY * jnp.exp(-0.5 * v * v)
            return 0

        lax.fori_loop(0, 3, expand, 0)

    def contract(i, _):
        c = cols(i)
        acc[:, c] = product(active[...], total[pl.ds(PROJ, FF), c]) + b2[:, c]
        return 0

    lax.fori_loop(0, D // 256, contract, 0)
    for b in range(spread):
        split(comes[b], lambda b=b: c_local(b, b).wait(), lambda b=b: c_copy(0, b, sibling).wait_recv())

    small[0] = jnp.zeros((16, D), F32)

    def norm_two(i, carry):
        d_gain, d_shift, d_bias = carry
        r = chunk(i)
        v = normed[r] * g1[...] + s1[...] + acc[r]
        centre = v - jnp.mean(v, axis=-1, keepdims=True)
        inv = lax.rsqrt(jnp.mean(centre * centre, axis=-1, keepdims=True) + EPSILON)
        n = centre * inv
        ybuf[r] = (n * g2[...] + s2[...]).astype(BF16)
        g = cot[r].astype(F32)
        scaled = g * g2[...]
        grad = inv * (
            scaled - jnp.mean(scaled, axis=-1, keepdims=True) - n * jnp.mean(scaled * n, axis=-1, keepdims=True)
        )
        grad_low = grad.astype(BF16)
        gout[r] = grad_low
        acc[r] = grad
        return d_gain + fold(g * n), d_shift + fold(g), d_bias + fold(grad_low.astype(F32))

    zero = jnp.zeros((8, D), F32)
    sums = lax.fori_loop(0, tokens // step, norm_two, (zero, zero, zero))
    for at, v in zip((6, 7, 5), sums):
        small[0, at : at + 1] = jnp.sum(v, axis=0, keepdims=True)

    homes = [(pair + sq // rows, side * spread + b) for b in range(spread)]
    at_home = [jnp.logical_and(h[0] == dp, h[1] == sq) for h in homes]

    def back(src, dst, b, lane_, to, slot):
        return pltpu.make_async_remote_copy(
            src.at[pl.ds(b * length, length)], dst.at[slot], ys.at[lane_, b], yr.at[lane_, slot], to, MESH
        )

    def home_local(src, dst, b, lane_):
        return pltpu.make_async_copy(src.at[pl.ds(b * length, length)], dst.at[sq % rows], xs.at[2 + lane_])

    def send_home(src, dst, lane_):
        for b in range(spread):
            split(
                at_home[b],
                lambda b=b: home_local(src, dst, b, lane_).start(),
                lambda b=b: back(src, dst, b, lane_, homes[b], sq % rows).start(),
            )

    def sent_home(src, dst, lane_):
        for b in range(spread):
            split(
                at_home[b],
                lambda b=b: home_local(src, dst, b, lane_).wait(),
                lambda b=b: back(src, dst, b, lane_, homes[b], sq % rows).wait_send(),
            )
        for r in range(rows):
            pl.when(jnp.logical_not(jnp.logical_and(half == side, sq == rows * side + r)))(
                lambda r=r: back(src, dst, 0, lane_, sibling, r).wait_recv()
            )

    send_home(ybuf, y_out, 0)


    def outer_part(n):
        def body(i, _):
            t = n * 6 + i
            total[pl.ds(pl.multiple_of(OUTER + t * 256, 256), 256)] = product(
                active[:, cols(t)].T, gout[...]
            ).astype(BF16)
            return 0

        lax.fori_loop(0, 6, body, 0)

    def inner_part(j):
        if j == 0:
            for i in range(3):
                hid_t[i * 256 : (i + 1) * 256] = hid[:, i * 256 : (i + 1) * 256].T

        def body(i, _):
            t = j * 3 + i
            up = product_nt(gout[...], total[pl.ds(pl.multiple_of(PROJ + t * 256, 256), 256)])
            gi = (up * slope[:, cols(t)]).astype(BF16)
            small[0, 8 + j : 9 + j, cols(i)] = jnp.sum(fold(gi.astype(F32)), axis=0, keepdims=True)
            view = inner_cols(j, i)
            acc[...] += product_nt(gi, view[...])
            view[...] = product(hid_t[...], gi).astype(BF16)
            return 0

        lax.fori_loop(0, 3, body, 0)

    def norm_one_part():
        def body(i, carry):
            d_gain, d_shift, d_bias = carry
            r = chunk(i)
            g, n = acc[r], normed[r]
            scaled = g * g1[...]
            grad = inv1[r][:, :1] * (
                scaled - jnp.mean(scaled, axis=-1, keepdims=True) - n * jnp.mean(scaled * n, axis=-1, keepdims=True)
            )
            grad_low = grad.astype(BF16)
            gout[r] = grad_low
            acc[r] = grad
            return d_gain + fold(g * n), d_shift + fold(g), d_bias + fold(grad_low.astype(F32))

        out = lax.fori_loop(0, tokens // step, body, (zero, zero, zero))
        for at, v in zip((3, 4, 2), out):
            small[0, at : at + 1] = jnp.sum(v, axis=0, keepdims=True)

    def branch_part():
        def body(i, _):
            total[pl.ds(pl.multiple_of(PROJ + i * 256, 256), 256)] = product(attn[:, cols(i)].T, gout[...]).astype(BF16)
            cot[:, cols(i)] = product_nt(gout[...], wproj[3, pl.ds(pl.multiple_of(i * 256, 256), 256)]).astype(BF16)
            return 0

        lax.fori_loop(0, D // 256, body, 0)

    def attention_part(n):
        def body(m, _):
            i = n * 2 + m
            c = cols(i, 128)
            qp, kp, vp, gp = qs[:, c], key[:, c], val[:, c], cot[:, c]
            dq, dk, dv = [], [], []
            for h in range(2):
                p = probs[2 * i + h]
                pf = p.astype(F32)
                weighted = pf * product_nt(gp * picks[h], vp)
                delta = jnp.sum(weighted, axis=-1, keepdims=True)
                gs = (weighted - pf * delta).astype(BF16)
                dq.append(product(gs, kp))
                dk.append(product_tn(gs, qp))
                dv.append(product_tn(p, gp))
            gq = (jnp.where(low_lanes, dq[0], dq[1]) * 0.125).astype(BF16)
            gk = jnp.where(low_lanes, dk[0], dk[1]).astype(BF16)
            gv = jnp.where(low_lanes, dv[0], dv[1]).astype(BF16)
            qs[:, c] = gq
            small[0, 0:1, c] = jnp.sum(fold(gq.astype(F32)), axis=0, keepdims=True)
            small[0, 1:2, c] = jnp.sum(fold(gv.astype(F32)), axis=0, keepdims=True)
            for b in range(2):
                active[:, cols(b * 6 + i, 128)] = gk[b * tokens : (b + 1) * tokens]
                active[:, cols(12 + b * 6 + i, 128)] = gv[b * tokens : (b + 1) * tokens]
            return 0

        lax.fori_loop(0, 2, body, 0)

    def query_part():
        def body(i, _):
            total[pl.ds(pl.multiple_of(PROJ + D + i * 256, 256), 256)] = product(
                xf[token_block(own), cols(i)].T, qs[...]
            ).astype(BF16)
            return 0

        lax.fori_loop(0, D // 256, body, 0)

    def key_part():
        def body(i, _):
            left = xf[pl.ds(0, tokens), cols(i)].T
            right = xf[pl.ds(tokens, tokens), cols(i)].T
            for n in range(2):
                base = n * 2 * D
                total[pl.ds(pl.multiple_of(PROJ + (2 + n) * D + i * 256, 256), 256)] = (
                    product(left, active[:, base : base + D]) + product(right, active[:, base + D : base + 2 * D])
                ).astype(BF16)
            return 0

        lax.fori_loop(0, D // 256, body, 0)

    dx_send = pltpu.make_async_remote_copy(hid, dx_far, xs.at[0], xs.at[1], sibling, MESH)

    def input_part():
        def both(s, w):
            return product_nt(active[:, pl.ds(pl.multiple_of(s * D, 128), D)], wproj[1, w]) + product_nt(
                active[:, pl.ds(pl.multiple_of((2 + s) * D, 128), D)], wproj[2, w]
            )

        def body(i, _):
            w = pl.ds(pl.multiple_of(i * 256, 256), 256)
            hid[:, cols(i)] = both(1 - side, w).astype(BF16)
            acc[:, cols(i)] += product_nt(qs[...], wproj[0, w]) + both(side, w)
            return 0

        lax.fori_loop(0, D // 256, body, 0)
        dx_send.start()

    bits = small_bits(plan.dp_size, seq_size)

    def small_copy(i):
        axis, bit = bits[i]
        if axis == "dp":
            tgt = (dp + bit * (1 - 2 * ((dp // bit) % 2)), sq)
        else:
            tgt = (dp, sq + bit * (1 - 2 * ((sq // bit) % 2)))
        return pltpu.make_async_remote_copy(small.at[i], small.at[len(bits) + 1 + i], ms.at[i], mr.at[i], tgt, MESH)

    def input_end():
        dx_send.wait_recv()

        def body(i, _):
            r = chunk(i)
            gout[r] = (acc[r] + dx_far[r].astype(F32)).astype(BF16)
            return 0

        lax.fori_loop(0, tokens // step, body, 0)
        send_home(gout, dx_out, 1)
        small_copy(0).start()

    def small_part(n):
        for i in range(n, n + 1 if n < SMALL_PARTS - 1 else len(bits)):
            small_copy(i).wait_recv()
            small[i + 1] = small[i] + small[len(bits) + 1 + i]
            if i + 1 < len(bits):
                small_copy(i + 1).start()

    parts = (
        [functools.partial(outer_part, n) for n in range(2)]
        + [functools.partial(inner_part, j) for j in range(4)]
        + [norm_one_part, branch_part]
        + [functools.partial(attention_part, n) for n in range(3)]
        + [query_part, key_part, input_part, input_end]
        + [functools.partial(small_part, n) for n in range(SMALL_PARTS)]
    )
    ready = {0: (0,), 1: (1,), 3: (2,), 5: (3,), 11: (4,), 12: (5,)}
    scripts = [iter(plan.script(p)) for p in plan.pieces]
    for entry in ORDER:
        if entry >= 0:
            next(scripts[entry])[1]()
            continue
        parts[-entry - 1]()
        for g in ready.get(-entry - 1, ()):
            for p in plan.pieces[3 * g : 3 * g + 3]:
                plan.rs_start(p, 0)
    small_out[...] = small[len(bits)]
    for i in range(len(bits)):
        small_copy(i).wait_send()
    dx_send.wait_send()
    sent_home(ybuf, y_out, 0)
    sent_home(gout, dx_out, 1)
    for r in range(rows):
        for c in range(2):
            pl.when(jnp.logical_not(mine[r][c]))(lambda r=r, c=c: s_copy(r, c, sq, sibling).wait_send())
        pl.when(jnp.logical_not(stays[r]))(lambda r=r: x_copy(r, spot, sibling, 0).wait_send())
        pl.when(jnp.logical_not(stays[r]))(lambda r=r: c_copy(r, spot, sibling).wait_send())
    for b in range(spread):
        forward(b, side * spread).wait_send()
    plan.finish()


def whole_layer(args, dp_size, seq_size):
    (layer_input, segment_ids, w_query, b_query, w_key, w_value, b_value, w_out, b_out, gain_one, shift_one,
     w_inner, b_inner, w_outer, b_outer, gain_two, shift_two, cotangent) = args
    plan = Exchange(dp_size, seq_size, 6)
    rows, length, width = layer_input.shape
    tokens = seq_size * length // 2
    vmem, anyw = pl.BlockSpec(memory_space=pltpu.VMEM), pl.BlockSpec(memory_space=pl.ANY)
    nbits = len(small_bits(dp_size, seq_size))
    back = pltpu.VMEM((rows, length, width), BF16)
    dma = pltpu.SemaphoreType.DMA
    return pl.pallas_call(
        functools.partial(layer_kernel, plan, seq_size),
        out_shape=(pltpu.VMEM((3 * FF, D), BF16), pltpu.VMEM((16, D), F32), back, back),
        in_specs=[anyw] * 9 + [vmem] * 9,
        out_specs=(vmem,) * 4,
        scratch_shapes=[
            pltpu.VMEM((3 * FF, D), BF16),
            pltpu.VMEM((plan.slots, D), BF16),
            pltpu.VMEM((4, D, D), BF16),
            pltpu.VMEM((2 * tokens, D), BF16),
            pltpu.VMEM((tokens, D), BF16),
            pltpu.VMEM((2 * tokens, D), BF16),
            pltpu.VMEM((2 * tokens, D), BF16),
            pltpu.VMEM((D // HD, tokens, 2 * tokens), BF16),
            pltpu.VMEM((tokens, D), BF16),
            pltpu.VMEM((tokens, D), F32),
            pltpu.VMEM((tokens, 128), F32),
            pltpu.VMEM((tokens, D), BF16),
            pltpu.VMEM((D, tokens), BF16),
            pltpu.VMEM((tokens, FF), BF16),
            pltpu.VMEM((tokens, FF), F32),
            pltpu.VMEM((tokens, D), BF16),
            pltpu.VMEM((tokens, D), BF16),
            pltpu.VMEM((tokens, D), BF16),
            pltpu.VMEM((tokens, D), F32),
            pltpu.VMEM((tokens, 2 * tokens), F32),
            pltpu.VMEM((seq_size, 1, length), jnp.int32),
            pltpu.VMEM((tokens, D), BF16),
            pltpu.VMEM((2 * nbits + 1, 16, D), F32),
            dma((plan.sems,)), dma((plan.sems,)),
            dma((5, 2)), dma((4, seq_size)), dma((3,)), dma((9,)),
            dma((nbits,)), dma((nbits,)), dma((2, 2)), dma((2, 2)), dma((4,)),
        ],
        compiler_params=pltpu.CompilerParams(collective_id=1, has_side_effects=True, vmem_limit_bytes=VMEM_LIMIT),
        name="layer",
    )(
        layer_input, cotangent, segment_ids.reshape(rows, 1, length), w_query, w_key, w_value, w_out, w_inner, w_outer,
        b_query, b_value, b_out, gain_one, shift_one, b_inner, b_outer, gain_two, shift_two,
    )


VMEM_LIMIT = 46 << 20


def widen_kernel(sums, small, y_in, dx_in, *refs):
    outs, (wide, sem, far) = refs[:17], refs[17:]
    (y, dx, d_query, d_b_query, d_key, d_value, d_b_value, d_out, d_b_out, d_gain_one, d_shift_one, d_inner,
     d_b_inner, d_outer, d_b_outer, d_gain_two, d_shift_two) = outs
    rows = [pltpu.make_async_copy(y_in, y, far.at[0]), pltpu.make_async_copy(dx_in, dx, far.at[1])]
    for c in rows:
        c.start()
    for i, o in enumerate((d_b_query, d_b_value, d_b_out, d_gain_one, d_shift_one, d_b_outer, d_gain_two, d_shift_two)):
        o[...] = small[i]
    for j in range(4):
        d_b_inner[j * D : (j + 1) * D] = small[8 + j]
    step = 384
    copies = []
    for n in range(3 * FF // step):
        at = n * step
        if at < INNER:
            view = d_outer.at[pl.ds(at, step)]
        elif at < PROJ:
            j, row = (at - INNER) // D, (at - INNER) % D
            view = d_inner.at[pl.ds(row, step), pl.ds(j * D, D)]
        else:
            j, row = (at - PROJ) // D, (at - PROJ) % D
            view = (d_out, d_query, d_key, d_value)[j].at[pl.ds(row, step)]
        slot = n % 4
        if n >= 4:
            copies[n - 4].wait()

        def body(i, _, at=at, slot=slot):
            wide[slot, pl.ds(pl.multiple_of(i * 32, 32), 32)] = sums[pl.ds(pl.multiple_of(at + i * 32, 32), 32)].astype(F32)
            return 0

        lax.fori_loop(0, step // 32, body, 0)
        copies.append(pltpu.make_async_copy(wide.at[slot], view, sem.at[slot]))
        copies[-1].start()
    for c in copies[-4:] + rows:
        c.wait()


def widen(sums, small, y, dx):
    vmem, anyw = pl.BlockSpec(memory_space=pltpu.VMEM), pl.BlockSpec(memory_space=pl.ANY)
    back = jax.ShapeDtypeStruct(y.shape, BF16)
    square, vector = jax.ShapeDtypeStruct((D, D), F32), jax.ShapeDtypeStruct((D,), F32)
    shapes = (
        back, back, square, vector, square, square, vector, square, vector, vector, vector,
        jax.ShapeDtypeStruct((D, FF), F32), jax.ShapeDtypeStruct((FF,), F32), jax.ShapeDtypeStruct((FF, D), F32),
        vector, vector, vector,
    )
    return pl.pallas_call(
        widen_kernel,
        out_shape=shapes,
        in_specs=[vmem] * 4,
        out_specs=tuple(vmem if len(o.shape) == 1 else anyw for o in shapes),
        scratch_shapes=[
            pltpu.VMEM((4, 384, D), F32), pltpu.SemaphoreType.DMA((4,)), pltpu.SemaphoreType.DMA((2,)),
        ],
        compiler_params=pltpu.CompilerParams(vmem_limit_bytes=16 << 20),
        name="widen",
    )(sums, small, y, dx)


def on_device(dp_size, seq_size, *args):
    return widen(*whole_layer(args, dp_size, seq_size))


def solution(mesh):
    sizes = (mesh.shape["dp"], mesh.shape["seq"])
    tokens = P("dp", "seq", None)
    return jax.shard_map(
        functools.partial(on_device, *sizes),
        mesh=mesh,
        in_specs=(tokens, P("dp", "seq")) + (P(),) * 15 + (tokens,),
        out_specs=(tokens, tokens) + (P(),) * 15,
        check_vma=False,
    )
```

```python
import functools

import jax
import jax.numpy as jnp
from jax import lax
from jax.experimental import pallas as pl
from jax.experimental.pallas import tpu as pltpu
from jax.sharding import PartitionSpec as P

HD = 64
EPSILON = 1e-12
MASKED = -1000000000.0
INV_ROOT_TWO = 0.7071067811865476
DENSITY = 0.3989422804014327
MESH = pl.DeviceIdType.MESH
BF16 = jnp.bfloat16
F32 = jnp.float32


def product(left, right):
    return jnp.dot(left, right, preferred_element_type=F32)


def product_tn(left, right):
    return lax.dot_general(left, right, (((0,), (0,)), ((), ())), preferred_element_type=F32)


def product_nt(left, right):
    return lax.dot_general(left, right, (((1,), (1,)), ((), ())), preferred_element_type=F32)


def place(seq_size):
    dp, sq = lax.axis_index("dp"), lax.axis_index("seq")
    side = dp % 2
    return dp, sq, side, dp - side


GROUP = 1536
PIECE = 512
ORDERS = (("xyz", "yxz", "zxy"), ("xyz", "yxz", "zyx"), ("xyz", "yxz", "zxy"), ("xyz", "yxz", "zyx"), ("xyz", "yxz", "yzx"), ("xyz", "yxz", "xzy"))
SUBS = 1
LANES = "cxyz"


class Exchange:
    def __init__(self, dp_size, seq_size, groups):
        self.dp_size, self.seq_size, self.groups = dp_size, seq_size, groups
        self.extra = []
        bit = 8
        while bit < dp_size:
            self.extra.append(bit)
            bit *= 2
        self.sems = 0
        self.slots = 0
        self.pieces = []
        for g in range(groups):
            for cls in range(3):
                self.pieces.append(self.plan(g * GROUP + cls * PIECE, ORDERS[g % len(ORDERS)][cls]))

    def sem(self):
        self.sems += 1
        return self.sems - 1

    def slot(self, rows):
        self.slots += rows
        return self.slots - rows

    def plan(self, base, order):
        stages, rows, ends = [], PIECE, False
        for axis in "c" + order:
            half = rows // 2
            st = dict(axis=axis, rows=half, ends=ends)
            if axis == "z":
                n = half // SUBS
                st["down"] = [dict(rs=self.sem(), ag=self.sem(), slot=self.slot(n), rows=n, at=i * n) for i in range(SUBS)]
                st["up"] = [dict(rs=self.sem(), ag=self.sem(), slot=self.slot(n), rows=n, at=i * n) for i in range(SUBS)]
                ends = True
            else:
                st.update(rs=self.sem(), ag=self.sem(), slot=None if axis == "c" else self.slot(half))
            stages.append(st)
            rows = half
        more = [dict(bit=b, rs=self.sem(), slot=self.slot(rows)) for b in self.extra]
        return dict(base=base, stages=stages, more=more, rows=rows)

    def bind(self, total, slots, final, send_sem, recv_sem):
        self.total, self.landing, self.final = total, slots, final
        self.ss, self.rs = send_sem, recv_sem
        dp, sq = lax.axis_index("dp"), lax.axis_index("seq")
        self.dp, self.sq = dp, sq
        self.bits = {"c": (1, dp % 2), "x": (2, (dp // 2) % 2), "y": (4, (dp // 4) % 2)}
        self.last = self.seq_size - 1
        self.edge = jnp.logical_or(sq == 0, sq == self.last)
        self.side = sq // self.last
        self.rows_sent = {}
        for p in self.pieces:
            off = p["base"]
            for st in p["stages"]:
                half = st["rows"]
                st["off"] = off
                value = self.side if st["axis"] == "z" else self.bits[st["axis"]][1]
                st["keep"] = off + value * half
                st["give"] = off + (1 - value) * half
                off = st["keep"]
            p["own"] = off

    def view(self, off, rows):
        return self.total.at[pl.ds(pl.multiple_of(off, 16), rows)]

    def partner(self, axis):
        bit, value = self.bits[axis]
        return (self.dp + bit * (1 - 2 * value), self.sq)

    def copy(self, src, dst, lane, sem, tgt):
        return pltpu.make_async_remote_copy(src, dst, self.ss.at[lane], self.rs.at[sem], tgt, MESH)

    def send(self, copy, lane, rows, who):
        copy.start()
        for place_ in who:
            self.rows_sent[lane, place_] = self.rows_sent.get((lane, place_), 0) + rows

    def everyone(self, st):
        return (0, self.last) if st["ends"] else range(self.seq_size)

    def gated(self, when, f):
        if when is None:
            f()
        else:
            pl.when(when)(f)

    def done(self, off, rows):
        return self.final.at[pl.ds(pl.multiple_of(off, 16), rows)]

    def landed(self, st):
        if st["slot"] is None:
            return self.done(st["give"], st["rows"])
        return self.landing.at[pl.ds(st["slot"], st["rows"])]

    def add(self, off, slot, rows, into=None):
        into = self.total if into is None else into
        source = self.final if slot is None else self.landing
        slot = off if slot is None else slot
        step = 32 if rows % 32 == 0 else 16

        def body(i, _):
            at = pl.multiple_of(off + i * step, 16)
            frm = pl.multiple_of(slot + i * step, 16)
            into[pl.ds(at, step)] = self.total[pl.ds(at, step)] + source[pl.ds(frm, step)]
            return 0

        lax.fori_loop(0, rows // step, body, 0)


    def rs_start(self, p, i):
        st = p["stages"][i]
        if st["axis"] == "z":
            for way, at, to, base in (("down", self.last, -1, 0), ("up", 0, 1, st["rows"])):
                when = self.sq == at

                def f(way=way, at=at, to=to, base=base):
                    for s in st[way]:
                        self.send(self.rs_copy(st, s, base, to), LANES.index("z"), s["rows"], (at,))
                self.gated(when, f)
        else:
            when = self.edge if st["ends"] else None

            def f():
                self.send(self.rs_pair(st), LANES.index(st["axis"]), st["rows"], self.everyone(st))
            self.gated(when, f)

    def rs_pair(self, st):
        return self.copy(
            self.view(st["give"], st["rows"]), self.landed(st), LANES.index(st["axis"]), st["rs"], self.partner(st["axis"])
        )

    def rs_hyper(self, p, i):
        st = p["stages"][i]

        def f():
            self.rs_pair(st).wait_recv()
            self.add(st["keep"], st["slot"], st["rows"], self.final if i + 1 == len(p["stages"]) else None)
        self.gated(self.edge if st["ends"] else None, f)

    def rs_hop(self, p, i, hop):
        st = p["stages"][i]
        for way, at, to, base in (("down", self.last - hop, -1, 0), ("up", hop, 1, st["rows"])):
            when = self.sq == at

            def f(way=way, at=at, to=to, base=base):
                for s in st[way]:
                    self.rs_copy(st, s, base, -to).wait_recv()
                    ended = hop == self.last and i + 1 == len(p["stages"])
                    self.add(st["off"] + base + s["at"], s["slot"], s["rows"], self.final if ended else None)
                    if hop < self.last:
                        self.send(self.rs_copy(st, s, base, to), LANES.index("z"), s["rows"], (at,))
            self.gated(when, f)

    def rs_copy(self, st, s, base, to):
        return self.copy(
            self.view(st["off"] + base + s["at"], s["rows"]), self.landing.at[pl.ds(s["slot"], s["rows"])],
            LANES.index("z"), s["rs"], (self.dp, self.sq + to),
        )

    def more(self, p):
        for m in p["more"]:
            bit = m["bit"]
            value = (self.dp // bit) % 2
            tgt = (self.dp + bit * (1 - 2 * value), self.sq)

            def f():
                c = self.copy(
                    self.done(p["own"], p["rows"]), self.landing.at[pl.ds(m["slot"], p["rows"])], len(LANES) * 2, m["rs"], tgt
                )
                c.start()
                c.wait()
                part = pl.ds(pl.multiple_of(p["own"], 16), p["rows"])
                self.final[part] = self.final[part] + self.landing[pl.ds(m["slot"], p["rows"])]
            self.gated(self.edge, f)


    def ag_start(self, p, i):
        st = p["stages"][i]
        if st["axis"] == "z":
            for way, at, to, base in (("down", self.last, -1, st["rows"]), ("up", 0, 1, 0)):
                when = self.sq == at

                def f(way=way, at=at, to=to, base=base):
                    for s in st[way]:
                        self.send(self.ag_copy(st, s, base, to), len(LANES) + LANES.index("z"), s["rows"], (at,))
                self.gated(when, f)
        else:
            when = self.edge if st["ends"] else None

            def f():
                self.send(
                    self.ag_pair(st, st["keep"]), len(LANES) + LANES.index(st["axis"]), st["rows"], self.everyone(st)
                )
            self.gated(when, f)

    def ag_copy(self, st, s, base, to):
        part = self.done(st["off"] + base + s["at"], s["rows"])
        return self.copy(part, part, len(LANES) + LANES.index("z"), s["ag"], (self.dp, self.sq + to))

    def ag_pair(self, st, off):
        part = self.done(off, st["rows"])
        return self.copy(part, part, len(LANES) + LANES.index(st["axis"]), st["ag"], self.partner(st["axis"]))

    def ag_hyper(self, p, i):
        st = p["stages"][i]

        def f():
            self.ag_pair(st, st["give"]).wait_recv()
        self.gated(self.edge if st["ends"] else None, f)

    def ag_hop(self, p, i, hop):
        st = p["stages"][i]
        for way, at, to, base in (("down", self.last - hop, -1, st["rows"]), ("up", hop, 1, 0)):
            when = self.sq == at

            def f(way=way, at=at, to=to, base=base):
                for s in st[way]:
                    self.ag_copy(st, s, base, -to).wait_recv()
                    if hop < self.last:
                        self.send(self.ag_copy(st, s, base, to), len(LANES) + LANES.index("z"), s["rows"], (at,))
            self.gated(when, f)

    def script(self, p):
        steps, n = [], len(p["stages"])
        for i, st in enumerate(p["stages"]):
            after = (lambda i=i: self.rs_start(p, i + 1)) if i + 1 < n else (lambda: (self.more(p), self.ag_start(p, n - 1)))
            if st["axis"] == "z":
                for hop in range(1, self.last + 1):
                    def step(i=i, hop=hop, after=after):
                        self.rs_hop(p, i, hop)
                        if hop == self.last:
                            after()
                    steps.append((f"rz{hop}", step))
            else:
                def step(i=i, after=after):
                    self.rs_hyper(p, i)
                    after()
                steps.append(("r" + st["axis"], step))
        for i in reversed(range(n)):
            st = p["stages"][i]
            after = (lambda i=i: self.ag_start(p, i - 1)) if i > 0 else (lambda: None)
            if st["axis"] == "z":
                for hop in range(1, self.last + 1):
                    def step(i=i, hop=hop, after=after):
                        self.ag_hop(p, i, hop)
                        if hop == self.last:
                            after()
                    steps.append((f"gz{hop}", step))
            else:
                def step(i=i, after=after):
                    self.ag_hyper(p, i)
                    after()
                steps.append(("g" + st["axis"], step))
        return steps

    def finish(self):
        for lane in range(2 * len(LANES)):
            rows = [self.rows_sent[lane, p] for p in range(self.seq_size)]

            def f(n, lane=lane):
                self.copy(self.total.at[pl.ds(0, n)], self.total.at[pl.ds(0, n)], lane, 0, self.partner("c")).wait_send()

            if min(rows) == max(rows):
                f(rows[0])
            else:
                for p in range(self.seq_size):
                    pl.when(self.sq == p)(functools.partial(f, rows[p]))


def small_bits(dp_size, seq_size):
    out, bit = [], 1
    while bit < dp_size:
        out.append(("dp", bit))
        bit *= 2
    bit = 1
    while bit < seq_size:
        out.append(("seq", bit))
        bit *= 2
    return out


D = 768
FF = 3072
OUTER, INNER, PROJ = 0, 3072, 6144
ORDER = (
    -1, -2, 0, -3, 1, 2, 3, 4, -4, 5, -5, 0, 6, 7, 1, 2, 8, -6, 3, -7, 4, 5, -8, 9,
    10, 0, 6, -9, 1, 8, 2, 11, -10, 0, 5, 4, 1, 7, -11, 3, -12, 9, 8, 2, -13, 0, 13, 12,
    1, 4, 14, 6, 10, 11, 15, 2, 5, 7, 16, 3, 9, -14, -15, 17, 6, 4, 7, 8, 9, 0, 12, 13,
    1, 11, 10, 3, 14, -16, 2, 15, 0, 5, 4, 1, 10, 17, 6, 16, 14, 8, 11, 7, -17, 4, 3, 9,
    12, 13, 0, 17, 6, 2, 5, 1, 7, 3, 10, -18, 15, 16, 12, 9, 0, 8, 13, 14, 1, 2, 6, 4,
    10, 11, -19, 5, 7, 15, 17, 0, 16, 3, 14, 1, 8, 9, 12, 4, 11, -20, 13, 5, 6, 17, 7, 3,
    2, 15, 12, 0, 10, 16, 13, 14, 1, 9, 6, 0, 17, 7, 8, 1, 15, 3, 5, 16, 4, 12, 2, 9,
    11, 6, 13, 10, 14, 17, 7, 8, 5, 4, 15, 12, 2, 16, 13, 10, 4, 9, 3, 2, 14, 11, 3, 17,
    8, 5, 6, 15, 12, 16, 13, 5, 10, 7, 6, 14, 11, 7, 12, 17, 8, 9, 15, 16, 8, 13, 9, 10,
    14, 11, 10, 15, 17, 12, 12, 16, 13, 11, 13, 15, 11, 14, 15, 14, 17, 16, 17, 16,
)


SMALL_PARTS = 5


class Row:
    def __init__(self, ref):
        self.ref = ref

    def __getitem__(self, at):
        return (self.ref[...] if at is Ellipsis else self.ref[at[1]]).reshape(1, -1)


def fold(values):
    return jnp.sum(values.reshape(values.shape[0] // 8, 8, values.shape[1]), axis=0)


def layer_kernel(plan, seq_size, *refs):
    x_ref, cot_ref, seg_ref, wq_hbm, wk_hbm, wv_hbm, wo_hbm, win_hbm, wout_hbm = refs[:9]
    vectors_hbm, vectors = refs[9:18], refs[-9:]
    final, small_out, y_out, dx_out = refs[18:22]
    (total, landing, wproj, xf, qs, key, val, probs, attn, normed, inv1, hid, hid_t, active, slope, cot, ybuf, gout, acc,
     mask, sg, dx_far, small, ss, rs, gs_, gr, gl, ws, ms, mr, ys, yr, xs) = refs[22:-9]
    plan.bind(total, landing, final, ss, rs)
    bq, bv, bo, g1, s1, bi, b2, g2, s2 = (Row(v) for v in vectors)
    dp, sq, side, pair = place(seq_size)
    sibling = (dp + 1 - 2 * side, sq)
    rows, length = x_ref.shape[0], x_ref.shape[1]
    spread = seq_size // 2
    tokens = spread * length
    own, far = side * tokens, (1 - side) * tokens

    barrier = pltpu.get_barrier_semaphore()
    column = [(pair + c, p) for p in range(seq_size) for c in range(2)]
    for to in column:
        pl.when(jnp.logical_not(jnp.logical_and(to[0] == dp, to[1] == sq)))(
            lambda to=to: pl.semaphore_signal(barrier, inc=1, device_id=to, device_id_type=MESH)
        )
    across = [bit for axis, bit in small_bits(plan.dp_size, seq_size) if axis == "dp" and bit > 1]
    for bit in across:
        to = (dp + bit * (1 - 2 * ((dp // bit) % 2)), sq)
        pl.semaphore_signal(barrier, inc=1, device_id=to, device_id_type=MESH)

    loads = {}

    def load(name, src, dst, i):
        loads.setdefault(name, []).append(pltpu.make_async_copy(src, dst, ws.at[i]))
        loads[name][-1].start()

    for i, (name, src) in enumerate((("q", wq_hbm), ("k", wk_hbm), ("v", wv_hbm), ("o", wo_hbm))):
        load(name, src, wproj.at[i], i)
    for i, (src, dst) in enumerate(zip(vectors_hbm, vectors)):
        load("vectors", src, dst, 9 + i)
    for j in range(4):
        load("in", win_hbm.at[:, pl.ds(j * D, D)], total.at[pl.ds(INNER + j * D, D)], 4 + j)
    load("out", wout_hbm, total.at[pl.ds(PROJ, FF)], 8)

    def loaded(name):
        for c in loads[name]:
            c.wait()

    pl.semaphore_wait(barrier, len(column) - 1 + len(across))

    half, spot = sq // spread, sq % spread

    def block(i):
        return pl.ds(pl.multiple_of(i * length, length), length)

    def x_copy(r, b, tgt, at):
        return pltpu.make_async_remote_copy(x_ref.at[r], xf.at[block(at)], gs_.at[0, r], gr.at[0, b], tgt, MESH)

    def c_copy(r, b, tgt):
        return pltpu.make_async_remote_copy(cot_ref.at[r], cot.at[block(b)], gs_.at[1, r], gr.at[1, b], tgt, MESH)

    def s_copy(r, c, at, tgt):
        return pltpu.make_async_remote_copy(seg_ref.at[r], sg.at[at], gs_.at[2 + c, r], gr.at[2, at], tgt, MESH)

    def forward(b, base):
        part = xf.at[block(base + b)]
        return pltpu.make_async_remote_copy(part, part, gs_.at[4, b], gr.at[3, b], sibling, MESH)

    def split(local, near, remote):
        pl.when(local)(near)
        pl.when(jnp.logical_not(local))(remote)

    stays = [jnp.logical_and(half == side, sq == rows * side + r) for r in range(rows)]
    comes = [jnp.logical_and(sq // rows == side, side * spread + b == sq) for b in range(spread)]

    def x_local(r, at):
        return pltpu.make_async_copy(x_ref.at[r], xf.at[block(at)], gl.at[0])

    def c_local(r, at):
        return pltpu.make_async_copy(cot_ref.at[r], cot.at[block(at)], gl.at[1])

    def s_local(r):
        return pltpu.make_async_copy(seg_ref.at[r], sg.at[sq], gl.at[2])

    mine = [[jnp.logical_and(side == c, sq == rows * side + r) for c in range(2)] for r in range(rows)]
    for r in range(rows):
        for c in range(2):
            split(
                mine[r][c],
                lambda r=r: s_local(r).start(),
                lambda r=r, c=c: s_copy(r, c, sq, (pair + c, rows * side + r)).start(),
            )
    for r in range(rows):
        at = half * spread + spot
        split(
            stays[r],
            lambda r=r, at=at: x_local(r, at).start(),
            lambda r=r, at=at: x_copy(r, spot, (pair + half, rows * side + r), at).start(),
        )

    for b in range(spread):
        split(
            comes[b],
            lambda b=b: x_local(b, side * spread + b).wait(),
            lambda b=b: x_copy(0, b, sibling, side * spread + b).wait_recv(),
        )
        forward(b, side * spread).start()
    for r in range(rows):
        split(
            stays[r],
            lambda r=r: c_local(r, spot).start(),
            lambda r=r: c_copy(r, spot, (pair + half, rows * side + r)).start(),
        )

    def token_block(which):
        return pl.ds(pl.multiple_of(which, tokens), tokens)

    def cols(i, n=256):
        return pl.ds(pl.multiple_of(i * n, 128), n)

    for name in ("vectors", "q", "k", "v"):
        loaded(name)

    def project(which, also_query):
        def body(i, _):
            xb = xf[token_block(which)]
            c = cols(i)
            if also_query:
                qs[:, c] = (product(xb, wproj[0, :, c]) + bq[:, c]).astype(BF16) * BF16(0.125)
            key[token_block(which), c] = product(xb, wproj[1, :, c]).astype(BF16)
            val[token_block(which), c] = (product(xb, wproj[2, :, c]) + bv[:, c]).astype(BF16)
            return 0

        lax.fori_loop(0, D // 256, body, 0)

    project(own, True)

    for p in range(seq_size):
        split(
            jnp.logical_and(sq // rows == side, p == sq),
            lambda: s_local(0).wait(),
            lambda p=p: s_copy(0, 0, p, sibling).wait_recv(),
        )
    diagonal = lax.broadcasted_iota(jnp.int32, (length, length), 0) == lax.broadcasted_iota(
        jnp.int32, (length, length), 1
    )
    for p in range(seq_size):
        column = jnp.sum(jnp.where(diagonal, jnp.broadcast_to(sg[p], (length, length)), 0), axis=1, keepdims=True)
        for b in range(spread):
            seen = jnp.broadcast_to(column, (length, length)) == jnp.broadcast_to(sg[side * spread + b], (length, length))
            mask[p * length : (p + 1) * length, b * length : (b + 1) * length] = jnp.where(seen, 0.0, MASKED)

    for b in range(spread):
        forward(b, (1 - side) * spread).wait_recv()
    project(far, False)

    lane = lax.broadcasted_iota(jnp.int32, (1, 128), 1)
    first = (lane < HD).astype(BF16)
    picks = (first, BF16(1.0) - first)
    low_lanes = lane < HD

    def attend(i, _):
        c = cols(i, 128)
        qp, kp = qs[:, c], key[:, c]
        vt = val[:, c].T
        outs = []
        for n in range(2):
            s = product_nt(kp, qp * picks[n]) + mask[...]
            e = jnp.exp(s - jnp.max(s, axis=0, keepdims=True))
            p = (e * (1.0 / jnp.sum(e, axis=0, keepdims=True))).astype(BF16)
            probs[2 * i + n] = p
            outs.append(product(vt[n * HD : (n + 1) * HD], p))
        attn[:, c] = jnp.concatenate(outs, axis=0).T.astype(BF16)
        return 0

    lax.fori_loop(0, D // 128, attend, 0)

    loaded("o")

    def branch(i, _):
        c = cols(i)
        acc[:, c] = product(attn[...], wproj[3, :, c]) + bo[:, c] + xf[token_block(own), c].astype(F32)
        return 0

    lax.fori_loop(0, D // 256, branch, 0)
    step = 32

    def chunk(i):
        return pl.ds(pl.multiple_of(i * step, step), step)

    def norm_one(i, _):
        r = chunk(i)
        v = acc[r]
        centre = v - jnp.mean(v, axis=-1, keepdims=True)
        inv = lax.rsqrt(jnp.mean(centre * centre, axis=-1, keepdims=True) + EPSILON)
        n = centre * inv
        normed[r] = n
        inv1[r] = jnp.broadcast_to(inv, (step, 128))
        hid[r] = (n * g1[...] + s1[...]).astype(BF16)
        return 0

    lax.fori_loop(0, tokens // step, norm_one, 0)

    loaded("in")
    loaded("out")

    def inner_cols(j, i):
        return total.at[pl.ds(INNER + j * D, D), cols(i)]

    for j in range(4):

        def expand(i, _, j=j):
            c = cols(j * 3 + i)
            v = product(hid[...], inner_cols(j, i)[...]) + bi[:, c]
            cdf = 0.5 * (1.0 + lax.erf(v * INV_ROOT_TWO))
            active[:, c] = (v * cdf).astype(BF16)
            slope[:, c] = cdf + v * DENSITY * jnp.exp(-0.5 * v * v)
            return 0

        lax.fori_loop(0, 3, expand, 0)

    def contract(i, _):
        c = cols(i)
        acc[:, c] = product(active[...], total[pl.ds(PROJ, FF), c]) + b2[:, c]
        return 0

    lax.fori_loop(0, D // 256, contract, 0)
    for b in range(spread):
        split(comes[b], lambda b=b: c_local(b, b).wait(), lambda b=b: c_copy(0, b, sibling).wait_recv())

    small[0] = jnp.zeros((16, D), F32)

    def norm_two(i, carry):
        d_gain, d_shift, d_bias = carry
        r = chunk(i)
        v = normed[r] * g1[...] + s1[...] + acc[r]
        centre = v - jnp.mean(v, axis=-1, keepdims=True)
        inv = lax.rsqrt(jnp.mean(centre * centre, axis=-1, keepdims=True) + EPSILON)
        n = centre * inv
        ybuf[r] = (n * g2[...] + s2[...]).astype(BF16)
        g = cot[r].astype(F32)
        scaled = g * g2[...]
        grad = inv * (
            scaled - jnp.mean(scaled, axis=-1, keepdims=True) - n * jnp.mean(scaled * n, axis=-1, keepdims=True)
        )
        grad_low = grad.astype(BF16)
        gout[r] = grad_low
        acc[r] = grad
        return d_gain + fold(g * n), d_shift + fold(g), d_bias + fold(grad_low.astype(F32))

    zero = jnp.zeros((8, D), F32)
    sums = lax.fori_loop(0, tokens // step, norm_two, (zero, zero, zero))
    for at, v in zip((6, 7, 5), sums):
        small[0, at : at + 1] = jnp.sum(v, axis=0, keepdims=True)

    homes = [(pair + sq // rows, side * spread + b) for b in range(spread)]
    at_home = [jnp.logical_and(h[0] == dp, h[1] == sq) for h in homes]

    def back(src, dst, b, lane_, to, slot):
        return pltpu.make_async_remote_copy(
            src.at[pl.ds(b * length, length)], dst.at[slot], ys.at[lane_, b], yr.at[lane_, slot], to, MESH
        )

    def home_local(src, dst, b, lane_):
        return pltpu.make_async_copy(src.at[pl.ds(b * length, length)], dst.at[sq % rows], xs.at[2 + lane_])

    def send_home(src, dst, lane_):
        for b in range(spread):
            split(
                at_home[b],
                lambda b=b: home_local(src, dst, b, lane_).start(),
                lambda b=b: back(src, dst, b, lane_, homes[b], sq % rows).start(),
            )

    def sent_home(src, dst, lane_):
        for b in range(spread):
            split(
                at_home[b],
                lambda b=b: home_local(src, dst, b, lane_).wait(),
                lambda b=b: back(src, dst, b, lane_, homes[b], sq % rows).wait_send(),
            )
        for r in range(rows):
            pl.when(jnp.logical_not(jnp.logical_and(half == side, sq == rows * side + r)))(
                lambda r=r: back(src, dst, 0, lane_, sibling, r).wait_recv()
            )

    send_home(ybuf, y_out, 0)


    def outer_part(n):
        def body(i, _):
            t = n * 6 + i
            total[pl.ds(pl.multiple_of(OUTER + t * 256, 256), 256)] = product(
                active[:, cols(t)].T, gout[...]
            ).astype(BF16)
            return 0

        lax.fori_loop(0, 6, body, 0)

    def inner_part(j):
        if j == 0:
            for i in range(3):
                hid_t[i * 256 : (i + 1) * 256] = hid[:, i * 256 : (i + 1) * 256].T

        def body(i, _):
            t = j * 3 + i
            up = product_nt(gout[...], total[pl.ds(pl.multiple_of(PROJ + t * 256, 256), 256)])
            gi = (up * slope[:, cols(t)]).astype(BF16)
            small[0, 8 + j : 9 + j, cols(i)] = jnp.sum(fold(gi.astype(F32)), axis=0, keepdims=True)
            view = inner_cols(j, i)
            acc[...] += product_nt(gi, view[...])
            view[...] = product(hid_t[...], gi).astype(BF16)
            return 0

        lax.fori_loop(0, 3, body, 0)

    def norm_one_part():
        def body(i, carry):
            d_gain, d_shift, d_bias = carry
            r = chunk(i)
            g, n = acc[r], normed[r]
            scaled = g * g1[...]
            grad = inv1[r][:, :1] * (
                scaled - jnp.mean(scaled, axis=-1, keepdims=True) - n * jnp.mean(scaled * n, axis=-1, keepdims=True)
            )
            grad_low = grad.astype(BF16)
            gout[r] = grad_low
            acc[r] = grad
            return d_gain + fold(g * n), d_shift + fold(g), d_bias + fold(grad_low.astype(F32))

        out = lax.fori_loop(0, tokens // step, body, (zero, zero, zero))
        for at, v in zip((3, 4, 2), out):
            small[0, at : at + 1] = jnp.sum(v, axis=0, keepdims=True)

    def branch_part():
        def body(i, _):
            total[pl.ds(pl.multiple_of(PROJ + i * 256, 256), 256)] = product(attn[:, cols(i)].T, gout[...]).astype(BF16)
            cot[:, cols(i)] = product_nt(gout[...], wproj[3, pl.ds(pl.multiple_of(i * 256, 256), 256)]).astype(BF16)
            return 0

        lax.fori_loop(0, D // 256, body, 0)

    def attention_part(n):
        def body(m, _):
            i = n * 2 + m
            c = cols(i, 128)
            qp, kp, vp, gp = qs[:, c], key[:, c], val[:, c], cot[:, c]
            kt = kp.T
            dq, dk, dv = [], [], []
            for h in range(2):
                p = probs[2 * i + h]
                pf = p.astype(F32)
                weighted = pf * product_nt(vp, gp * picks[h])
                gs = (weighted - pf * jnp.sum(weighted, axis=0, keepdims=True)).astype(BF16)
                dq.append(product(kt[h * HD : (h + 1) * HD], gs))
                dk.append(product(gs, qp))
                dv.append(product(p, gp))
            gq = (jnp.concatenate(dq, axis=0).T * 0.125).astype(BF16)
            gk = jnp.where(low_lanes, dk[0], dk[1]).astype(BF16)
            gv = jnp.where(low_lanes, dv[0], dv[1]).astype(BF16)
            qs[:, c] = gq
            small[0, 0:1, c] = jnp.sum(fold(gq.astype(F32)), axis=0, keepdims=True)
            small[0, 1:2, c] = jnp.sum(fold(gv.astype(F32)), axis=0, keepdims=True)
            for b in range(2):
                active[:, cols(b * 6 + i, 128)] = gk[b * tokens : (b + 1) * tokens]
                active[:, cols(12 + b * 6 + i, 128)] = gv[b * tokens : (b + 1) * tokens]
            return 0

        lax.fori_loop(0, 2, body, 0)

    def query_part():
        def body(i, _):
            total[pl.ds(pl.multiple_of(PROJ + D + i * 256, 256), 256)] = product(
                xf[token_block(own), cols(i)].T, qs[...]
            ).astype(BF16)
            return 0

        lax.fori_loop(0, D // 256, body, 0)

    def key_part():
        def body(i, _):
            left = xf[pl.ds(0, tokens), cols(i)].T
            right = xf[pl.ds(tokens, tokens), cols(i)].T
            for n in range(2):
                base = n * 2 * D
                total[pl.ds(pl.multiple_of(PROJ + (2 + n) * D + i * 256, 256), 256)] = (
                    product(left, active[:, base : base + D]) + product(right, active[:, base + D : base + 2 * D])
                ).astype(BF16)
            return 0

        lax.fori_loop(0, D // 256, body, 0)

    dx_send = pltpu.make_async_remote_copy(hid, dx_far, xs.at[0], xs.at[1], sibling, MESH)

    def input_part():
        def both(s, w):
            return product_nt(active[:, pl.ds(pl.multiple_of(s * D, 128), D)], wproj[1, w]) + product_nt(
                active[:, pl.ds(pl.multiple_of((2 + s) * D, 128), D)], wproj[2, w]
            )

        def body(i, _):
            w = pl.ds(pl.multiple_of(i * 256, 256), 256)
            hid[:, cols(i)] = both(1 - side, w).astype(BF16)
            acc[:, cols(i)] += product_nt(qs[...], wproj[0, w]) + both(side, w)
            return 0

        lax.fori_loop(0, D // 256, body, 0)
        dx_send.start()

    bits = small_bits(plan.dp_size, seq_size)

    def small_copy(i):
        axis, bit = bits[i]
        if axis == "dp":
            tgt = (dp + bit * (1 - 2 * ((dp // bit) % 2)), sq)
        else:
            tgt = (dp, sq + bit * (1 - 2 * ((sq // bit) % 2)))
        return pltpu.make_async_remote_copy(small.at[i], small.at[len(bits) + 1 + i], ms.at[i], mr.at[i], tgt, MESH)

    def input_end():
        dx_send.wait_recv()

        def body(i, _):
            r = chunk(i)
            gout[r] = (acc[r] + dx_far[r].astype(F32)).astype(BF16)
            return 0

        lax.fori_loop(0, tokens // step, body, 0)
        send_home(gout, dx_out, 1)
        small_copy(0).start()

    def small_part(n):
        for i in range(n, n + 1 if n < SMALL_PARTS - 1 else len(bits)):
            small_copy(i).wait_recv()
            small[i + 1] = small[i] + small[len(bits) + 1 + i]
            if i + 1 < len(bits):
                small_copy(i + 1).start()

    parts = (
        [functools.partial(outer_part, n) for n in range(2)]
        + [functools.partial(inner_part, j) for j in range(4)]
        + [norm_one_part, branch_part]
        + [functools.partial(attention_part, n) for n in range(3)]
        + [query_part, key_part, input_part, input_end]
        + [functools.partial(small_part, n) for n in range(SMALL_PARTS)]
    )
    ready = {0: (0,), 1: (1,), 3: (2,), 5: (3,), 11: (4,), 12: (5,)}
    scripts = [iter(plan.script(p)) for p in plan.pieces]
    for entry in ORDER:
        if entry >= 0:
            next(scripts[entry])[1]()
            continue
        parts[-entry - 1]()
        for g in ready.get(-entry - 1, ()):
            for p in plan.pieces[3 * g : 3 * g + 3]:
                plan.rs_start(p, 0)
    small_out[...] = small[len(bits)]
    for i in range(len(bits)):
        small_copy(i).wait_send()
    dx_send.wait_send()
    sent_home(ybuf, y_out, 0)
    sent_home(gout, dx_out, 1)
    for r in range(rows):
        for c in range(2):
            pl.when(jnp.logical_not(mine[r][c]))(lambda r=r, c=c: s_copy(r, c, sq, sibling).wait_send())
        pl.when(jnp.logical_not(stays[r]))(lambda r=r: x_copy(r, spot, sibling, 0).wait_send())
        pl.when(jnp.logical_not(stays[r]))(lambda r=r: c_copy(r, spot, sibling).wait_send())
    for b in range(spread):
        forward(b, side * spread).wait_send()
    plan.finish()


def whole_layer(args, dp_size, seq_size):
    (layer_input, segment_ids, w_query, b_query, w_key, w_value, b_value, w_out, b_out, gain_one, shift_one,
     w_inner, b_inner, w_outer, b_outer, gain_two, shift_two, cotangent) = args
    plan = Exchange(dp_size, seq_size, 6)
    rows, length, width = layer_input.shape
    tokens = seq_size * length // 2
    vmem, anyw = pl.BlockSpec(memory_space=pltpu.VMEM), pl.BlockSpec(memory_space=pl.ANY)
    nbits = len(small_bits(dp_size, seq_size))
    back = pltpu.VMEM((rows, length, width), BF16)
    dma = pltpu.SemaphoreType.DMA
    vectors = (b_query, b_value, b_out, gain_one, shift_one, b_inner, b_outer, gain_two, shift_two)
    return pl.pallas_call(
        functools.partial(layer_kernel, plan, seq_size),
        out_shape=(pltpu.VMEM((3 * FF, D), BF16), pltpu.VMEM((16, D), F32), back, back),
        in_specs=[anyw] * 18,
        out_specs=(vmem,) * 4,
        scratch_shapes=[
            pltpu.VMEM((3 * FF, D), BF16),
            pltpu.VMEM((plan.slots, D), BF16),
            pltpu.VMEM((4, D, D), BF16),
            pltpu.VMEM((2 * tokens, D), BF16),
            pltpu.VMEM((tokens, D), BF16),
            pltpu.VMEM((2 * tokens, D), BF16),
            pltpu.VMEM((2 * tokens, D), BF16),
            pltpu.VMEM((D // HD, 2 * tokens, tokens), BF16),
            pltpu.VMEM((tokens, D), BF16),
            pltpu.VMEM((tokens, D), F32),
            pltpu.VMEM((tokens, 128), F32),
            pltpu.VMEM((tokens, D), BF16),
            pltpu.VMEM((D, tokens), BF16),
            pltpu.VMEM((tokens, FF), BF16),
            pltpu.VMEM((tokens, FF), F32),
            pltpu.VMEM((tokens, D), BF16),
            pltpu.VMEM((tokens, D), BF16),
            pltpu.VMEM((tokens, D), BF16),
            pltpu.VMEM((tokens, D), F32),
            pltpu.VMEM((2 * tokens, tokens), F32),
            pltpu.VMEM((seq_size, 1, length), jnp.int32),
            pltpu.VMEM((tokens, D), BF16),
            pltpu.VMEM((2 * nbits + 1, 16, D), F32),
            dma((2 * len(LANES) + 1,)), dma((plan.sems,)),
            dma((5, 2)), dma((4, seq_size)), dma((3,)), dma((18,)),
            dma((nbits,)), dma((nbits,)), dma((2, 2)), dma((2, 2)), dma((4,)),
        ]
        + [pltpu.VMEM(v.shape, F32) for v in vectors],
        compiler_params=pltpu.CompilerParams(collective_id=1, has_side_effects=True, vmem_limit_bytes=VMEM_LIMIT),
        name="layer",
    )(
        layer_input, cotangent, segment_ids.reshape(rows, 1, length), w_query, w_key, w_value, w_out, w_inner, w_outer,
        *vectors,
    )


VMEM_LIMIT = 46 << 20


def widen_kernel(sums, small, y_in, dx_in, *refs):
    outs, (wide, sem, far) = refs[:17], refs[17:]
    (y, dx, d_query, d_b_query, d_key, d_value, d_b_value, d_out, d_b_out, d_gain_one, d_shift_one, d_inner,
     d_b_inner, d_outer, d_b_outer, d_gain_two, d_shift_two) = outs
    rows = [pltpu.make_async_copy(y_in, y, far.at[0]), pltpu.make_async_copy(dx_in, dx, far.at[1])]
    for c in rows:
        c.start()
    for i, o in enumerate((d_b_query, d_b_value, d_b_out, d_gain_one, d_shift_one, d_b_outer, d_gain_two, d_shift_two)):
        o[...] = small[i]
    for j in range(4):
        d_b_inner[j * D : (j + 1) * D] = small[8 + j]
    step = 384
    copies = []
    for n in range(3 * FF // step):
        at = n * step
        if at < INNER:
            view = d_outer.at[pl.ds(at, step)]
        elif at < PROJ:
            j, row = (at - INNER) // D, (at - INNER) % D
            view = d_inner.at[pl.ds(row, step), pl.ds(j * D, D)]
        else:
            j, row = (at - PROJ) // D, (at - PROJ) % D
            view = (d_out, d_query, d_key, d_value)[j].at[pl.ds(row, step)]
        slot = n % 4
        if n >= 4:
            copies[n - 4].wait()

        def body(i, _, at=at, slot=slot):
            wide[slot, pl.ds(pl.multiple_of(i * 32, 32), 32)] = sums[pl.ds(pl.multiple_of(at + i * 32, 32), 32)].astype(F32)
            return 0

        lax.fori_loop(0, step // 32, body, 0)
        copies.append(pltpu.make_async_copy(wide.at[slot], view, sem.at[slot]))
        copies[-1].start()
    for c in copies[-4:] + rows:
        c.wait()


def widen(sums, small, y, dx):
    vmem, anyw = pl.BlockSpec(memory_space=pltpu.VMEM), pl.BlockSpec(memory_space=pl.ANY)
    back = jax.ShapeDtypeStruct(y.shape, BF16)
    square, vector = jax.ShapeDtypeStruct((D, D), F32), jax.ShapeDtypeStruct((D,), F32)
    shapes = (
        back, back, square, vector, square, square, vector, square, vector, vector, vector,
        jax.ShapeDtypeStruct((D, FF), F32), jax.ShapeDtypeStruct((FF,), F32), jax.ShapeDtypeStruct((FF, D), F32),
        vector, vector, vector,
    )
    return pl.pallas_call(
        widen_kernel,
        out_shape=shapes,
        in_specs=[vmem] * 4,
        out_specs=tuple(vmem if len(o.shape) == 1 else anyw for o in shapes),
        scratch_shapes=[
            pltpu.VMEM((4, 384, D), F32), pltpu.SemaphoreType.DMA((4,)), pltpu.SemaphoreType.DMA((2,)),
        ],
        compiler_params=pltpu.CompilerParams(vmem_limit_bytes=16 << 20),
        name="widen",
    )(sums, small, y, dx)


def on_device(dp_size, seq_size, *args):
    return widen(*whole_layer(args, dp_size, seq_size))


def solution(mesh):
    sizes = (mesh.shape["dp"], mesh.shape["seq"])
    tokens = P("dp", "seq", None)
    return jax.shard_map(
        functools.partial(on_device, *sizes),
        mesh=mesh,
        in_specs=(tokens, P("dp", "seq")) + (P(),) * 15 + (tokens,),
        out_specs=(tokens, tokens) + (P(),) * 15,
        check_vma=False,
    )
```

```python
import functools

import jax
import jax.numpy as jnp
from jax import lax
from jax.experimental import pallas as pl
from jax.experimental.pallas import tpu as pltpu
from jax.sharding import PartitionSpec as P

HD = 64
EPSILON = 1e-12
MASKED = -1000000000.0
INV_ROOT_TWO = 0.7071067811865476
DENSITY = 0.3989422804014327
MESH = pl.DeviceIdType.MESH
BF16 = jnp.bfloat16
F32 = jnp.float32


def product(left, right):
    return jnp.dot(left, right, preferred_element_type=F32)


def product_tn(left, right):
    return lax.dot_general(left, right, (((0,), (0,)), ((), ())), preferred_element_type=F32)


def product_nt(left, right):
    return lax.dot_general(left, right, (((1,), (1,)), ((), ())), preferred_element_type=F32)


def place(seq_size):
    dp, sq = lax.axis_index("dp"), lax.axis_index("seq")
    side = dp % 2
    return dp, sq, side, dp - side


GROUP = 1536
PIECE = 512
ORDERS = (("yxz", "xyz", "zyx"), ("zxy", "xyz", "yxz"), ("xyz", "yxz", "zxy"), ("zxy", "yxz", "yxz"), ("xyz", "xyz", "yzx"), ("xyz", "yxz", "yxz"))
SUBS = 1
LANES = "cxyz"


class Exchange:
    def __init__(self, dp_size, seq_size, groups):
        self.dp_size, self.seq_size, self.groups = dp_size, seq_size, groups
        self.extra = []
        bit = 8
        while bit < dp_size:
            self.extra.append(bit)
            bit *= 2
        self.sems = 0
        self.slots = 0
        self.pieces = []
        for g in range(groups):
            for cls in range(3):
                self.pieces.append(self.plan(g * GROUP + cls * PIECE, ORDERS[g % len(ORDERS)][cls]))

    def sem(self):
        self.sems += 1
        return self.sems - 1

    def slot(self, rows):
        self.slots += rows
        return self.slots - rows

    def plan(self, base, order):
        stages, rows, ends = [], PIECE, False
        for axis in "c" + order:
            half = rows // 2
            st = dict(axis=axis, rows=half, ends=ends)
            if axis == "z":
                n = half // SUBS
                st["down"] = [dict(rs=self.sem(), ag=self.sem(), slot=self.slot(n), rows=n, at=i * n) for i in range(SUBS)]
                st["up"] = [dict(rs=self.sem(), ag=self.sem(), slot=self.slot(n), rows=n, at=i * n) for i in range(SUBS)]
                ends = True
            else:
                st.update(rs=self.sem(), ag=self.sem(), slot=None if axis == "c" else self.slot(half))
            stages.append(st)
            rows = half
        more = [dict(bit=b, rs=self.sem(), slot=self.slot(rows)) for b in self.extra]
        return dict(base=base, stages=stages, more=more, rows=rows)

    def bind(self, total, slots, final, send_sem, recv_sem):
        self.total, self.landing, self.final = total, slots, final
        self.ss, self.rs = send_sem, recv_sem
        dp, sq = lax.axis_index("dp"), lax.axis_index("seq")
        self.dp, self.sq = dp, sq
        self.bits = {"c": (1, dp % 2), "x": (2, (dp // 2) % 2), "y": (4, (dp // 4) % 2)}
        self.last = self.seq_size - 1
        self.edge = jnp.logical_or(sq == 0, sq == self.last)
        self.side = sq // self.last
        self.rows_sent = {}
        for p in self.pieces:
            off = p["base"]
            for st in p["stages"]:
                half = st["rows"]
                st["off"] = off
                value = self.side if st["axis"] == "z" else self.bits[st["axis"]][1]
                st["keep"] = off + value * half
                st["give"] = off + (1 - value) * half
                off = st["keep"]
            p["own"] = off

    def view(self, off, rows):
        return self.total.at[pl.ds(pl.multiple_of(off, 16), rows)]

    def partner(self, axis):
        bit, value = self.bits[axis]
        return (self.dp + bit * (1 - 2 * value), self.sq)

    def copy(self, src, dst, lane, sem, tgt):
        return pltpu.make_async_remote_copy(src, dst, self.ss.at[lane], self.rs.at[sem], tgt, MESH)

    def send(self, copy, lane, rows, who):
        copy.start()
        for place_ in who:
            self.rows_sent[lane, place_] = self.rows_sent.get((lane, place_), 0) + rows

    def everyone(self, st):
        return (0, self.last) if st["ends"] else range(self.seq_size)

    def gated(self, when, f):
        if when is None:
            f()
        else:
            pl.when(when)(f)

    def done(self, off, rows):
        return self.final.at[pl.ds(pl.multiple_of(off, 16), rows)]

    def landed(self, st):
        if st["slot"] is None:
            return self.done(st["give"], st["rows"])
        return self.landing.at[pl.ds(st["slot"], st["rows"])]

    def add(self, off, slot, rows, into=None):
        into = self.total if into is None else into
        source = self.final if slot is None else self.landing
        slot = off if slot is None else slot
        step = 32 if rows % 32 == 0 else 16

        def body(i, _):
            at = pl.multiple_of(off + i * step, 16)
            frm = pl.multiple_of(slot + i * step, 16)
            into[pl.ds(at, step)] = self.total[pl.ds(at, step)] + source[pl.ds(frm, step)]
            return 0

        lax.fori_loop(0, rows // step, body, 0)


    def rs_start(self, p, i):
        st = p["stages"][i]
        if st["axis"] == "z":
            for way, at, to, base in (("down", self.last, -1, 0), ("up", 0, 1, st["rows"])):
                when = self.sq == at

                def f(way=way, at=at, to=to, base=base):
                    for s in st[way]:
                        self.send(self.rs_copy(st, s, base, to), LANES.index("z"), s["rows"], (at,))
                self.gated(when, f)
        else:
            when = self.edge if st["ends"] else None

            def f():
                self.send(self.rs_pair(st), LANES.index(st["axis"]), st["rows"], self.everyone(st))
            self.gated(when, f)

    def rs_pair(self, st):
        return self.copy(
            self.view(st["give"], st["rows"]), self.landed(st), LANES.index(st["axis"]), st["rs"], self.partner(st["axis"])
        )

    def rs_hyper(self, p, i):
        st = p["stages"][i]

        def f():
            self.rs_pair(st).wait_recv()
            self.add(st["keep"], st["slot"], st["rows"], self.final if i + 1 == len(p["stages"]) else None)
        self.gated(self.edge if st["ends"] else None, f)

    def rs_hop(self, p, i, hop):
        st = p["stages"][i]
        for way, at, to, base in (("down", self.last - hop, -1, 0), ("up", hop, 1, st["rows"])):
            when = self.sq == at

            def f(way=way, at=at, to=to, base=base):
                for s in st[way]:
                    self.rs_copy(st, s, base, -to).wait_recv()
                    ended = hop == self.last and i + 1 == len(p["stages"])
                    self.add(st["off"] + base + s["at"], s["slot"], s["rows"], self.final if ended else None)
                    if hop < self.last:
                        self.send(self.rs_copy(st, s, base, to), LANES.index("z"), s["rows"], (at,))
            self.gated(when, f)

    def rs_copy(self, st, s, base, to):
        return self.copy(
            self.view(st["off"] + base + s["at"], s["rows"]), self.landing.at[pl.ds(s["slot"], s["rows"])],
            LANES.index("z"), s["rs"], (self.dp, self.sq + to),
        )

    def more(self, p):
        for m in p["more"]:
            bit = m["bit"]
            value = (self.dp // bit) % 2
            tgt = (self.dp + bit * (1 - 2 * value), self.sq)

            def f():
                c = self.copy(
                    self.done(p["own"], p["rows"]), self.landing.at[pl.ds(m["slot"], p["rows"])], len(LANES) * 2, m["rs"], tgt
                )
                c.start()
                c.wait()
                part = pl.ds(pl.multiple_of(p["own"], 16), p["rows"])
                self.final[part] = self.final[part] + self.landing[pl.ds(m["slot"], p["rows"])]
            self.gated(self.edge, f)


    def ag_start(self, p, i):
        st = p["stages"][i]
        if st["axis"] == "z":
            for way, at, to, base in (("down", self.last, -1, st["rows"]), ("up", 0, 1, 0)):
                when = self.sq == at

                def f(way=way, at=at, to=to, base=base):
                    for s in st[way]:
                        self.send(self.ag_copy(st, s, base, to), len(LANES) + LANES.index("z"), s["rows"], (at,))
                self.gated(when, f)
        else:
            when = self.edge if st["ends"] else None

            def f():
                self.send(
                    self.ag_pair(st, st["keep"]), len(LANES) + LANES.index(st["axis"]), st["rows"], self.everyone(st)
                )
            self.gated(when, f)

    def ag_copy(self, st, s, base, to):
        part = self.done(st["off"] + base + s["at"], s["rows"])
        return self.copy(part, part, len(LANES) + LANES.index("z"), s["ag"], (self.dp, self.sq + to))

    def ag_pair(self, st, off):
        part = self.done(off, st["rows"])
        return self.copy(part, part, len(LANES) + LANES.index(st["axis"]), st["ag"], self.partner(st["axis"]))

    def ag_hyper(self, p, i):
        st = p["stages"][i]

        def f():
            self.ag_pair(st, st["give"]).wait_recv()
        self.gated(self.edge if st["ends"] else None, f)

    def ag_hop(self, p, i, hop):
        st = p["stages"][i]
        for way, at, to, base in (("down", self.last - hop, -1, st["rows"]), ("up", hop, 1, 0)):
            when = self.sq == at

            def f(way=way, at=at, to=to, base=base):
                for s in st[way]:
                    self.ag_copy(st, s, base, -to).wait_recv()
                    if hop < self.last:
                        self.send(self.ag_copy(st, s, base, to), len(LANES) + LANES.index("z"), s["rows"], (at,))
            self.gated(when, f)

    def script(self, p):
        steps, n = [], len(p["stages"])
        for i, st in enumerate(p["stages"]):
            after = (lambda i=i: self.rs_start(p, i + 1)) if i + 1 < n else (lambda: (self.more(p), self.ag_start(p, n - 1)))
            if st["axis"] == "z":
                for hop in range(1, self.last + 1):
                    def step(i=i, hop=hop, after=after):
                        self.rs_hop(p, i, hop)
                        if hop == self.last:
                            after()
                    steps.append((f"rz{hop}", step))
            else:
                def step(i=i, after=after):
                    self.rs_hyper(p, i)
                    after()
                steps.append(("r" + st["axis"], step))
        for i in reversed(range(n)):
            st = p["stages"][i]
            after = (lambda i=i: self.ag_start(p, i - 1)) if i > 0 else (lambda: None)
            if st["axis"] == "z":
                for hop in range(1, self.last + 1):
                    def step(i=i, hop=hop, after=after):
                        self.ag_hop(p, i, hop)
                        if hop == self.last:
                            after()
                    steps.append((f"gz{hop}", step))
            else:
                def step(i=i, after=after):
                    self.ag_hyper(p, i)
                    after()
                steps.append(("g" + st["axis"], step))
        return steps

    def finish(self):
        for lane in range(2 * len(LANES)):
            rows = [self.rows_sent[lane, p] for p in range(self.seq_size)]

            def f(n, lane=lane):
                self.copy(self.total.at[pl.ds(0, n)], self.total.at[pl.ds(0, n)], lane, 0, self.partner("c")).wait_send()

            if min(rows) == max(rows):
                f(rows[0])
            else:
                for p in range(self.seq_size):
                    pl.when(self.sq == p)(functools.partial(f, rows[p]))


def small_bits(dp_size, seq_size):
    out, bit = [], 1
    while bit < dp_size:
        out.append(("dp", bit))
        bit *= 2
    bit = 1
    while bit < seq_size:
        out.append(("seq", bit))
        bit *= 2
    return out


D = 768
FF = 3072
OUTER, INNER, PROJ = 0, 3072, 6144
ORDER = (
    -1, -2, -3, -4, 0, -5, 1, -6, 2, -7, 3, 5, 4, -8, 0, 6, 1, -9, 2, 7, 8, 5, -10, 0,
    1, 3, 9, 4, -11, 10, -12, 11, 2, -13, 0, 6, 7, 12, 1, 5, 4, 8, 3, -14, 0, 2, 10, 1,
    7, 9, -15, 5, 4, -16, 3, 0, 7, 11, 12, 8, -17, 6, 14, 0, 13, 2, 10, 1, 9, 3, -18, 15,
    6, 11, 12, 5, 4, 7, 16, 10, 8, -19, -20, 0, 1, 17, 6, 11, 14, 10, 13, 12, 3, 9, 2, 5,
    4, 7, 16, 15, 8, -21, 14, 17, 1, 5, 9, 4, 11, 13, 0, 2, 7, 12, 3, 6, 10, 16, 14, 15,
    13, 1, 5, 8, 11, 6, 4, 17, -22, 12, 10, 7, 9, 16, 0, 13, 14, 15, 6, 2, 5, 11, 3, 10,
    4, 17, 16, 1, -23, 15, 14, 8, 7, 12, 11, 9, 13, 5, 17, 6, 10, 12, 16, 2, 0, 15, 1, 11,
    14, 0, 4, 1, 17, 12, 3, 8, -24, 13, 2, 7, 5, 16, 15, 5, 9, 6, 14, 3, 10, 12, 17, 13,
    11, 16, 2, 15, 2, 7, 8, 14, 4, 7, 3, 17, 13, 4, 16, 3, 10, 9, 15, 6, 10, 8, 14, 6,
    17, 11, 12, 11, 13, 9, 12, 16, 15, 8, 17, 8, 14, 9, 13, 14, 9, 13, 16, 15, 16, 15, 17, 17,
)


SMALL_PARTS = 5


class Row:
    def __init__(self, ref):
        self.ref = ref

    def __getitem__(self, at):
        return (self.ref[...] if at is Ellipsis else self.ref[at[1]]).reshape(1, -1)


def fold(values):
    return jnp.sum(values.reshape(values.shape[0] // 8, 8, values.shape[1]), axis=0)


def layer_kernel(plan, seq_size, *refs):
    x_ref, cot_ref, seg_ref, wq_hbm, wk_hbm, wv_hbm, wo_hbm, win_hbm, wout_hbm = refs[:9]
    vectors_hbm, vectors = refs[9:18], refs[-9:]
    final, small_out, y_out, dx_out = refs[18:22]
    (total, landing, wproj, xf, qs, key, val, probs, attn, normed, inv1, hid, hid_t, active, slope, cot, ybuf, gout, acc,
     mask, sg, dx_far, small, ss, rs, gs_, gr, gl, ws, ms, mr, ys, yr, xs) = refs[22:-9]
    plan.bind(total, landing, final, ss, rs)
    bq, bv, bo, g1, s1, bi, b2, g2, s2 = (Row(v) for v in vectors)
    dp, sq, side, pair = place(seq_size)
    sibling = (dp + 1 - 2 * side, sq)
    rows, length = x_ref.shape[0], x_ref.shape[1]
    spread = seq_size // 2
    tokens = spread * length
    own, far = side * tokens, (1 - side) * tokens

    barrier = pltpu.get_barrier_semaphore()
    column = [(pair + c, p) for p in range(seq_size) for c in range(2)]
    for to in column:
        pl.when(jnp.logical_not(jnp.logical_and(to[0] == dp, to[1] == sq)))(
            lambda to=to: pl.semaphore_signal(barrier, inc=1, device_id=to, device_id_type=MESH)
        )
    across = [bit for axis, bit in small_bits(plan.dp_size, seq_size) if axis == "dp" and bit > 1]
    for bit in across:
        to = (dp + bit * (1 - 2 * ((dp // bit) % 2)), sq)
        pl.semaphore_signal(barrier, inc=1, device_id=to, device_id_type=MESH)

    loads = {}

    def load(name, src, dst, i):
        loads.setdefault(name, []).append(pltpu.make_async_copy(src, dst, ws.at[i]))
        loads[name][-1].start()

    for i, (name, src) in enumerate((("q", wq_hbm), ("k", wk_hbm), ("v", wv_hbm), ("o", wo_hbm))):
        load(name, src, wproj.at[i], i)
    for i, (src, dst) in enumerate(zip(vectors_hbm, vectors)):
        load("vectors", src, dst, 9 + i)
    for j in range(4):
        load("in", win_hbm.at[:, pl.ds(j * D, D)], total.at[pl.ds(INNER + j * D, D)], 4 + j)
    load("out", wout_hbm, total.at[pl.ds(PROJ, FF)], 8)

    def loaded(name):
        for c in loads[name]:
            c.wait()

    pl.semaphore_wait(barrier, len(column) - 1 + len(across))

    half, spot = sq // spread, sq % spread

    def block(i):
        return pl.ds(pl.multiple_of(i * length, length), length)

    def x_copy(r, b, tgt, at):
        return pltpu.make_async_remote_copy(x_ref.at[r], xf.at[block(at)], gs_.at[0, r], gr.at[0, b], tgt, MESH)

    def c_copy(r, b, tgt):
        return pltpu.make_async_remote_copy(cot_ref.at[r], cot.at[block(b)], gs_.at[1, r], gr.at[1, b], tgt, MESH)

    def s_copy(r, c, at, tgt):
        return pltpu.make_async_remote_copy(seg_ref.at[r], sg.at[at], gs_.at[2 + c, r], gr.at[2, at], tgt, MESH)

    def forward(b, base):
        part = xf.at[block(base + b)]
        return pltpu.make_async_remote_copy(part, part, gs_.at[4, b], gr.at[3, b], sibling, MESH)

    def split(local, near, remote):
        pl.when(local)(near)
        pl.when(jnp.logical_not(local))(remote)

    stays = [jnp.logical_and(half == side, sq == rows * side + r) for r in range(rows)]
    comes = [jnp.logical_and(sq // rows == side, side * spread + b == sq) for b in range(spread)]

    def x_local(r, at):
        return pltpu.make_async_copy(x_ref.at[r], xf.at[block(at)], gl.at[0])

    def c_local(r, at):
        return pltpu.make_async_copy(cot_ref.at[r], cot.at[block(at)], gl.at[1])

    def s_local(r):
        return pltpu.make_async_copy(seg_ref.at[r], sg.at[sq], gl.at[2])

    mine = [[jnp.logical_and(side == c, sq == rows * side + r) for c in range(2)] for r in range(rows)]
    for r in range(rows):
        for c in range(2):
            split(
                mine[r][c],
                lambda r=r: s_local(r).start(),
                lambda r=r, c=c: s_copy(r, c, sq, (pair + c, rows * side + r)).start(),
            )
    for r in range(rows):
        at = half * spread + spot
        split(
            stays[r],
            lambda r=r, at=at: x_local(r, at).start(),
            lambda r=r, at=at: x_copy(r, spot, (pair + half, rows * side + r), at).start(),
        )

    for b in range(spread):
        split(
            comes[b],
            lambda b=b: x_local(b, side * spread + b).wait(),
            lambda b=b: x_copy(0, b, sibling, side * spread + b).wait_recv(),
        )
        forward(b, side * spread).start()
    for r in range(rows):
        split(
            stays[r],
            lambda r=r: c_local(r, spot).start(),
            lambda r=r: c_copy(r, spot, (pair + half, rows * side + r)).start(),
        )

    def token_block(which):
        return pl.ds(pl.multiple_of(which, tokens), tokens)

    def cols(i, n=256):
        return pl.ds(pl.multiple_of(i * n, 128), n)

    for name in ("vectors", "q", "k", "v"):
        loaded(name)

    def project(which, also_query):
        def body(i, _):
            xb = xf[token_block(which)]
            c = cols(i)
            if also_query:
                qs[:, c] = (product(xb, wproj[0, :, c]) + bq[:, c]).astype(BF16) * BF16(0.125)
            key[token_block(which), c] = product(xb, wproj[1, :, c]).astype(BF16)
            val[token_block(which), c] = (product(xb, wproj[2, :, c]) + bv[:, c]).astype(BF16)
            return 0

        lax.fori_loop(0, D // 256, body, 0, unroll=3)

    project(own, True)

    for p in range(seq_size):
        split(
            jnp.logical_and(sq // rows == side, p == sq),
            lambda: s_local(0).wait(),
            lambda p=p: s_copy(0, 0, p, sibling).wait_recv(),
        )
    diagonal = lax.broadcasted_iota(jnp.int32, (length, length), 0) == lax.broadcasted_iota(
        jnp.int32, (length, length), 1
    )
    for b in range(spread):
        mine_seg = jnp.broadcast_to(sg[side * spread + b], (length, length))
        column = jnp.sum(jnp.where(diagonal, mine_seg, 0), axis=1, keepdims=True)
        for p in range(seq_size):
            seen = jnp.broadcast_to(column, (length, length)) == jnp.broadcast_to(sg[p], (length, length))
            mask[b * length : (b + 1) * length, p * length : (p + 1) * length] = jnp.where(seen, 0.0, MASKED)

    for b in range(spread):
        forward(b, (1 - side) * spread).wait_recv()
    project(far, False)

    lane = lax.broadcasted_iota(jnp.int32, (1, 128), 1)
    first = (lane < HD).astype(BF16)
    picks = (first, BF16(1.0) - first)
    low_lanes = lane < HD

    def attend(i, _):
        c = cols(i, 128)
        qp, kp, vp = qs[:, c], key[:, c], val[:, c]
        outs = []
        for n in range(2):
            s = product_nt(qp * picks[n], kp) + mask[...]
            e = jnp.exp(s - jnp.max(s, axis=-1, keepdims=True))
            p = (e * (1.0 / jnp.sum(e, axis=-1, keepdims=True))).astype(BF16)
            probs[2 * i + n] = p
            outs.append(product(p, vp))
        attn[:, c] = jnp.where(low_lanes, outs[0], outs[1]).astype(BF16)
        return 0

    lax.fori_loop(0, D // 128, attend, 0, unroll=3)

    loaded("o")

    def branch(i, _):
        c = cols(i)
        acc[:, c] = product(attn[...], wproj[3, :, c]) + bo[:, c] + xf[token_block(own), c].astype(F32)
        return 0

    lax.fori_loop(0, D // 256, branch, 0, unroll=3)
    step = 32

    def chunk(i):
        return pl.ds(pl.multiple_of(i * step, step), step)

    def norm_one(i, _):
        r = chunk(i)
        v = acc[r]
        centre = v - jnp.mean(v, axis=-1, keepdims=True)
        inv = lax.rsqrt(jnp.mean(centre * centre, axis=-1, keepdims=True) + EPSILON)
        n = centre * inv
        normed[r] = n
        inv1[r] = jnp.broadcast_to(inv, (step, 128))
        hid[r] = (n * g1[...] + s1[...]).astype(BF16)
        return 0

    lax.fori_loop(0, tokens // step, norm_one, 0, unroll=2)

    loaded("in")
    loaded("out")

    def inner_cols(j, i):
        return total.at[pl.ds(INNER + j * D, D), cols(i)]

    for j in range(4):

        def expand(i, _, j=j):
            c = cols(j * 3 + i)
            v = product(hid[...], inner_cols(j, i)[...]) + bi[:, c]
            cdf = 0.5 * (1.0 + lax.erf(v * INV_ROOT_TWO))
            active[:, c] = (v * cdf).astype(BF16)
            slope[:, c] = cdf + v * DENSITY * jnp.exp(-0.5 * v * v)
            return 0

        lax.fori_loop(0, 3, expand, 0, unroll=3)

    def contract(i, _):
        c = cols(i)
        acc[:, c] = product(active[...], total[pl.ds(PROJ, FF), c]) + b2[:, c]
        return 0

    lax.fori_loop(0, D // 256, contract, 0, unroll=3)
    for b in range(spread):
        split(comes[b], lambda b=b: c_local(b, b).wait(), lambda b=b: c_copy(0, b, sibling).wait_recv())

    small[0] = jnp.zeros((16, D), F32)

    def norm_two(i, carry):
        d_gain, d_shift, d_bias = carry
        r = chunk(i)
        v = normed[r] * g1[...] + s1[...] + acc[r]
        centre = v - jnp.mean(v, axis=-1, keepdims=True)
        inv = lax.rsqrt(jnp.mean(centre * centre, axis=-1, keepdims=True) + EPSILON)
        n = centre * inv
        ybuf[r] = (n * g2[...] + s2[...]).astype(BF16)
        g = cot[r].astype(F32)
        scaled = g * g2[...]
        grad = inv * (
            scaled - jnp.mean(scaled, axis=-1, keepdims=True) - n * jnp.mean(scaled * n, axis=-1, keepdims=True)
        )
        grad_low = grad.astype(BF16)
        gout[r] = grad_low
        acc[r] = grad
        return d_gain + fold(g * n), d_shift + fold(g), d_bias + fold(grad_low.astype(F32))

    zero = jnp.zeros((8, D), F32)
    sums = lax.fori_loop(0, tokens // step, norm_two, (zero, zero, zero), unroll=2)
    for at, v in zip((6, 7, 5), sums):
        small[0, at : at + 1] = jnp.sum(v, axis=0, keepdims=True)

    homes = [(pair + sq // rows, side * spread + b) for b in range(spread)]
    at_home = [jnp.logical_and(h[0] == dp, h[1] == sq) for h in homes]

    def back(src, dst, b, lane_, to, slot):
        return pltpu.make_async_remote_copy(
            src.at[pl.ds(b * length, length)], dst.at[slot], ys.at[lane_, b], yr.at[lane_, slot], to, MESH
        )

    def home_local(src, dst, b, lane_):
        return pltpu.make_async_copy(src.at[pl.ds(b * length, length)], dst.at[sq % rows], xs.at[2 + lane_])

    def send_home(src, dst, lane_):
        for b in range(spread):
            split(
                at_home[b],
                lambda b=b: home_local(src, dst, b, lane_).start(),
                lambda b=b: back(src, dst, b, lane_, homes[b], sq % rows).start(),
            )

    def sent_home(src, dst, lane_):
        for b in range(spread):
            split(
                at_home[b],
                lambda b=b: home_local(src, dst, b, lane_).wait(),
                lambda b=b: back(src, dst, b, lane_, homes[b], sq % rows).wait_send(),
            )
        for r in range(rows):
            pl.when(jnp.logical_not(jnp.logical_and(half == side, sq == rows * side + r)))(
                lambda r=r: back(src, dst, 0, lane_, sibling, r).wait_recv()
            )

    send_home(ybuf, y_out, 0)


    bits = small_bits(plan.dp_size, seq_size)

    def small_copy(i):
        axis, bit = bits[i]
        if axis == "dp":
            tgt = (dp + bit * (1 - 2 * ((dp // bit) % 2)), sq)
        else:
            tgt = (dp, sq + bit * (1 - 2 * ((sq // bit) % 2)))
        return pltpu.make_async_remote_copy(small.at[i], small.at[len(bits) + 1 + i], ms.at[i], mr.at[i], tgt, MESH)

    def outer_part(n):
        def body(i, _):
            t = n * 2 + i
            total[pl.ds(pl.multiple_of(OUTER + t * 256, 256), 256)] = product(
                active[:, cols(t)].T, gout[...]
            ).astype(BF16)
            return 0

        lax.fori_loop(0, 2, body, 0, unroll=2)

    def inner_part(j):
        if j == 0:
            for i in range(3):
                hid_t[i * 256 : (i + 1) * 256] = hid[:, i * 256 : (i + 1) * 256].T

        def body(i, _):
            t = j * 3 + i
            up = product_nt(gout[...], total[pl.ds(pl.multiple_of(PROJ + t * 256, 256), 256)])
            gi = (up * slope[:, cols(t)]).astype(BF16)
            small[0, 8 + j : 9 + j, cols(i)] = jnp.sum(fold(gi.astype(F32)), axis=0, keepdims=True)
            view = inner_cols(j, i)
            acc[...] += product_nt(gi, view[...])
            view[...] = product(hid_t[...], gi).astype(BF16)
            return 0

        lax.fori_loop(0, 3, body, 0, unroll=3)

    def norm_one_part():
        def body(i, carry):
            d_gain, d_shift, d_bias = carry
            r = chunk(i)
            g, n = acc[r], normed[r]
            scaled = g * g1[...]
            grad = inv1[r][:, :1] * (
                scaled - jnp.mean(scaled, axis=-1, keepdims=True) - n * jnp.mean(scaled * n, axis=-1, keepdims=True)
            )
            grad_low = grad.astype(BF16)
            gout[r] = grad_low
            acc[r] = grad
            return d_gain + fold(g * n), d_shift + fold(g), d_bias + fold(grad_low.astype(F32))

        out = lax.fori_loop(0, tokens // step, body, (zero, zero, zero), unroll=2)
        for at, v in zip((3, 4, 2), out):
            small[0, at : at + 1] = jnp.sum(v, axis=0, keepdims=True)

    def branch_part():
        def body(i, _):
            total[pl.ds(pl.multiple_of(PROJ + i * 256, 256), 256)] = product(attn[:, cols(i)].T, gout[...]).astype(BF16)
            cot[:, cols(i)] = product_nt(gout[...], wproj[3, pl.ds(pl.multiple_of(i * 256, 256), 256)]).astype(BF16)
            return 0

        lax.fori_loop(0, D // 256, body, 0, unroll=3)

    def attention_part(n):
        def body(m, _):
            i = n * 2 + m
            c = cols(i, 128)
            qp, kp, vp, gp = qs[:, c], key[:, c], val[:, c], cot[:, c]
            dq, dk, dv = [], [], []
            for h in range(2):
                p = probs[2 * i + h]
                pf = p.astype(F32)
                weighted = pf * product_nt(gp * picks[h], vp)
                delta = jnp.sum(weighted, axis=-1, keepdims=True)
                gs = (weighted - pf * delta).astype(BF16)
                dq.append(product(gs, kp))
                dk.append(product_tn(gs, qp))
                dv.append(product_tn(p, gp))
            gq = (jnp.where(low_lanes, dq[0], dq[1]) * 0.125).astype(BF16)
            gk = jnp.where(low_lanes, dk[0], dk[1]).astype(BF16)
            gv = jnp.where(low_lanes, dv[0], dv[1]).astype(BF16)
            qs[:, c] = gq
            small[0, 0:1, c] = jnp.sum(fold(gq.astype(F32)), axis=0, keepdims=True)
            small[0, 1:2, c] = jnp.sum(fold(gv.astype(F32)), axis=0, keepdims=True)
            for b in range(2):
                active[:, cols(b * 6 + i, 128)] = gk[b * tokens : (b + 1) * tokens]
                active[:, cols(12 + b * 6 + i, 128)] = gv[b * tokens : (b + 1) * tokens]
            return 0

        lax.fori_loop(0, 2, body, 0, unroll=2)
        if n == 2:
            small_copy(0).start()

    def query_part():
        def body(i, _):
            total[pl.ds(pl.multiple_of(PROJ + D + i * 256, 256), 256)] = product(
                xf[token_block(own), cols(i)].T, qs[...]
            ).astype(BF16)
            return 0

        lax.fori_loop(0, D // 256, body, 0, unroll=3)

    def key_part():
        def body(i, _):
            left = xf[pl.ds(0, tokens), cols(i)].T
            right = xf[pl.ds(tokens, tokens), cols(i)].T
            for n in range(2):
                base = n * 2 * D
                total[pl.ds(pl.multiple_of(PROJ + (2 + n) * D + i * 256, 256), 256)] = (
                    product(left, active[:, base : base + D]) + product(right, active[:, base + D : base + 2 * D])
                ).astype(BF16)
            return 0

        lax.fori_loop(0, D // 256, body, 0, unroll=3)

    dx_send = pltpu.make_async_remote_copy(hid, dx_far, xs.at[0], xs.at[1], sibling, MESH)

    def input_part():
        def both(s, w):
            return product_nt(active[:, pl.ds(pl.multiple_of(s * D, 128), D)], wproj[1, w]) + product_nt(
                active[:, pl.ds(pl.multiple_of((2 + s) * D, 128), D)], wproj[2, w]
            )

        def body(i, _):
            w = pl.ds(pl.multiple_of(i * 256, 256), 256)
            hid[:, cols(i)] = both(1 - side, w).astype(BF16)
            acc[:, cols(i)] += product_nt(qs[...], wproj[0, w]) + both(side, w)
            return 0

        lax.fori_loop(0, D // 256, body, 0, unroll=3)
        dx_send.start()

    def input_end():
        dx_send.wait_recv()

        def body(i, _):
            r = chunk(i)
            gout[r] = (acc[r] + dx_far[r].astype(F32)).astype(BF16)
            return 0

        lax.fori_loop(0, tokens // step, body, 0)
        send_home(gout, dx_out, 1)

    def small_part(n):
        for i in range(n, n + 1 if n < SMALL_PARTS - 1 else len(bits)):
            small_copy(i).wait_recv()
            small[i + 1] = small[i] + small[len(bits) + 1 + i]
            if i + 1 < len(bits):
                small_copy(i + 1).start()

    parts = (
        [functools.partial(outer_part, n) for n in range(6)]
        + [functools.partial(inner_part, j) for j in range(4)]
        + [norm_one_part, branch_part]
        + [functools.partial(attention_part, n) for n in range(3)]
        + [query_part, key_part, input_part, input_end]
        + [functools.partial(small_part, n) for n in range(SMALL_PARTS)]
    )
    ready = {n: (n,) for n in range(6)}
    ready.update({6: (6,), 7: (7, 8), 8: (9,), 9: (10, 11), 11: (12,), 15: (13, 14), 16: (15, 16, 17)})
    scripts = [iter(plan.script(p)) for p in plan.pieces]
    for entry in ORDER:
        if entry >= 0:
            next(scripts[entry])[1]()
            continue
        parts[-entry - 1]()
        for n in ready.get(-entry - 1, ()):
            plan.rs_start(plan.pieces[n], 0)
    small_out[...] = small[len(bits)]
    for i in range(len(bits)):
        small_copy(i).wait_send()
    dx_send.wait_send()
    sent_home(ybuf, y_out, 0)
    sent_home(gout, dx_out, 1)
    for r in range(rows):
        for c in range(2):
            pl.when(jnp.logical_not(mine[r][c]))(lambda r=r, c=c: s_copy(r, c, sq, sibling).wait_send())
        pl.when(jnp.logical_not(stays[r]))(lambda r=r: x_copy(r, spot, sibling, 0).wait_send())
        pl.when(jnp.logical_not(stays[r]))(lambda r=r: c_copy(r, spot, sibling).wait_send())
    for b in range(spread):
        forward(b, side * spread).wait_send()
    plan.finish()


def whole_layer(args, dp_size, seq_size):
    (layer_input, segment_ids, w_query, b_query, w_key, w_value, b_value, w_out, b_out, gain_one, shift_one,
     w_inner, b_inner, w_outer, b_outer, gain_two, shift_two, cotangent) = args
    plan = Exchange(dp_size, seq_size, 6)
    rows, length, width = layer_input.shape
    tokens = seq_size * length // 2
    vmem, anyw = pl.BlockSpec(memory_space=pltpu.VMEM), pl.BlockSpec(memory_space=pl.ANY)
    nbits = len(small_bits(dp_size, seq_size))
    back = pltpu.VMEM((rows, length, width), BF16)
    dma = pltpu.SemaphoreType.DMA
    vectors = (b_query, b_value, b_out, gain_one, shift_one, b_inner, b_outer, gain_two, shift_two)
    return pl.pallas_call(
        functools.partial(layer_kernel, plan, seq_size),
        out_shape=(pltpu.VMEM((3 * FF, D), BF16), pltpu.VMEM((16, D), F32), back, back),
        in_specs=[anyw] * 18,
        out_specs=(vmem,) * 4,
        scratch_shapes=[
            pltpu.VMEM((3 * FF, D), BF16),
            pltpu.VMEM((plan.slots, D), BF16),
            pltpu.VMEM((4, D, D), BF16),
            pltpu.VMEM((2 * tokens, D), BF16),
            pltpu.VMEM((tokens, D), BF16),
            pltpu.VMEM((2 * tokens, D), BF16),
            pltpu.VMEM((2 * tokens, D), BF16),
            pltpu.VMEM((D // HD, tokens, 2 * tokens), BF16),
            pltpu.VMEM((tokens, D), BF16),
            pltpu.VMEM((tokens, D), F32),
            pltpu.VMEM((tokens, 128), F32),
            pltpu.VMEM((tokens, D), BF16),
            pltpu.VMEM((D, tokens), BF16),
            pltpu.VMEM((tokens, FF), BF16),
            pltpu.VMEM((tokens, FF), F32),
            pltpu.VMEM((tokens, D), BF16),
            pltpu.VMEM((tokens, D), BF16),
            pltpu.VMEM((tokens, D), BF16),
            pltpu.VMEM((tokens, D), F32),
            pltpu.VMEM((tokens, 2 * tokens), F32),
            pltpu.VMEM((seq_size, 1, length), jnp.int32),
            pltpu.VMEM((tokens, D), BF16),
            pltpu.VMEM((2 * nbits + 1, 16, D), F32),
            dma((2 * len(LANES) + 1,)), dma((plan.sems,)),
            dma((5, 2)), dma((4, seq_size)), dma((3,)), dma((18,)),
            dma((nbits,)), dma((nbits,)), dma((2, 2)), dma((2, 2)), dma((4,)),
        ]
        + [pltpu.VMEM(v.shape, F32) for v in vectors],
        compiler_params=pltpu.CompilerParams(collective_id=1, has_side_effects=True, vmem_limit_bytes=VMEM_LIMIT),
        name="layer",
    )(
        layer_input, cotangent, segment_ids.reshape(rows, 1, length), w_query, w_key, w_value, w_out, w_inner, w_outer,
        *vectors,
    )


VMEM_LIMIT = 46 << 20


def widen_kernel(sums, small, y_in, dx_in, *refs):
    outs, (wide, sem, far) = refs[:17], refs[17:]
    (y, dx, d_query, d_b_query, d_key, d_value, d_b_value, d_out, d_b_out, d_gain_one, d_shift_one, d_inner,
     d_b_inner, d_outer, d_b_outer, d_gain_two, d_shift_two) = outs
    rows = [pltpu.make_async_copy(y_in, y, far.at[0]), pltpu.make_async_copy(dx_in, dx, far.at[1])]
    for c in rows:
        c.start()
    for i, o in enumerate((d_b_query, d_b_value, d_b_out, d_gain_one, d_shift_one, d_b_outer, d_gain_two, d_shift_two)):
        o[...] = small[i]
    for j in range(4):
        d_b_inner[j * D : (j + 1) * D] = small[8 + j]
    step = 384
    copies = []
    for n in range(3 * FF // step):
        at = n * step
        if at < INNER:
            view = d_outer.at[pl.ds(at, step)]
        elif at < PROJ:
            j, row = (at - INNER) // D, (at - INNER) % D
            view = d_inner.at[pl.ds(row, step), pl.ds(j * D, D)]
        else:
            j, row = (at - PROJ) // D, (at - PROJ) % D
            view = (d_out, d_query, d_key, d_value)[j].at[pl.ds(row, step)]
        slot = n % 4
        if n >= 4:
            copies[n - 4].wait()

        def body(i, _, at=at, slot=slot):
            wide[slot, pl.ds(pl.multiple_of(i * 32, 32), 32)] = sums[pl.ds(pl.multiple_of(at + i * 32, 32), 32)].astype(F32)
            return 0

        lax.fori_loop(0, step // 32, body, 0)
        copies.append(pltpu.make_async_copy(wide.at[slot], view, sem.at[slot]))
        copies[-1].start()
    for c in copies[-4:] + rows:
        c.wait()


def widen(sums, small, y, dx):
    vmem, anyw = pl.BlockSpec(memory_space=pltpu.VMEM), pl.BlockSpec(memory_space=pl.ANY)
    back = jax.ShapeDtypeStruct(y.shape, BF16)
    square, vector = jax.ShapeDtypeStruct((D, D), F32), jax.ShapeDtypeStruct((D,), F32)
    shapes = (
        back, back, square, vector, square, square, vector, square, vector, vector, vector,
        jax.ShapeDtypeStruct((D, FF), F32), jax.ShapeDtypeStruct((FF,), F32), jax.ShapeDtypeStruct((FF, D), F32),
        vector, vector, vector,
    )
    return pl.pallas_call(
        widen_kernel,
        out_shape=shapes,
        in_specs=[vmem] * 4,
        out_specs=tuple(vmem if len(o.shape) == 1 else anyw for o in shapes),
        scratch_shapes=[
            pltpu.VMEM((4, 384, D), F32), pltpu.SemaphoreType.DMA((4,)), pltpu.SemaphoreType.DMA((2,)),
        ],
        compiler_params=pltpu.CompilerParams(vmem_limit_bytes=16 << 20),
        name="widen",
    )(sums, small, y, dx)


def on_device(dp_size, seq_size, *args):
    return widen(*whole_layer(args, dp_size, seq_size))


def solution(mesh):
    sizes = (mesh.shape["dp"], mesh.shape["seq"])
    tokens = P("dp", "seq", None)
    return jax.shard_map(
        functools.partial(on_device, *sizes),
        mesh=mesh,
        in_specs=(tokens, P("dp", "seq")) + (P(),) * 15 + (tokens,),
        out_specs=(tokens, tokens) + (P(),) * 15,
        check_vma=False,
    )
```

```python
import functools

import jax
import jax.numpy as jnp
from jax import lax
from jax.experimental import pallas as pl
from jax.experimental.pallas import tpu as pltpu
from jax.sharding import PartitionSpec as P

HD = 64
EPSILON = 1e-12
MASKED = -1000000000.0
INV_ROOT_TWO = 0.7071067811865476
DENSITY = 0.3989422804014327
MESH = pl.DeviceIdType.MESH
BF16 = jnp.bfloat16
F32 = jnp.float32


def product(left, right):
    return jnp.dot(left, right, preferred_element_type=F32)


def product_tn(left, right):
    return lax.dot_general(left, right, (((0,), (0,)), ((), ())), preferred_element_type=F32)


def product_nt(left, right):
    return lax.dot_general(left, right, (((1,), (1,)), ((), ())), preferred_element_type=F32)


def place(seq_size):
    dp, sq = lax.axis_index("dp"), lax.axis_index("seq")
    side = dp % 2
    return dp, sq, side, dp - side


GROUP = 1536
PIECE = 512
ORDERS = (("yxz", "yxz", "zxy"), ("zyx", "xyz", "xyz"), ("yxz", "xzy", "yxz"), ("zxy", "xyz", "xyz"), ("yzx", "xyz", "yxz"), ("yzx", "xyz", "yxz"))
SUBS = 1
LANES = "cxyz"


class Exchange:
    def __init__(self, dp_size, seq_size, groups):
        self.dp_size, self.seq_size, self.groups = dp_size, seq_size, groups
        self.extra = []
        bit = 8
        while bit < dp_size:
            self.extra.append(bit)
            bit *= 2
        self.sems = 0
        self.slots = 0
        self.pieces = []
        for g in range(groups):
            for cls in range(3):
                self.pieces.append(self.plan(g * GROUP + cls * PIECE, ORDERS[g % len(ORDERS)][cls]))

    def sem(self):
        self.sems += 1
        return self.sems - 1

    def slot(self, rows):
        self.slots += rows
        return self.slots - rows

    def plan(self, base, order):
        stages, rows, ends = [], PIECE, False
        for axis in "c" + order:
            half = rows // 2
            st = dict(axis=axis, rows=half, ends=ends)
            if axis == "z":
                n = half // SUBS
                st["down"] = [dict(rs=self.sem(), ag=self.sem(), slot=self.slot(n), rows=n, at=i * n) for i in range(SUBS)]
                st["up"] = [dict(rs=self.sem(), ag=self.sem(), slot=self.slot(n), rows=n, at=i * n) for i in range(SUBS)]
                ends = True
            else:
                st.update(rs=self.sem(), ag=self.sem(), slot=None if axis == "c" else self.slot(half))
            stages.append(st)
            rows = half
        more = [dict(bit=b, rs=self.sem(), slot=self.slot(rows)) for b in self.extra]
        return dict(base=base, stages=stages, more=more, rows=rows)

    def bind(self, total, slots, final, send_sem, recv_sem):
        self.total, self.landing, self.final = total, slots, final
        self.ss, self.rs = send_sem, recv_sem
        dp, sq = lax.axis_index("dp"), lax.axis_index("seq")
        self.dp, self.sq = dp, sq
        self.bits = {"c": (1, dp % 2), "x": (2, (dp // 2) % 2), "y": (4, (dp // 4) % 2)}
        self.last = self.seq_size - 1
        self.edge = jnp.logical_or(sq == 0, sq == self.last)
        self.side = sq // self.last
        self.rows_sent = {}
        for p in self.pieces:
            off = p["base"]
            for st in p["stages"]:
                half = st["rows"]
                st["off"] = off
                value = self.side if st["axis"] == "z" else self.bits[st["axis"]][1]
                st["keep"] = off + value * half
                st["give"] = off + (1 - value) * half
                off = st["keep"]
            p["own"] = off

    def view(self, off, rows):
        return self.total.at[pl.ds(pl.multiple_of(off, 16), rows)]

    def partner(self, axis):
        bit, value = self.bits[axis]
        return (self.dp + bit * (1 - 2 * value), self.sq)

    def copy(self, src, dst, lane, sem, tgt):
        return pltpu.make_async_remote_copy(src, dst, self.ss.at[lane], self.rs.at[sem], tgt, MESH)

    def send(self, copy, lane, rows, who):
        copy.start()
        for place_ in who:
            self.rows_sent[lane, place_] = self.rows_sent.get((lane, place_), 0) + rows

    def everyone(self, st):
        return (0, self.last) if st["ends"] else range(self.seq_size)

    def gated(self, when, f):
        if when is None:
            f()
        else:
            pl.when(when)(f)

    def done(self, off, rows):
        return self.final.at[pl.ds(pl.multiple_of(off, 16), rows)]

    def landed(self, st):
        if st["slot"] is None:
            return self.done(st["give"], st["rows"])
        return self.landing.at[pl.ds(st["slot"], st["rows"])]

    def add(self, off, slot, rows, into=None):
        into = self.total if into is None else into
        source = self.final if slot is None else self.landing
        slot = off if slot is None else slot
        step = 32 if rows % 32 == 0 else 16

        def body(i, _):
            at = pl.multiple_of(off + i * step, 16)
            frm = pl.multiple_of(slot + i * step, 16)
            into[pl.ds(at, step)] = self.total[pl.ds(at, step)] + source[pl.ds(frm, step)]
            return 0

        lax.fori_loop(0, rows // step, body, 0)


    def rs_start(self, p, i):
        st = p["stages"][i]
        if st["axis"] == "z":
            for way, at, to, base in (("down", self.last, -1, 0), ("up", 0, 1, st["rows"])):
                when = self.sq == at

                def f(way=way, at=at, to=to, base=base):
                    for s in st[way]:
                        self.send(self.rs_copy(st, s, base, to), LANES.index("z"), s["rows"], (at,))
                self.gated(when, f)
        else:
            when = self.edge if st["ends"] else None

            def f():
                self.send(self.rs_pair(st), LANES.index(st["axis"]), st["rows"], self.everyone(st))
            self.gated(when, f)

    def rs_pair(self, st):
        return self.copy(
            self.view(st["give"], st["rows"]), self.landed(st), LANES.index(st["axis"]), st["rs"], self.partner(st["axis"])
        )

    def rs_hyper(self, p, i):
        st = p["stages"][i]

        def f():
            self.rs_pair(st).wait_recv()
            self.add(st["keep"], st["slot"], st["rows"], self.final if i + 1 == len(p["stages"]) else None)
        self.gated(self.edge if st["ends"] else None, f)

    def rs_hop(self, p, i, hop):
        st = p["stages"][i]
        for way, at, to, base in (("down", self.last - hop, -1, 0), ("up", hop, 1, st["rows"])):
            when = self.sq == at

            def f(way=way, at=at, to=to, base=base):
                for s in st[way]:
                    self.rs_copy(st, s, base, -to).wait_recv()
                    ended = hop == self.last and i + 1 == len(p["stages"])
                    self.add(st["off"] + base + s["at"], s["slot"], s["rows"], self.final if ended else None)
                    if hop < self.last:
                        self.send(self.rs_copy(st, s, base, to), LANES.index("z"), s["rows"], (at,))
            self.gated(when, f)

    def rs_copy(self, st, s, base, to):
        return self.copy(
            self.view(st["off"] + base + s["at"], s["rows"]), self.landing.at[pl.ds(s["slot"], s["rows"])],
            LANES.index("z"), s["rs"], (self.dp, self.sq + to),
        )

    def more(self, p):
        for m in p["more"]:
            bit = m["bit"]
            value = (self.dp // bit) % 2
            tgt = (self.dp + bit * (1 - 2 * value), self.sq)

            def f():
                c = self.copy(
                    self.done(p["own"], p["rows"]), self.landing.at[pl.ds(m["slot"], p["rows"])], len(LANES) * 2, m["rs"], tgt
                )
                c.start()
                c.wait()
                part = pl.ds(pl.multiple_of(p["own"], 16), p["rows"])
                self.final[part] = self.final[part] + self.landing[pl.ds(m["slot"], p["rows"])]
            self.gated(self.edge, f)


    def ag_start(self, p, i):
        st = p["stages"][i]
        if st["axis"] == "z":
            for way, at, to, base in (("down", self.last, -1, st["rows"]), ("up", 0, 1, 0)):
                when = self.sq == at

                def f(way=way, at=at, to=to, base=base):
                    for s in st[way]:
                        self.send(self.ag_copy(st, s, base, to), len(LANES) + LANES.index("z"), s["rows"], (at,))
                self.gated(when, f)
        else:
            when = self.edge if st["ends"] else None

            def f():
                self.send(
                    self.ag_pair(st, st["keep"]), len(LANES) + LANES.index(st["axis"]), st["rows"], self.everyone(st)
                )
            self.gated(when, f)

    def ag_copy(self, st, s, base, to):
        part = self.done(st["off"] + base + s["at"], s["rows"])
        return self.copy(part, part, len(LANES) + LANES.index("z"), s["ag"], (self.dp, self.sq + to))

    def ag_pair(self, st, off):
        part = self.done(off, st["rows"])
        return self.copy(part, part, len(LANES) + LANES.index(st["axis"]), st["ag"], self.partner(st["axis"]))

    def ag_hyper(self, p, i):
        st = p["stages"][i]

        def f():
            self.ag_pair(st, st["give"]).wait_recv()
        self.gated(self.edge if st["ends"] else None, f)

    def ag_hop(self, p, i, hop):
        st = p["stages"][i]
        for way, at, to, base in (("down", self.last - hop, -1, st["rows"]), ("up", hop, 1, 0)):
            when = self.sq == at

            def f(way=way, at=at, to=to, base=base):
                for s in st[way]:
                    self.ag_copy(st, s, base, -to).wait_recv()
                    if hop < self.last:
                        self.send(self.ag_copy(st, s, base, to), len(LANES) + LANES.index("z"), s["rows"], (at,))
            self.gated(when, f)

    def script(self, p):
        steps, n = [], len(p["stages"])
        for i, st in enumerate(p["stages"]):
            after = (lambda i=i: self.rs_start(p, i + 1)) if i + 1 < n else (lambda: (self.more(p), self.ag_start(p, n - 1)))
            if st["axis"] == "z":
                for hop in range(1, self.last + 1):
                    def step(i=i, hop=hop, after=after):
                        self.rs_hop(p, i, hop)
                        if hop == self.last:
                            after()
                    steps.append((f"rz{hop}", step))
            else:
                def step(i=i, after=after):
                    self.rs_hyper(p, i)
                    after()
                steps.append(("r" + st["axis"], step))
        for i in reversed(range(n)):
            st = p["stages"][i]
            after = (lambda i=i: self.ag_start(p, i - 1)) if i > 0 else (lambda: None)
            if st["axis"] == "z":
                for hop in range(1, self.last + 1):
                    def step(i=i, hop=hop, after=after):
                        self.ag_hop(p, i, hop)
                        if hop == self.last:
                            after()
                    steps.append((f"gz{hop}", step))
            else:
                def step(i=i, after=after):
                    self.ag_hyper(p, i)
                    after()
                steps.append(("g" + st["axis"], step))
        return steps

    def finish(self):
        for lane in range(2 * len(LANES)):
            rows = [self.rows_sent[lane, p] for p in range(self.seq_size)]

            def f(n, lane=lane):
                self.copy(self.total.at[pl.ds(0, n)], self.total.at[pl.ds(0, n)], lane, 0, self.partner("c")).wait_send()

            if min(rows) == max(rows):
                f(rows[0])
            else:
                for p in range(self.seq_size):
                    pl.when(self.sq == p)(functools.partial(f, rows[p]))


def small_bits(dp_size, seq_size):
    out, bit = [], 1
    while bit < dp_size:
        out.append(("dp", bit))
        bit *= 2
    bit = 1
    while bit < seq_size:
        out.append(("seq", bit))
        bit *= 2
    return out


D = 768
FF = 3072
OUTER, INNER, PROJ = 0, 3072, 6144
ORDER = (
    -1, -2, -3, -4, 0, -5, -6, 1, -7, 3, 2, 4, -8, 6, 5, 0, -9, 7, 8, -10, 1, 3, 4, 9,
    -11, -12, 10, 11, -13, 6, 5, 2, 0, 12, -14, 3, 9, 8, -15, 4, 7, 0, -16, 1, 5, 2, -17, 13,
    4, 3, 14, -18, 7, 9, 15, 12, 16, 0, 1, 10, 17, 4, 5, -19, -20, 3, 2, 11, 7, 12, 1, 6,
    5, 9, 14, 0, 8, 4, 15, 13, 6, 10, 0, 8, 4, 16, 12, 7, -21, 17, 15, 6, 1, 3, 10, 0,
    5, 11, 8, 2, 4, 12, 13, 1, 6, 9, 5, 15, 0, 16, 11, 10, 8, 7, 13, 14, 1, 4, -22, 6,
    5, 2, 17, 16, 11, 15, 3, 8, 9, 13, 10, 7, 14, 12, 6, 1, 16, -23, 17, 4, 0, 8, 5, 15,
    10, 2, 14, 11, 12, 13, 3, 7, 6, 9, -24, 1, 17, 16, 10, 11, 8, 14, 12, 7, 17, 4, 0, 13,
    11, 10, 15, 4, 5, 0, 2, 12, 7, 3, 13, 11, 6, 16, 1, 14, 9, 17, 12, 1, 10, 13, 8, 15,
    11, 3, 16, 14, 5, 2, 17, 6, 5, 15, 6, 3, 7, 9, 16, 3, 12, 14, 7, 17, 2, 12, 13, 10,
    15, 10, 9, 8, 11, 2, 8, 16, 11, 14, 2, 17, 9, 15, 9, 15, 13, 14, 13, 14, 16, 17, 16, 17,
)


SMALL_PARTS = 5


class Row:
    def __init__(self, ref):
        self.ref = ref

    def __getitem__(self, at):
        return (self.ref[...] if at is Ellipsis else self.ref[at[1]]).reshape(1, -1)


def fold(values):
    return jnp.sum(values.reshape(values.shape[0] // 8, 8, values.shape[1]), axis=0)


def layer_kernel(plan, seq_size, *refs):
    x_ref, cot_ref, seg_ref, wq_hbm, wk_hbm, wv_hbm, wo_hbm, win_hbm, wout_hbm = refs[:9]
    vectors_hbm, vectors = refs[9:18], refs[-9:]
    final, small_out, y_out, dx_out = refs[18:22]
    (total, landing, wproj, xf, qs, key, val, probs, attn, normed, inv1, hid, hid_t, active, slope, cot, ybuf, gout, acc,
     mask, sg, dx_far, small, ss, rs, gs_, gr, gl, ws, ms, mr, ys, yr, xs) = refs[22:-9]
    plan.bind(total, landing, final, ss, rs)
    bq, bv, bo, g1, s1, bi, b2, g2, s2 = (Row(v) for v in vectors)
    dp, sq, side, pair = place(seq_size)
    sibling = (dp + 1 - 2 * side, sq)
    rows, length = x_ref.shape[0], x_ref.shape[1]
    spread = seq_size // 2
    tokens = spread * length
    own, far = side * tokens, (1 - side) * tokens

    barrier = pltpu.get_barrier_semaphore()
    column = [(pair + c, p) for p in range(seq_size) for c in range(2)]
    for to in column:
        pl.when(jnp.logical_not(jnp.logical_and(to[0] == dp, to[1] == sq)))(
            lambda to=to: pl.semaphore_signal(barrier, inc=1, device_id=to, device_id_type=MESH)
        )
    across = [bit for axis, bit in small_bits(plan.dp_size, seq_size) if axis == "dp" and bit > 1]
    for bit in across:
        to = (dp + bit * (1 - 2 * ((dp // bit) % 2)), sq)
        pl.semaphore_signal(barrier, inc=1, device_id=to, device_id_type=MESH)

    loads = {}

    def load(name, src, dst, i):
        loads.setdefault(name, []).append(pltpu.make_async_copy(src, dst, ws.at[i]))
        loads[name][-1].start()

    for i, (name, src) in enumerate((("q", wq_hbm), ("k", wk_hbm), ("v", wv_hbm), ("o", wo_hbm))):
        load(name, src, wproj.at[i], i)
    for i, (src, dst) in enumerate(zip(vectors_hbm, vectors)):
        load("vectors", src, dst, 9 + i)
    for j in range(4):
        load("in", win_hbm.at[:, pl.ds(j * D, D)], total.at[pl.ds(INNER + j * D, D)], 4 + j)
    load("out", wout_hbm, total.at[pl.ds(PROJ, FF)], 8)

    def loaded(name):
        for c in loads[name]:
            c.wait()

    pl.semaphore_wait(barrier, len(column) - 1 + len(across))

    half, spot = sq % 2, sq // 2
    near = sq // 2

    def block(i):
        return pl.ds(pl.multiple_of(i * length, length), length)

    def x_copy(r, b, tgt, at):
        return pltpu.make_async_remote_copy(x_ref.at[r], xf.at[block(at)], gs_.at[0, r], gr.at[0, b], tgt, MESH)

    def c_copy(r, b, tgt):
        return pltpu.make_async_remote_copy(cot_ref.at[r], cot.at[block(b)], gs_.at[1, r], gr.at[1, b], tgt, MESH)

    def s_copy(r, c, at, tgt):
        return pltpu.make_async_remote_copy(seg_ref.at[r], sg.at[at], gs_.at[2 + c, r], gr.at[2, at], tgt, MESH)

    def forward(b, base):
        part = xf.at[block(base + b)]
        return pltpu.make_async_remote_copy(part, part, gs_.at[4, b], gr.at[3, b], sibling, MESH)

    def split(local, near, remote):
        pl.when(local)(near)
        pl.when(jnp.logical_not(local))(remote)

    stays = [jnp.logical_and(half == side, sq == rows * side + r) for r in range(rows)]
    comes = [jnp.logical_and(sq // rows == side, 2 * b + side == sq) for b in range(spread)]

    def x_local(r, at):
        return pltpu.make_async_copy(x_ref.at[r], xf.at[block(at)], gl.at[0])

    def c_local(r, at):
        return pltpu.make_async_copy(cot_ref.at[r], cot.at[block(at)], gl.at[1])

    def s_local(r):
        return pltpu.make_async_copy(seg_ref.at[r], sg.at[sq], gl.at[2])

    mine = [[jnp.logical_and(side == c, sq == rows * side + r) for c in range(2)] for r in range(rows)]
    for r in range(rows):
        for c in range(2):
            split(
                mine[r][c],
                lambda r=r: s_local(r).start(),
                lambda r=r, c=c: s_copy(r, c, sq, (pair + c, rows * side + r)).start(),
            )
    for r in range(rows):
        at = half * spread + spot
        split(
            stays[r],
            lambda r=r, at=at: x_local(r, at).start(),
            lambda r=r, at=at: x_copy(r, spot, (pair + half, rows * side + r), at).start(),
        )

    def token_block(which):
        return pl.ds(pl.multiple_of(which, tokens), tokens)

    def cols(i, n=256):
        return pl.ds(pl.multiple_of(i * n, 128), n)

    def arrive(b):
        split(
            jnp.logical_and(sq // rows == side, 2 * b + side == sq),
            lambda: x_local(0, side * spread + b).wait(),
            lambda: x_copy(0, b, sibling, side * spread + b).wait_recv(),
        )
        forward(b, side * spread).start()

    def project(b, of, also_query):
        at = block(of * spread + b)

        def body(i, _):
            xb = xf[at]
            c = cols(i)
            if also_query:
                qs[block(b), c] = (product(xb, wproj[0, :, c]) + bq[:, c]).astype(BF16) * BF16(0.125)
            key[at, c] = product(xb, wproj[1, :, c]).astype(BF16)
            val[at, c] = (product(xb, wproj[2, :, c]) + bv[:, c]).astype(BF16)
            return 0

        lax.fori_loop(0, D // 256, body, 0, unroll=3)

    arrive(near)
    for name in ("vectors", "q", "k", "v"):
        loaded(name)
    project(near, side, True)
    forward(near, (1 - side) * spread).wait_recv()
    project(near, 1 - side, False)

    for p in range(seq_size):
        split(
            jnp.logical_and(sq // rows == side, p == sq),
            lambda: s_local(0).wait(),
            lambda p=p: s_copy(0, 0, p, sibling).wait_recv(),
        )
    diagonal = lax.broadcasted_iota(jnp.int32, (length, length), 0) == lax.broadcasted_iota(
        jnp.int32, (length, length), 1
    )
    for b in range(spread):
        mine_seg = jnp.broadcast_to(sg[2 * b + side], (length, length))
        column = jnp.sum(jnp.where(diagonal, mine_seg, 0), axis=1, keepdims=True)
        for p in range(seq_size):
            at = (p % 2) * spread + p // 2
            seen = jnp.broadcast_to(column, (length, length)) == jnp.broadcast_to(sg[p], (length, length))
            mask[b * length : (b + 1) * length, at * length : (at + 1) * length] = jnp.where(seen, 0.0, MASKED)

    arrive(1 - near)
    for r in range(rows):
        split(
            stays[r],
            lambda r=r: c_local(r, spot).start(),
            lambda r=r: c_copy(r, spot, (pair + half, rows * side + r)).start(),
        )
    project(1 - near, side, True)
    forward(1 - near, (1 - side) * spread).wait_recv()
    project(1 - near, 1 - side, False)

    lane = lax.broadcasted_iota(jnp.int32, (1, 128), 1)
    first = (lane < HD).astype(BF16)
    picks = (first, BF16(1.0) - first)
    low_lanes = lane < HD

    def attend(i, _):
        c = cols(i, 128)
        qp, kp, vp = qs[:, c], key[:, c], val[:, c]
        outs = []
        for n in range(2):
            s = product_nt(qp * picks[n], kp) + mask[...]
            e = jnp.exp(s - jnp.max(s, axis=-1, keepdims=True))
            p = (e * (1.0 / jnp.sum(e, axis=-1, keepdims=True))).astype(BF16)
            probs[2 * i + n] = p
            outs.append(product(p, vp))
        attn[:, c] = jnp.where(low_lanes, outs[0], outs[1]).astype(BF16)
        return 0

    lax.fori_loop(0, D // 128, attend, 0, unroll=3)

    loaded("o")

    def branch(i, _):
        c = cols(i)
        acc[:, c] = product(attn[...], wproj[3, :, c]) + bo[:, c] + xf[token_block(own), c].astype(F32)
        return 0

    lax.fori_loop(0, D // 256, branch, 0, unroll=3)
    step = 32

    def chunk(i):
        return pl.ds(pl.multiple_of(i * step, step), step)

    def norm_one(i, _):
        r = chunk(i)
        v = acc[r]
        centre = v - jnp.mean(v, axis=-1, keepdims=True)
        inv = lax.rsqrt(jnp.mean(centre * centre, axis=-1, keepdims=True) + EPSILON)
        n = centre * inv
        normed[r] = n
        inv1[r] = jnp.broadcast_to(inv, (step, 128))
        hid[r] = (n * g1[...] + s1[...]).astype(BF16)
        return 0

    lax.fori_loop(0, tokens // step, norm_one, 0, unroll=4)

    loaded("in")
    loaded("out")

    def inner_cols(j, i):
        return total.at[pl.ds(INNER + j * D, D), cols(i)]

    for j in range(4):

        def expand(i, _, j=j):
            c = cols(j * 3 + i)
            v = product(hid[...], inner_cols(j, i)[...]) + bi[:, c]
            cdf = 0.5 * (1.0 + lax.erf(v * INV_ROOT_TWO))
            active[:, c] = (v * cdf).astype(BF16)
            slope[:, c] = v
            return 0

        lax.fori_loop(0, 3, expand, 0, unroll=3)

    def contract(i, _):
        c = cols(i)
        acc[:, c] = product(active[...], total[pl.ds(PROJ, FF), c]) + b2[:, c]
        return 0

    lax.fori_loop(0, D // 256, contract, 0, unroll=3)
    for b in range(spread):
        split(comes[b], lambda b=b: c_local(b, b).wait(), lambda b=b: c_copy(0, b, sibling).wait_recv())

    small[0] = jnp.zeros((16, D), F32)

    def norm_two(i, carry):
        d_gain, d_shift, d_bias = carry
        r = chunk(i)
        v = normed[r] * g1[...] + s1[...] + acc[r]
        centre = v - jnp.mean(v, axis=-1, keepdims=True)
        inv = lax.rsqrt(jnp.mean(centre * centre, axis=-1, keepdims=True) + EPSILON)
        n = centre * inv
        ybuf[r] = (n * g2[...] + s2[...]).astype(BF16)
        g = cot[r].astype(F32)
        scaled = g * g2[...]
        grad = inv * (
            scaled - jnp.mean(scaled, axis=-1, keepdims=True) - n * jnp.mean(scaled * n, axis=-1, keepdims=True)
        )
        grad_low = grad.astype(BF16)
        gout[r] = grad_low
        acc[r] = grad
        return d_gain + fold(g * n), d_shift + fold(g), d_bias + fold(grad_low.astype(F32))

    zero = jnp.zeros((8, D), F32)
    sums = lax.fori_loop(0, tokens // step, norm_two, (zero, zero, zero), unroll=4)
    for at, v in zip((6, 7, 5), sums):
        small[0, at : at + 1] = jnp.sum(v, axis=0, keepdims=True)

    homes = [(pair + sq // rows, 2 * b + side) for b in range(spread)]
    at_home = [jnp.logical_and(h[0] == dp, h[1] == sq) for h in homes]

    def back(src, dst, b, lane_, to, slot):
        return pltpu.make_async_remote_copy(
            src.at[pl.ds(b * length, length)], dst.at[slot], ys.at[lane_, b], yr.at[lane_, slot], to, MESH
        )

    def home_local(src, dst, b, lane_):
        return pltpu.make_async_copy(src.at[pl.ds(b * length, length)], dst.at[sq % rows], xs.at[2 + lane_])

    def send_home(src, dst, lane_):
        for b in range(spread):
            split(
                at_home[b],
                lambda b=b: home_local(src, dst, b, lane_).start(),
                lambda b=b: back(src, dst, b, lane_, homes[b], sq % rows).start(),
            )

    def sent_home(src, dst, lane_):
        for b in range(spread):
            split(
                at_home[b],
                lambda b=b: home_local(src, dst, b, lane_).wait(),
                lambda b=b: back(src, dst, b, lane_, homes[b], sq % rows).wait_send(),
            )
        for r in range(rows):
            pl.when(jnp.logical_not(jnp.logical_and(half == side, sq == rows * side + r)))(
                lambda r=r: back(src, dst, 0, lane_, sibling, r).wait_recv()
            )

    send_home(ybuf, y_out, 0)


    bits = small_bits(plan.dp_size, seq_size)

    def small_copy(i):
        axis, bit = bits[i]
        if axis == "dp":
            tgt = (dp + bit * (1 - 2 * ((dp // bit) % 2)), sq)
        else:
            tgt = (dp, sq + bit * (1 - 2 * ((sq // bit) % 2)))
        return pltpu.make_async_remote_copy(small.at[i], small.at[len(bits) + 1 + i], ms.at[i], mr.at[i], tgt, MESH)

    def outer_part(n):
        def body(i, _):
            t = n * 2 + i
            total[pl.ds(pl.multiple_of(OUTER + t * 256, 256), 256)] = product(
                active[:, cols(t)].T, gout[...]
            ).astype(BF16)
            return 0

        lax.fori_loop(0, 2, body, 0, unroll=2)

    def inner_part(j):
        if j == 0:
            for i in range(3):
                hid_t[i * 256 : (i + 1) * 256] = hid[:, i * 256 : (i + 1) * 256].T

        def body(i, _):
            t = j * 3 + i
            up = product_nt(gout[...], total[pl.ds(pl.multiple_of(PROJ + t * 256, 256), 256)])
            v = slope[:, cols(t)]
            cdf = 0.5 * (1.0 + lax.erf(v * INV_ROOT_TWO))
            gi = (up * (cdf + v * DENSITY * jnp.exp(-0.5 * v * v))).astype(BF16)
            small[0, 8 + j : 9 + j, cols(i)] = jnp.sum(fold(gi.astype(F32)), axis=0, keepdims=True)
            view = inner_cols(j, i)
            acc[...] += product_nt(gi, view[...])
            view[...] = product(hid_t[...], gi).astype(BF16)
            return 0

        lax.fori_loop(0, 3, body, 0, unroll=3)

    def norm_one_part():
        def body(i, carry):
            d_gain, d_shift, d_bias = carry
            r = chunk(i)
            g, n = acc[r], normed[r]
            scaled = g * g1[...]
            grad = inv1[r][:, :1] * (
                scaled - jnp.mean(scaled, axis=-1, keepdims=True) - n * jnp.mean(scaled * n, axis=-1, keepdims=True)
            )
            grad_low = grad.astype(BF16)
            gout[r] = grad_low
            acc[r] = grad
            return d_gain + fold(g * n), d_shift + fold(g), d_bias + fold(grad_low.astype(F32))

        out = lax.fori_loop(0, tokens // step, body, (zero, zero, zero), unroll=2)
        for at, v in zip((3, 4, 2), out):
            small[0, at : at + 1] = jnp.sum(v, axis=0, keepdims=True)

    def branch_part():
        def body(i, _):
            total[pl.ds(pl.multiple_of(PROJ + i * 256, 256), 256)] = product(attn[:, cols(i)].T, gout[...]).astype(BF16)
            cot[:, cols(i)] = product_nt(gout[...], wproj[3, pl.ds(pl.multiple_of(i * 256, 256), 256)]).astype(BF16)
            return 0

        lax.fori_loop(0, D // 256, body, 0, unroll=3)

    def attention_part(n):
        def body(m, _):
            i = n * 2 + m
            c = cols(i, 128)
            qp, kp, vp, gp = qs[:, c], key[:, c], val[:, c], cot[:, c]
            dq, dk, dv = [], [], []
            for h in range(2):
                p = probs[2 * i + h]
                pf = p.astype(F32)
                weighted = pf * product_nt(gp * picks[h], vp)
                delta = jnp.sum(weighted, axis=-1, keepdims=True)
                gs = (weighted - pf * delta).astype(BF16)
                dq.append(product(gs, kp))
                dk.append(product_tn(gs, qp))
                dv.append(product_tn(p, gp))
            gq = (jnp.where(low_lanes, dq[0], dq[1]) * 0.125).astype(BF16)
            gk = jnp.where(low_lanes, dk[0], dk[1]).astype(BF16)
            gv = jnp.where(low_lanes, dv[0], dv[1]).astype(BF16)
            qs[:, c] = gq
            small[0, 0:1, c] = jnp.sum(fold(gq.astype(F32)), axis=0, keepdims=True)
            small[0, 1:2, c] = jnp.sum(fold(gv.astype(F32)), axis=0, keepdims=True)
            for b in range(2):
                active[:, cols(b * 6 + i, 128)] = gk[b * tokens : (b + 1) * tokens]
                active[:, cols(12 + b * 6 + i, 128)] = gv[b * tokens : (b + 1) * tokens]
            return 0

        lax.fori_loop(0, 2, body, 0, unroll=2)
        if n == 2:
            small_copy(0).start()

    def query_part():
        def body(i, _):
            total[pl.ds(pl.multiple_of(PROJ + D + i * 256, 256), 256)] = product(
                xf[token_block(own), cols(i)].T, qs[...]
            ).astype(BF16)
            return 0

        lax.fori_loop(0, D // 256, body, 0, unroll=3)

    def key_part():
        def body(i, _):
            left = xf[pl.ds(0, tokens), cols(i)].T
            right = xf[pl.ds(tokens, tokens), cols(i)].T
            for n in range(2):
                base = n * 2 * D
                total[pl.ds(pl.multiple_of(PROJ + (2 + n) * D + i * 256, 256), 256)] = (
                    product(left, active[:, base : base + D]) + product(right, active[:, base + D : base + 2 * D])
                ).astype(BF16)
            return 0

        lax.fori_loop(0, D // 256, body, 0, unroll=3)

    dx_send = pltpu.make_async_remote_copy(hid, dx_far, xs.at[0], xs.at[1], sibling, MESH)

    def input_part():
        def both(s, w):
            return product_nt(active[:, pl.ds(pl.multiple_of(s * D, 128), D)], wproj[1, w]) + product_nt(
                active[:, pl.ds(pl.multiple_of((2 + s) * D, 128), D)], wproj[2, w]
            )

        def body(i, _):
            w = pl.ds(pl.multiple_of(i * 256, 256), 256)
            hid[:, cols(i)] = both(1 - side, w).astype(BF16)
            acc[:, cols(i)] += product_nt(qs[...], wproj[0, w]) + both(side, w)
            return 0

        lax.fori_loop(0, D // 256, body, 0, unroll=3)
        dx_send.start()

    def input_end():
        dx_send.wait_recv()

        def body(i, _):
            r = chunk(i)
            gout[r] = (acc[r] + dx_far[r].astype(F32)).astype(BF16)
            return 0

        lax.fori_loop(0, tokens // step, body, 0)
        send_home(gout, dx_out, 1)

    def small_part(n):
        for i in range(n, n + 1 if n < SMALL_PARTS - 1 else len(bits)):
            small_copy(i).wait_recv()
            small[i + 1] = small[i] + small[len(bits) + 1 + i]
            if i + 1 < len(bits):
                small_copy(i + 1).start()

    parts = (
        [functools.partial(outer_part, n) for n in range(6)]
        + [functools.partial(inner_part, j) for j in range(4)]
        + [norm_one_part, branch_part]
        + [functools.partial(attention_part, n) for n in range(3)]
        + [query_part, key_part, input_part, input_end]
        + [functools.partial(small_part, n) for n in range(SMALL_PARTS)]
    )
    ready = {n: (n,) for n in range(6)}
    ready.update({6: (6,), 7: (7, 8), 8: (9,), 9: (10, 11), 11: (12,), 15: (13, 14), 16: (15, 16, 17)})
    scripts = [iter(plan.script(p)) for p in plan.pieces]
    for entry in ORDER:
        if entry >= 0:
            next(scripts[entry])[1]()
            continue
        parts[-entry - 1]()
        for n in ready.get(-entry - 1, ()):
            plan.rs_start(plan.pieces[n], 0)
    small_out[...] = small[len(bits)]
    for i in range(len(bits)):
        small_copy(i).wait_send()
    dx_send.wait_send()
    sent_home(ybuf, y_out, 0)
    sent_home(gout, dx_out, 1)
    for r in range(rows):
        for c in range(2):
            pl.when(jnp.logical_not(mine[r][c]))(lambda r=r, c=c: s_copy(r, c, sq, sibling).wait_send())
        pl.when(jnp.logical_not(stays[r]))(lambda r=r: x_copy(r, spot, sibling, 0).wait_send())
        pl.when(jnp.logical_not(stays[r]))(lambda r=r: c_copy(r, spot, sibling).wait_send())
    for b in range(spread):
        forward(b, side * spread).wait_send()
    plan.finish()


def whole_layer(args, dp_size, seq_size):
    (layer_input, segment_ids, w_query, b_query, w_key, w_value, b_value, w_out, b_out, gain_one, shift_one,
     w_inner, b_inner, w_outer, b_outer, gain_two, shift_two, cotangent) = args
    plan = Exchange(dp_size, seq_size, 6)
    rows, length, width = layer_input.shape
    tokens = seq_size * length // 2
    vmem, anyw = pl.BlockSpec(memory_space=pltpu.VMEM), pl.BlockSpec(memory_space=pl.ANY)
    nbits = len(small_bits(dp_size, seq_size))
    back = pltpu.VMEM((rows, length, width), BF16)
    dma = pltpu.SemaphoreType.DMA
    vectors = (b_query, b_value, b_out, gain_one, shift_one, b_inner, b_outer, gain_two, shift_two)
    return pl.pallas_call(
        functools.partial(layer_kernel, plan, seq_size),
        out_shape=(pltpu.VMEM((3 * FF, D), BF16), pltpu.VMEM((16, D), F32), back, back),
        in_specs=[anyw] * 18,
        out_specs=(vmem,) * 4,
        scratch_shapes=[
            pltpu.VMEM((3 * FF, D), BF16),
            pltpu.VMEM((plan.slots, D), BF16),
            pltpu.VMEM((4, D, D), BF16),
            pltpu.VMEM((2 * tokens, D), BF16),
            pltpu.VMEM((tokens, D), BF16),
            pltpu.VMEM((2 * tokens, D), BF16),
            pltpu.VMEM((2 * tokens, D), BF16),
            pltpu.VMEM((D // HD, tokens, 2 * tokens), BF16),
            pltpu.VMEM((tokens, D), BF16),
            pltpu.VMEM((tokens, D), F32),
            pltpu.VMEM((tokens, 128), F32),
            pltpu.VMEM((tokens, D), BF16),
            pltpu.VMEM((D, tokens), BF16),
            pltpu.VMEM((tokens, FF), BF16),
            pltpu.VMEM((tokens, FF), F32),
            pltpu.VMEM((tokens, D), BF16),
            pltpu.VMEM((tokens, D), BF16),
            pltpu.VMEM((tokens, D), BF16),
            pltpu.VMEM((tokens, D), F32),
            pltpu.VMEM((tokens, 2 * tokens), F32),
            pltpu.VMEM((seq_size, 1, length), jnp.int32),
            pltpu.VMEM((tokens, D), BF16),
            pltpu.VMEM((2 * nbits + 1, 16, D), F32),
            dma((2 * len(LANES) + 1,)), dma((plan.sems,)),
            dma((5, 2)), dma((4, seq_size)), dma((3,)), dma((18,)),
            dma((nbits,)), dma((nbits,)), dma((2, 2)), dma((2, 2)), dma((4,)),
        ]
        + [pltpu.VMEM(v.shape, F32) for v in vectors],
        compiler_params=pltpu.CompilerParams(collective_id=1, has_side_effects=True, vmem_limit_bytes=VMEM_LIMIT),
        name="layer",
    )(
        layer_input, cotangent, segment_ids.reshape(rows, 1, length), w_query, w_key, w_value, w_out, w_inner, w_outer,
        *vectors,
    )


VMEM_LIMIT = 46 << 20


def widen_kernel(sums, small, y_in, dx_in, *refs):
    outs, (wide, sem, far) = refs[:17], refs[17:]
    (y, dx, d_query, d_b_query, d_key, d_value, d_b_value, d_out, d_b_out, d_gain_one, d_shift_one, d_inner,
     d_b_inner, d_outer, d_b_outer, d_gain_two, d_shift_two) = outs
    rows = [pltpu.make_async_copy(y_in, y, far.at[0]), pltpu.make_async_copy(dx_in, dx, far.at[1])]
    for c in rows:
        c.start()
    for i, o in enumerate((d_b_query, d_b_value, d_b_out, d_gain_one, d_shift_one, d_b_outer, d_gain_two, d_shift_two)):
        o[...] = small[i]
    for j in range(4):
        d_b_inner[j * D : (j + 1) * D] = small[8 + j]
    step = 384
    copies = []
    for n in range(3 * FF // step):
        at = n * step
        if at < INNER:
            view = d_outer.at[pl.ds(at, step)]
        elif at < PROJ:
            j, row = (at - INNER) // D, (at - INNER) % D
            view = d_inner.at[pl.ds(row, step), pl.ds(j * D, D)]
        else:
            j, row = (at - PROJ) // D, (at - PROJ) % D
            view = (d_out, d_query, d_key, d_value)[j].at[pl.ds(row, step)]
        slot = n % 4
        if n >= 4:
            copies[n - 4].wait()

        def body(i, _, at=at, slot=slot):
            wide[slot, pl.ds(pl.multiple_of(i * 32, 32), 32)] = sums[pl.ds(pl.multiple_of(at + i * 32, 32), 32)].astype(F32)
            return 0

        lax.fori_loop(0, step // 32, body, 0, unroll=4)
        copies.append(pltpu.make_async_copy(wide.at[slot], view, sem.at[slot]))
        copies[-1].start()
    for c in copies[-4:] + rows:
        c.wait()


def widen(sums, small, y, dx):
    vmem, anyw = pl.BlockSpec(memory_space=pltpu.VMEM), pl.BlockSpec(memory_space=pl.ANY)
    back = jax.ShapeDtypeStruct(y.shape, BF16)
    square, vector = jax.ShapeDtypeStruct((D, D), F32), jax.ShapeDtypeStruct((D,), F32)
    shapes = (
        back, back, square, vector, square, square, vector, square, vector, vector, vector,
        jax.ShapeDtypeStruct((D, FF), F32), jax.ShapeDtypeStruct((FF,), F32), jax.ShapeDtypeStruct((FF, D), F32),
        vector, vector, vector,
    )
    return pl.pallas_call(
        widen_kernel,
        out_shape=shapes,
        in_specs=[vmem] * 4,
        out_specs=tuple(vmem if len(o.shape) == 1 else anyw for o in shapes),
        scratch_shapes=[
            pltpu.VMEM((4, 384, D), F32), pltpu.SemaphoreType.DMA((4,)), pltpu.SemaphoreType.DMA((2,)),
        ],
        compiler_params=pltpu.CompilerParams(vmem_limit_bytes=16 << 20),
        name="widen",
    )(sums, small, y, dx)


def on_device(dp_size, seq_size, *args):
    return widen(*whole_layer(args, dp_size, seq_size))


def solution(mesh):
    sizes = (mesh.shape["dp"], mesh.shape["seq"])
    tokens = P("dp", "seq", None)
    return jax.shard_map(
        functools.partial(on_device, *sizes),
        mesh=mesh,
        in_specs=(tokens, P("dp", "seq")) + (P(),) * 15 + (tokens,),
        out_specs=(tokens, tokens) + (P(),) * 15,
        check_vma=False,
    )
```

```python
import functools

import jax
import jax.numpy as jnp
from jax import lax
from jax.experimental import pallas as pl
from jax.experimental.pallas import tpu as pltpu
from jax.sharding import PartitionSpec as P

HD = 64
EPSILON = 1e-12
MASKED = -1000000000.0
INV_ROOT_TWO = 0.7071067811865476
DENSITY = 0.3989422804014327
MESH = pl.DeviceIdType.MESH
BF16 = jnp.bfloat16
F32 = jnp.float32


def product(left, right):
    return jnp.dot(left, right, preferred_element_type=F32)


def product_tn(left, right):
    return lax.dot_general(left, right, (((0,), (0,)), ((), ())), preferred_element_type=F32)


def product_nt(left, right):
    return lax.dot_general(left, right, (((1,), (1,)), ((), ())), preferred_element_type=F32)


def place(seq_size):
    dp, sq = lax.axis_index("dp"), lax.axis_index("seq")
    side = dp % 2
    return dp, sq, side, dp - side


GROUP = 1536
PIECE = 512
ORDERS = (("yxz", "yxz", "zxy"), ("zyx", "xyz", "xyz"), ("yxz", "xzy", "yxz"), ("zxy", "xyz", "xyz"), ("yzx", "xyz", "yxz"), ("yzx", "xyz", "yxz"))
SUBS = 1
LANES = "cxyz"


class Exchange:
    def __init__(self, dp_size, seq_size, groups):
        self.dp_size, self.seq_size, self.groups = dp_size, seq_size, groups
        self.extra = []
        bit = 8
        while bit < dp_size:
            self.extra.append(bit)
            bit *= 2
        self.sems = 0
        self.slots = 0
        self.pieces = []
        for g in range(groups):
            for cls in range(3):
                self.pieces.append(self.plan(g * GROUP + cls * PIECE, ORDERS[g % len(ORDERS)][cls]))

    def sem(self):
        self.sems += 1
        return self.sems - 1

    def slot(self, rows):
        self.slots += rows
        return self.slots - rows

    def plan(self, base, order):
        stages, rows, ends = [], PIECE, False
        for axis in "c" + order:
            half = rows // 2
            st = dict(axis=axis, rows=half, ends=ends)
            if axis == "z":
                n = half // SUBS
                st["down"] = [dict(rs=self.sem(), ag=self.sem(), slot=self.slot(n), rows=n, at=i * n) for i in range(SUBS)]
                st["up"] = [dict(rs=self.sem(), ag=self.sem(), slot=self.slot(n), rows=n, at=i * n) for i in range(SUBS)]
                ends = True
            else:
                st.update(rs=self.sem(), ag=self.sem(), slot=None if axis == "c" else self.slot(half))
            stages.append(st)
            rows = half
        more = [dict(bit=b, rs=self.sem(), slot=self.slot(rows)) for b in self.extra]
        return dict(base=base, stages=stages, more=more, rows=rows)

    def bind(self, total, slots, final, send_sem, recv_sem):
        self.total, self.landing, self.final = total, slots, final
        self.ss, self.rs = send_sem, recv_sem
        dp, sq = lax.axis_index("dp"), lax.axis_index("seq")
        self.dp, self.sq = dp, sq
        self.bits = {"c": (1, dp % 2), "x": (2, (dp // 2) % 2), "y": (4, (dp // 4) % 2)}
        self.last = self.seq_size - 1
        self.edge = jnp.logical_or(sq == 0, sq == self.last)
        self.side = sq // self.last
        self.rows_sent = {}
        for p in self.pieces:
            off = p["base"]
            for st in p["stages"]:
                half = st["rows"]
                st["off"] = off
                value = self.side if st["axis"] == "z" else self.bits[st["axis"]][1]
                st["keep"] = off + value * half
                st["give"] = off + (1 - value) * half
                off = st["keep"]
            p["own"] = off

    def view(self, off, rows):
        return self.total.at[pl.ds(pl.multiple_of(off, 16), rows)]

    def partner(self, axis):
        bit, value = self.bits[axis]
        return (self.dp + bit * (1 - 2 * value), self.sq)

    def copy(self, src, dst, lane, sem, tgt):
        return pltpu.make_async_remote_copy(src, dst, self.ss.at[lane], self.rs.at[sem], tgt, MESH)

    def send(self, copy, lane, rows, who):
        copy.start()
        for place_ in who:
            self.rows_sent[lane, place_] = self.rows_sent.get((lane, place_), 0) + rows

    def everyone(self, st):
        return (0, self.last) if st["ends"] else range(self.seq_size)

    def gated(self, when, f):
        if when is None:
            f()
        else:
            pl.when(when)(f)

    def done(self, off, rows):
        return self.final.at[pl.ds(pl.multiple_of(off, 16), rows)]

    def landed(self, st):
        if st["slot"] is None:
            return self.done(st["give"], st["rows"])
        return self.landing.at[pl.ds(st["slot"], st["rows"])]

    def add(self, off, slot, rows, into=None):
        into = self.total if into is None else into
        source = self.final if slot is None else self.landing
        slot = off if slot is None else slot
        step = 32 if rows % 32 == 0 else 16

        def body(i, _):
            at = pl.multiple_of(off + i * step, 16)
            frm = pl.multiple_of(slot + i * step, 16)
            into[pl.ds(at, step)] = self.total[pl.ds(at, step)] + source[pl.ds(frm, step)]
            return 0

        lax.fori_loop(0, rows // step, body, 0)


    def rs_start(self, p, i):
        st = p["stages"][i]
        if st["axis"] == "z":
            for way, at, to, base in (("down", self.last, -1, 0), ("up", 0, 1, st["rows"])):
                when = self.sq == at

                def f(way=way, at=at, to=to, base=base):
                    for s in st[way]:
                        self.send(self.rs_copy(st, s, base, to), LANES.index("z"), s["rows"], (at,))
                self.gated(when, f)
        else:
            when = self.edge if st["ends"] else None

            def f():
                self.send(self.rs_pair(st), LANES.index(st["axis"]), st["rows"], self.everyone(st))
            self.gated(when, f)

    def rs_pair(self, st):
        return self.copy(
            self.view(st["give"], st["rows"]), self.landed(st), LANES.index(st["axis"]), st["rs"], self.partner(st["axis"])
        )

    def rs_hyper(self, p, i):
        st = p["stages"][i]

        def f():
            self.rs_pair(st).wait_recv()
            self.add(st["keep"], st["slot"], st["rows"], self.final if i + 1 == len(p["stages"]) else None)
        self.gated(self.edge if st["ends"] else None, f)

    def rs_hop(self, p, i, hop):
        st = p["stages"][i]
        for way, at, to, base in (("down", self.last - hop, -1, 0), ("up", hop, 1, st["rows"])):
            when = self.sq == at

            def f(way=way, at=at, to=to, base=base):
                for s in st[way]:
                    self.rs_copy(st, s, base, -to).wait_recv()
                    ended = hop == self.last and i + 1 == len(p["stages"])
                    self.add(st["off"] + base + s["at"], s["slot"], s["rows"], self.final if ended else None)
                    if hop < self.last:
                        self.send(self.rs_copy(st, s, base, to), LANES.index("z"), s["rows"], (at,))
            self.gated(when, f)

    def rs_copy(self, st, s, base, to):
        return self.copy(
            self.view(st["off"] + base + s["at"], s["rows"]), self.landing.at[pl.ds(s["slot"], s["rows"])],
            LANES.index("z"), s["rs"], (self.dp, self.sq + to),
        )

    def more(self, p):
        for m in p["more"]:
            bit = m["bit"]
            value = (self.dp // bit) % 2
            tgt = (self.dp + bit * (1 - 2 * value), self.sq)

            def f():
                c = self.copy(
                    self.done(p["own"], p["rows"]), self.landing.at[pl.ds(m["slot"], p["rows"])], len(LANES) * 2, m["rs"], tgt
                )
                c.start()
                c.wait()
                part = pl.ds(pl.multiple_of(p["own"], 16), p["rows"])
                self.final[part] = self.final[part] + self.landing[pl.ds(m["slot"], p["rows"])]
            self.gated(self.edge, f)


    def ag_start(self, p, i):
        st = p["stages"][i]
        if st["axis"] == "z":
            for way, at, to, base in (("down", self.last, -1, st["rows"]), ("up", 0, 1, 0)):
                when = self.sq == at

                def f(way=way, at=at, to=to, base=base):
                    for s in st[way]:
                        self.send(self.ag_copy(st, s, base, to), len(LANES) + LANES.index("z"), s["rows"], (at,))
                self.gated(when, f)
        else:
            when = self.edge if st["ends"] else None

            def f():
                self.send(
                    self.ag_pair(st, st["keep"]), len(LANES) + LANES.index(st["axis"]), st["rows"], self.everyone(st)
                )
            self.gated(when, f)

    def ag_copy(self, st, s, base, to):
        part = self.done(st["off"] + base + s["at"], s["rows"])
        return self.copy(part, part, len(LANES) + LANES.index("z"), s["ag"], (self.dp, self.sq + to))

    def ag_pair(self, st, off):
        part = self.done(off, st["rows"])
        return self.copy(part, part, len(LANES) + LANES.index(st["axis"]), st["ag"], self.partner(st["axis"]))

    def ag_hyper(self, p, i):
        st = p["stages"][i]

        def f():
            self.ag_pair(st, st["give"]).wait_recv()
        self.gated(self.edge if st["ends"] else None, f)

    def ag_hop(self, p, i, hop):
        st = p["stages"][i]
        for way, at, to, base in (("down", self.last - hop, -1, st["rows"]), ("up", hop, 1, 0)):
            when = self.sq == at

            def f(way=way, at=at, to=to, base=base):
                for s in st[way]:
                    self.ag_copy(st, s, base, -to).wait_recv()
                    if hop < self.last:
                        self.send(self.ag_copy(st, s, base, to), len(LANES) + LANES.index("z"), s["rows"], (at,))
            self.gated(when, f)

    def script(self, p):
        steps, n = [], len(p["stages"])
        for i, st in enumerate(p["stages"]):
            after = (lambda i=i: self.rs_start(p, i + 1)) if i + 1 < n else (lambda: (self.more(p), self.ag_start(p, n - 1)))
            if st["axis"] == "z":
                for hop in range(1, self.last + 1):
                    def step(i=i, hop=hop, after=after):
                        self.rs_hop(p, i, hop)
                        if hop == self.last:
                            after()
                    steps.append((f"rz{hop}", step))
            else:
                def step(i=i, after=after):
                    self.rs_hyper(p, i)
                    after()
                steps.append(("r" + st["axis"], step))
        for i in reversed(range(n)):
            st = p["stages"][i]
            after = (lambda i=i: self.ag_start(p, i - 1)) if i > 0 else (lambda: None)
            if st["axis"] == "z":
                for hop in range(1, self.last + 1):
                    def step(i=i, hop=hop, after=after):
                        self.ag_hop(p, i, hop)
                        if hop == self.last:
                            after()
                    steps.append((f"gz{hop}", step))
            else:
                def step(i=i, after=after):
                    self.ag_hyper(p, i)
                    after()
                steps.append(("g" + st["axis"], step))
        return steps

    def finish(self):
        for lane in range(2 * len(LANES)):
            rows = [self.rows_sent[lane, p] for p in range(self.seq_size)]

            def f(n, lane=lane):
                self.copy(self.total.at[pl.ds(0, n)], self.total.at[pl.ds(0, n)], lane, 0, self.partner("c")).wait_send()

            if min(rows) == max(rows):
                f(rows[0])
            else:
                for p in range(self.seq_size):
                    pl.when(self.sq == p)(functools.partial(f, rows[p]))


def small_bits(dp_size, seq_size):
    out, bit = [], 1
    while bit < dp_size:
        out.append(("dp", bit))
        bit *= 2
    bit = 1
    while bit < seq_size:
        out.append(("seq", bit))
        bit *= 2
    return out


D = 768
FF = 3072
OUTER, INNER, PROJ = 0, 3072, 6144
ORDER = (
    -1, -2, -3, -4, 0, -5, -6, 1, -7, 3, 2, 4, -8, 6, 5, 0, -9, 7, 8, -10, 1, 3, 4, 9,
    -11, -12, 10, 11, -13, 6, 5, 2, 0, 12, -14, 3, 9, 8, -15, 4, 7, 0, -16, 1, 5, 2, -17, 13,
    4, 3, 14, -18, 7, 9, 15, 12, 16, 0, 1, 10, 17, 4, 5, -19, -20, 3, 2, 11, 7, 12, 1, 6,
    5, 9, 14, 0, 8, 4, 15, 13, 6, 10, 0, 8, 4, 16, 12, 7, -21, 17, 15, 6, 1, 3, 10, 0,
    5, 11, 8, 2, 4, 12, 13, 1, 6, 9, 5, 15, 0, 16, 11, 10, 8, 7, 13, 14, 1, 4, -22, 6,
    5, 2, 17, 16, 11, 15, 3, 8, 9, 13, 10, 7, 14, 12, 6, 1, 16, -23, 17, 4, 0, 8, 5, 15,
    10, 2, 14, 11, 12, 13, 3, 7, 6, 9, -24, 1, 17, 16, 10, 11, 8, 14, 12, 7, 17, 4, 0, 13,
    11, 10, 15, 4, 5, 0, 2, 12, 7, 3, 13, 11, 6, 16, 1, 14, 9, 17, 12, 1, 10, 13, 8, 15,
    11, 3, 16, 14, 5, 2, 17, 6, 5, 15, 6, 3, 7, 9, 16, 3, 12, 14, 7, 17, 2, 12, 13, 10,
    15, 10, 9, 8, 11, 2, 8, 16, 11, 14, 2, 17, 9, 15, 9, 15, 13, 14, 13, 14, 16, 17, 16, 17,
)


SMALL_PARTS = 5


class Row:
    def __init__(self, ref):
        self.ref = ref

    def __getitem__(self, at):
        return (self.ref[...] if at is Ellipsis else self.ref[at[1]]).reshape(1, -1)


def fold(values):
    return jnp.sum(values.reshape(values.shape[0] // 8, 8, values.shape[1]), axis=0)


def layer_kernel(plan, seq_size, *refs):
    x_ref, cot_ref, seg_ref, wq_hbm, wk_hbm, wv_hbm, wo_hbm, win_hbm, wout_hbm = refs[:9]
    vectors_hbm, vectors = refs[9:18], refs[-9:]
    final, small_out, y_out, dx_out = refs[18:22]
    (total, landing, wproj, xf, qs, key, val, probs, attn, normed, inv1, hid, hid_t, active, slope, cot, ybuf, gout, acc,
     mask, sg, dx_far, small, ss, rs, gs_, gr, gl, ws, ms, mr, ys, yr, xs) = refs[22:-9]
    plan.bind(total, landing, final, ss, rs)
    bq, bv, bo, g1, s1, bi, b2, g2, s2 = (Row(v) for v in vectors)
    dp, sq, side, pair = place(seq_size)
    sibling = (dp + 1 - 2 * side, sq)
    rows, length = x_ref.shape[0], x_ref.shape[1]
    spread = seq_size // 2
    tokens = spread * length
    own, far = side * tokens, (1 - side) * tokens

    barrier = pltpu.get_barrier_semaphore()
    column = [(pair + c, p) for p in range(seq_size) for c in range(2)]
    for to in column:
        pl.when(jnp.logical_not(jnp.logical_and(to[0] == dp, to[1] == sq)))(
            lambda to=to: pl.semaphore_signal(barrier, inc=1, device_id=to, device_id_type=MESH)
        )
    across = [bit for axis, bit in small_bits(plan.dp_size, seq_size) if axis == "dp" and bit > 1]
    for bit in across:
        to = (dp + bit * (1 - 2 * ((dp // bit) % 2)), sq)
        pl.semaphore_signal(barrier, inc=1, device_id=to, device_id_type=MESH)

    loads = {}

    def load(name, src, dst, i):
        loads.setdefault(name, []).append(pltpu.make_async_copy(src, dst, ws.at[i]))
        loads[name][-1].start()

    for i, (name, src) in enumerate((("q", wq_hbm), ("k", wk_hbm), ("v", wv_hbm), ("o", wo_hbm))):
        load(name, src, wproj.at[i], i)
    for i, (src, dst) in enumerate(zip(vectors_hbm, vectors)):
        load("vectors", src, dst, 9 + i)
    for j in range(4):
        load("in", win_hbm.at[:, pl.ds(j * D, D)], total.at[pl.ds(INNER + j * D, D)], 4 + j)
    load("out", wout_hbm, total.at[pl.ds(PROJ, FF)], 8)

    def loaded(name):
        for c in loads[name]:
            c.wait()

    pl.semaphore_wait(barrier, len(column) - 1 + len(across))

    half, spot = sq % 2, sq // 2
    near = sq // 2

    def block(i):
        return pl.ds(pl.multiple_of(i * length, length), length)

    def x_copy(r, b, tgt, at):
        return pltpu.make_async_remote_copy(x_ref.at[r], xf.at[block(at)], gs_.at[0, r], gr.at[0, b], tgt, MESH)

    def c_copy(r, b, tgt):
        return pltpu.make_async_remote_copy(cot_ref.at[r], cot.at[block(b)], gs_.at[1, r], gr.at[1, b], tgt, MESH)

    def s_copy(r, c, at, tgt):
        return pltpu.make_async_remote_copy(seg_ref.at[r], sg.at[at], gs_.at[2 + c, r], gr.at[2, at], tgt, MESH)

    def forward(b, base):
        part = xf.at[block(base + b)]
        return pltpu.make_async_remote_copy(part, part, gs_.at[4, b], gr.at[3, b], sibling, MESH)

    def split(local, near, remote):
        pl.when(local)(near)
        pl.when(jnp.logical_not(local))(remote)

    stays = [jnp.logical_and(half == side, sq == rows * side + r) for r in range(rows)]
    comes = [jnp.logical_and(sq // rows == side, 2 * b + side == sq) for b in range(spread)]

    def x_local(r, at):
        return pltpu.make_async_copy(x_ref.at[r], xf.at[block(at)], gl.at[0])

    def c_local(r, at):
        return pltpu.make_async_copy(cot_ref.at[r], cot.at[block(at)], gl.at[1])

    def s_local(r):
        return pltpu.make_async_copy(seg_ref.at[r], sg.at[sq], gl.at[2])

    mine = [[jnp.logical_and(side == c, sq == rows * side + r) for c in range(2)] for r in range(rows)]
    for r in range(rows):
        for c in range(2):
            split(
                mine[r][c],
                lambda r=r: s_local(r).start(),
                lambda r=r, c=c: s_copy(r, c, sq, (pair + c, rows * side + r)).start(),
            )
    for r in range(rows):
        at = half * spread + spot
        split(
            stays[r],
            lambda r=r, at=at: x_local(r, at).start(),
            lambda r=r, at=at: x_copy(r, spot, (pair + half, rows * side + r), at).start(),
        )

    def token_block(which):
        return pl.ds(pl.multiple_of(which, tokens), tokens)

    def cols(i, n=256):
        return pl.ds(pl.multiple_of(i * n, 128), n)

    def arrive(b):
        split(
            jnp.logical_and(sq // rows == side, 2 * b + side == sq),
            lambda: x_local(0, side * spread + b).wait(),
            lambda: x_copy(0, b, sibling, side * spread + b).wait_recv(),
        )
        forward(b, side * spread).start()

    def project(b, of, also_query):
        at = block(of * spread + b)

        def body(i, _):
            xb = xf[at]
            c = cols(i)
            if also_query:
                qs[block(b), c] = (product(xb, wproj[0, :, c]) + bq[:, c]).astype(BF16) * BF16(0.125)
            key[at, c] = product(xb, wproj[1, :, c]).astype(BF16)
            val[at, c] = (product(xb, wproj[2, :, c]) + bv[:, c]).astype(BF16)
            return 0

        lax.fori_loop(0, D // 256, body, 0, unroll=3)

    arrive(near)
    for name in ("vectors", "q", "k", "v"):
        loaded(name)
    project(near, side, True)
    forward(near, (1 - side) * spread).wait_recv()
    project(near, 1 - side, False)

    for p in range(seq_size):
        split(
            jnp.logical_and(sq // rows == side, p == sq),
            lambda: s_local(0).wait(),
            lambda p=p: s_copy(0, 0, p, sibling).wait_recv(),
        )
    diagonal = lax.broadcasted_iota(jnp.int32, (length, length), 0) == lax.broadcasted_iota(
        jnp.int32, (length, length), 1
    )
    for b in range(spread):
        mine_seg = jnp.broadcast_to(sg[2 * b + side], (length, length))
        column = jnp.sum(jnp.where(diagonal, mine_seg, 0), axis=1, keepdims=True)
        for p in range(seq_size):
            at = (p % 2) * spread + p // 2
            seen = jnp.broadcast_to(column, (length, length)) == jnp.broadcast_to(sg[p], (length, length))
            mask[b * length : (b + 1) * length, at * length : (at + 1) * length] = jnp.where(seen, 0.0, MASKED)

    arrive(1 - near)
    for r in range(rows):
        split(
            stays[r],
            lambda r=r: c_local(r, spot).start(),
            lambda r=r: c_copy(r, spot, (pair + half, rows * side + r)).start(),
        )
    project(1 - near, side, True)
    forward(1 - near, (1 - side) * spread).wait_recv()
    project(1 - near, 1 - side, False)

    lane = lax.broadcasted_iota(jnp.int32, (1, 128), 1)
    first = (lane < HD).astype(BF16)
    picks = (first, BF16(1.0) - first)
    low_lanes = lane < HD

    def attend(i, _):
        c = cols(i, 128)
        qp, kp, vp = qs[:, c], key[:, c], val[:, c]
        both = jnp.concatenate([qp * picks[0], qp * picks[1]], axis=0)
        s = product_nt(both, kp)
        for n in range(2):
            t = s[n * tokens : (n + 1) * tokens] + mask[...]
            e = jnp.exp(t - jnp.max(t, axis=-1, keepdims=True))
            probs[pl.ds(pl.multiple_of((2 * i + n) * tokens, tokens), tokens)] = (
                e * (1.0 / jnp.sum(e, axis=-1, keepdims=True))
            ).astype(BF16)
        out = product(probs[pl.ds(pl.multiple_of(2 * i * tokens, 2 * tokens), 2 * tokens)], vp)
        attn[:, c] = jnp.where(low_lanes, out[:tokens], out[tokens:]).astype(BF16)
        return 0

    lax.fori_loop(0, D // 128, attend, 0, unroll=3)

    loaded("o")

    def branch(i, _):
        c = cols(i)
        acc[:, c] = product(attn[...], wproj[3, :, c]) + bo[:, c] + xf[token_block(own), c].astype(F32)
        return 0

    lax.fori_loop(0, D // 256, branch, 0, unroll=3)
    step = 32

    def chunk(i):
        return pl.ds(pl.multiple_of(i * step, step), step)

    def norm_one(i, _):
        r = chunk(i)
        v = acc[r]
        centre = v - jnp.mean(v, axis=-1, keepdims=True)
        inv = lax.rsqrt(jnp.mean(centre * centre, axis=-1, keepdims=True) + EPSILON)
        n = centre * inv
        normed[r] = n
        inv1[r] = jnp.broadcast_to(inv, (step, 128))
        hid[r] = (n * g1[...] + s1[...]).astype(BF16)
        return 0

    lax.fori_loop(0, tokens // step, norm_one, 0, unroll=4)

    loaded("in")
    loaded("out")

    def inner_cols(j, i):
        return total.at[pl.ds(INNER + j * D, D), cols(i)]

    for j in range(4):

        def expand(i, _, j=j):
            c = cols(j * 3 + i)
            v = product(hid[...], inner_cols(j, i)[...]) + bi[:, c]
            cdf = 0.5 * (1.0 + lax.erf(v * INV_ROOT_TWO))
            active[:, c] = (v * cdf).astype(BF16)
            slope[:, c] = v
            return 0

        lax.fori_loop(0, 3, expand, 0, unroll=3)

    def contract(i, _):
        c = cols(i)
        acc[:, c] = product(active[...], total[pl.ds(PROJ, FF), c]) + b2[:, c]
        return 0

    lax.fori_loop(0, D // 256, contract, 0, unroll=3)
    for b in range(spread):
        split(comes[b], lambda b=b: c_local(b, b).wait(), lambda b=b: c_copy(0, b, sibling).wait_recv())

    small[0] = jnp.zeros((16, D), F32)

    def norm_two(i, carry):
        d_gain, d_shift, d_bias = carry
        r = chunk(i)
        v = normed[r] * g1[...] + s1[...] + acc[r]
        centre = v - jnp.mean(v, axis=-1, keepdims=True)
        inv = lax.rsqrt(jnp.mean(centre * centre, axis=-1, keepdims=True) + EPSILON)
        n = centre * inv
        ybuf[r] = (n * g2[...] + s2[...]).astype(BF16)
        g = cot[r].astype(F32)
        scaled = g * g2[...]
        grad = inv * (
            scaled - jnp.mean(scaled, axis=-1, keepdims=True) - n * jnp.mean(scaled * n, axis=-1, keepdims=True)
        )
        grad_low = grad.astype(BF16)
        gout[r] = grad_low
        acc[r] = grad
        return d_gain + fold(g * n), d_shift + fold(g), d_bias + fold(grad_low.astype(F32))

    zero = jnp.zeros((8, D), F32)
    sums = lax.fori_loop(0, tokens // step, norm_two, (zero, zero, zero), unroll=4)
    for at, v in zip((6, 7, 5), sums):
        small[0, at : at + 1] = jnp.sum(v, axis=0, keepdims=True)

    homes = [(pair + sq // rows, 2 * b + side) for b in range(spread)]
    at_home = [jnp.logical_and(h[0] == dp, h[1] == sq) for h in homes]

    def back(src, dst, b, lane_, to, slot):
        return pltpu.make_async_remote_copy(
            src.at[pl.ds(b * length, length)], dst.at[slot], ys.at[lane_, b], yr.at[lane_, slot], to, MESH
        )

    def home_local(src, dst, b, lane_):
        return pltpu.make_async_copy(src.at[pl.ds(b * length, length)], dst.at[sq % rows], xs.at[2 + lane_])

    def send_home(src, dst, lane_):
        for b in range(spread):
            split(
                at_home[b],
                lambda b=b: home_local(src, dst, b, lane_).start(),
                lambda b=b: back(src, dst, b, lane_, homes[b], sq % rows).start(),
            )

    def sent_home(src, dst, lane_):
        for b in range(spread):
            split(
                at_home[b],
                lambda b=b: home_local(src, dst, b, lane_).wait(),
                lambda b=b: back(src, dst, b, lane_, homes[b], sq % rows).wait_send(),
            )
        for r in range(rows):
            pl.when(jnp.logical_not(jnp.logical_and(half == side, sq == rows * side + r)))(
                lambda r=r: back(src, dst, 0, lane_, sibling, r).wait_recv()
            )

    send_home(ybuf, y_out, 0)


    bits = small_bits(plan.dp_size, seq_size)

    def small_copy(i):
        axis, bit = bits[i]
        if axis == "dp":
            tgt = (dp + bit * (1 - 2 * ((dp // bit) % 2)), sq)
        else:
            tgt = (dp, sq + bit * (1 - 2 * ((sq // bit) % 2)))
        return pltpu.make_async_remote_copy(small.at[i], small.at[len(bits) + 1 + i], ms.at[i], mr.at[i], tgt, MESH)

    def outer_part(n):
        def body(i, _):
            t = n * 2 + i
            total[pl.ds(pl.multiple_of(OUTER + t * 256, 256), 256)] = product(
                active[:, cols(t)].T, gout[...]
            ).astype(BF16)
            return 0

        lax.fori_loop(0, 2, body, 0, unroll=2)

    def inner_part(j):
        if j == 0:
            for i in range(3):
                hid_t[i * 256 : (i + 1) * 256] = hid[:, i * 256 : (i + 1) * 256].T

        def body(i, _):
            t = j * 3 + i
            up = product_nt(gout[...], total[pl.ds(pl.multiple_of(PROJ + t * 256, 256), 256)])
            v = slope[:, cols(t)]
            cdf = 0.5 * (1.0 + lax.erf(v * INV_ROOT_TWO))
            gi = (up * (cdf + v * DENSITY * jnp.exp(-0.5 * v * v))).astype(BF16)
            small[0, 8 + j : 9 + j, cols(i)] = jnp.sum(fold(gi.astype(F32)), axis=0, keepdims=True)
            view = inner_cols(j, i)
            acc[...] += product_nt(gi, view[...])
            view[...] = product(hid_t[...], gi).astype(BF16)
            return 0

        lax.fori_loop(0, 3, body, 0, unroll=3)

    def norm_one_part():
        def body(i, carry):
            d_gain, d_shift, d_bias = carry
            r = chunk(i)
            g, n = acc[r], normed[r]
            scaled = g * g1[...]
            grad = inv1[r][:, :1] * (
                scaled - jnp.mean(scaled, axis=-1, keepdims=True) - n * jnp.mean(scaled * n, axis=-1, keepdims=True)
            )
            grad_low = grad.astype(BF16)
            gout[r] = grad_low
            acc[r] = grad
            return d_gain + fold(g * n), d_shift + fold(g), d_bias + fold(grad_low.astype(F32))

        out = lax.fori_loop(0, tokens // step, body, (zero, zero, zero), unroll=2)
        for at, v in zip((3, 4, 2), out):
            small[0, at : at + 1] = jnp.sum(v, axis=0, keepdims=True)

    def branch_part():
        def body(i, _):
            total[pl.ds(pl.multiple_of(PROJ + i * 256, 256), 256)] = product(attn[:, cols(i)].T, gout[...]).astype(BF16)
            cot[:, cols(i)] = product_nt(gout[...], wproj[3, pl.ds(pl.multiple_of(i * 256, 256), 256)]).astype(BF16)
            return 0

        lax.fori_loop(0, D // 256, body, 0, unroll=3)

    def attention_part(n):
        def body(m, _):
            i = n * 2 + m
            c = cols(i, 128)
            qp, kp, vp, gp = qs[:, c], key[:, c], val[:, c], cot[:, c]
            queries = jnp.concatenate([qp * picks[0], qp * picks[1]], axis=0)
            grads = jnp.concatenate([gp * picks[0], gp * picks[1]], axis=0)
            p = probs[pl.ds(pl.multiple_of(2 * i * tokens, 2 * tokens), 2 * tokens)]
            pf = p.astype(F32)
            weighted = pf * product_nt(grads, vp)
            gs = (weighted - pf * jnp.sum(weighted, axis=-1, keepdims=True)).astype(BF16)
            dq = product(gs, kp)
            gq = (jnp.where(low_lanes, dq[:tokens], dq[tokens:]) * 0.125).astype(BF16)
            gk = product_tn(gs, queries).astype(BF16)
            gv = product_tn(p, grads).astype(BF16)
            qs[:, c] = gq
            small[0, 0:1, c] = jnp.sum(fold(gq.astype(F32)), axis=0, keepdims=True)
            small[0, 1:2, c] = jnp.sum(fold(gv.astype(F32)), axis=0, keepdims=True)
            for b in range(2):
                active[:, cols(b * 6 + i, 128)] = gk[b * tokens : (b + 1) * tokens]
                active[:, cols(12 + b * 6 + i, 128)] = gv[b * tokens : (b + 1) * tokens]
            return 0

        lax.fori_loop(0, 2, body, 0, unroll=2)
        if n == 2:
            small_copy(0).start()

    def query_part():
        def body(i, _):
            total[pl.ds(pl.multiple_of(PROJ + D + i * 256, 256), 256)] = product(
                xf[token_block(own), cols(i)].T, qs[...]
            ).astype(BF16)
            return 0

        lax.fori_loop(0, D // 256, body, 0, unroll=3)

    def key_part():
        def body(i, _):
            left = xf[pl.ds(0, tokens), cols(i)].T
            right = xf[pl.ds(tokens, tokens), cols(i)].T
            for n in range(2):
                base = n * 2 * D
                total[pl.ds(pl.multiple_of(PROJ + (2 + n) * D + i * 256, 256), 256)] = (
                    product(left, active[:, base : base + D]) + product(right, active[:, base + D : base + 2 * D])
                ).astype(BF16)
            return 0

        lax.fori_loop(0, D // 256, body, 0, unroll=3)

    dx_send = pltpu.make_async_remote_copy(hid, dx_far, xs.at[0], xs.at[1], sibling, MESH)

    def input_part():
        def both(s, w):
            return product_nt(active[:, pl.ds(pl.multiple_of(s * D, 128), D)], wproj[1, w]) + product_nt(
                active[:, pl.ds(pl.multiple_of((2 + s) * D, 128), D)], wproj[2, w]
            )

        def body(i, _):
            w = pl.ds(pl.multiple_of(i * 256, 256), 256)
            hid[:, cols(i)] = both(1 - side, w).astype(BF16)
            acc[:, cols(i)] += product_nt(qs[...], wproj[0, w]) + both(side, w)
            return 0

        lax.fori_loop(0, D // 256, body, 0, unroll=3)
        dx_send.start()

    def input_end():
        dx_send.wait_recv()

        def body(i, _):
            r = chunk(i)
            gout[r] = (acc[r] + dx_far[r].astype(F32)).astype(BF16)
            return 0

        lax.fori_loop(0, tokens // step, body, 0)
        send_home(gout, dx_out, 1)

    def small_part(n):
        for i in range(n, n + 1 if n < SMALL_PARTS - 1 else len(bits)):
            small_copy(i).wait_recv()
            small[i + 1] = small[i] + small[len(bits) + 1 + i]
            if i + 1 < len(bits):
                small_copy(i + 1).start()

    parts = (
        [functools.partial(outer_part, n) for n in range(6)]
        + [functools.partial(inner_part, j) for j in range(4)]
        + [norm_one_part, branch_part]
        + [functools.partial(attention_part, n) for n in range(3)]
        + [query_part, key_part, input_part, input_end]
        + [functools.partial(small_part, n) for n in range(SMALL_PARTS)]
    )
    ready = {n: (n,) for n in range(6)}
    ready.update({6: (6,), 7: (7, 8), 8: (9,), 9: (10, 11), 11: (12,), 15: (13, 14), 16: (15, 16, 17)})
    scripts = [iter(plan.script(p)) for p in plan.pieces]
    for entry in ORDER:
        if entry >= 0:
            next(scripts[entry])[1]()
            continue
        parts[-entry - 1]()
        for n in ready.get(-entry - 1, ()):
            plan.rs_start(plan.pieces[n], 0)
    small_out[...] = small[len(bits)]
    for i in range(len(bits)):
        small_copy(i).wait_send()
    dx_send.wait_send()
    sent_home(ybuf, y_out, 0)
    sent_home(gout, dx_out, 1)
    for r in range(rows):
        for c in range(2):
            pl.when(jnp.logical_not(mine[r][c]))(lambda r=r, c=c: s_copy(r, c, sq, sibling).wait_send())
        pl.when(jnp.logical_not(stays[r]))(lambda r=r: x_copy(r, spot, sibling, 0).wait_send())
        pl.when(jnp.logical_not(stays[r]))(lambda r=r: c_copy(r, spot, sibling).wait_send())
    for b in range(spread):
        forward(b, side * spread).wait_send()
    plan.finish()


def whole_layer(args, dp_size, seq_size):
    (layer_input, segment_ids, w_query, b_query, w_key, w_value, b_value, w_out, b_out, gain_one, shift_one,
     w_inner, b_inner, w_outer, b_outer, gain_two, shift_two, cotangent) = args
    plan = Exchange(dp_size, seq_size, 6)
    rows, length, width = layer_input.shape
    tokens = seq_size * length // 2
    vmem, anyw = pl.BlockSpec(memory_space=pltpu.VMEM), pl.BlockSpec(memory_space=pl.ANY)
    nbits = len(small_bits(dp_size, seq_size))
    back = pltpu.VMEM((rows, length, width), BF16)
    dma = pltpu.SemaphoreType.DMA
    vectors = (b_query, b_value, b_out, gain_one, shift_one, b_inner, b_outer, gain_two, shift_two)
    return pl.pallas_call(
        functools.partial(layer_kernel, plan, seq_size),
        out_shape=(pltpu.VMEM((3 * FF, D), BF16), pltpu.VMEM((16, D), F32), back, back),
        in_specs=[anyw] * 18,
        out_specs=(vmem,) * 4,
        scratch_shapes=[
            pltpu.VMEM((3 * FF, D), BF16),
            pltpu.VMEM((plan.slots, D), BF16),
            pltpu.VMEM((4, D, D), BF16),
            pltpu.VMEM((2 * tokens, D), BF16),
            pltpu.VMEM((tokens, D), BF16),
            pltpu.VMEM((2 * tokens, D), BF16),
            pltpu.VMEM((2 * tokens, D), BF16),
            pltpu.VMEM((D // HD * tokens, 2 * tokens), BF16),
            pltpu.VMEM((tokens, D), BF16),
            pltpu.VMEM((tokens, D), F32),
            pltpu.VMEM((tokens, 128), F32),
            pltpu.VMEM((tokens, D), BF16),
            pltpu.VMEM((D, tokens), BF16),
            pltpu.VMEM((tokens, FF), BF16),
            pltpu.VMEM((tokens, FF), F32),
            pltpu.VMEM((tokens, D), BF16),
            pltpu.VMEM((tokens, D), BF16),
            pltpu.VMEM((tokens, D), BF16),
            pltpu.VMEM((tokens, D), F32),
            pltpu.VMEM((tokens, 2 * tokens), F32),
            pltpu.VMEM((seq_size, 1, length), jnp.int32),
            pltpu.VMEM((tokens, D), BF16),
            pltpu.VMEM((2 * nbits + 1, 16, D), F32),
            dma((2 * len(LANES) + 1,)), dma((plan.sems,)),
            dma((5, 2)), dma((4, seq_size)), dma((3,)), dma((18,)),
            dma((nbits,)), dma((nbits,)), dma((2, 2)), dma((2, 2)), dma((4,)),
        ]
        + [pltpu.VMEM(v.shape, F32) for v in vectors],
        compiler_params=pltpu.CompilerParams(collective_id=1, has_side_effects=True, vmem_limit_bytes=VMEM_LIMIT),
        name="layer",
    )(
        layer_input, cotangent, segment_ids.reshape(rows, 1, length), w_query, w_key, w_value, w_out, w_inner, w_outer,
        *vectors,
    )


VMEM_LIMIT = 46 << 20


def widen_kernel(sums, small, y_in, dx_in, *refs):
    outs, (wide, sem, far) = refs[:17], refs[17:]
    (y, dx, d_query, d_b_query, d_key, d_value, d_b_value, d_out, d_b_out, d_gain_one, d_shift_one, d_inner,
     d_b_inner, d_outer, d_b_outer, d_gain_two, d_shift_two) = outs
    rows = [pltpu.make_async_copy(y_in, y, far.at[0]), pltpu.make_async_copy(dx_in, dx, far.at[1])]
    for c in rows:
        c.start()
    for i, o in enumerate((d_b_query, d_b_value, d_b_out, d_gain_one, d_shift_one, d_b_outer, d_gain_two, d_shift_two)):
        o[...] = small[i]
    for j in range(4):
        d_b_inner[j * D : (j + 1) * D] = small[8 + j]
    step = 384
    copies = []
    for n in range(3 * FF // step):
        at = n * step
        if at < INNER:
            view = d_outer.at[pl.ds(at, step)]
        elif at < PROJ:
            j, row = (at - INNER) // D, (at - INNER) % D
            view = d_inner.at[pl.ds(row, step), pl.ds(j * D, D)]
        else:
            j, row = (at - PROJ) // D, (at - PROJ) % D
            view = (d_out, d_query, d_key, d_value)[j].at[pl.ds(row, step)]
        slot = n % 4
        if n >= 4:
            copies[n - 4].wait()

        def body(i, _, at=at, slot=slot):
            wide[slot, pl.ds(pl.multiple_of(i * 32, 32), 32)] = sums[pl.ds(pl.multiple_of(at + i * 32, 32), 32)].astype(F32)
            return 0

        lax.fori_loop(0, step // 32, body, 0, unroll=4)
        copies.append(pltpu.make_async_copy(wide.at[slot], view, sem.at[slot]))
        copies[-1].start()
    for c in copies[-4:] + rows:
        c.wait()


def widen(sums, small, y, dx):
    vmem, anyw = pl.BlockSpec(memory_space=pltpu.VMEM), pl.BlockSpec(memory_space=pl.ANY)
    back = jax.ShapeDtypeStruct(y.shape, BF16)
    square, vector = jax.ShapeDtypeStruct((D, D), F32), jax.ShapeDtypeStruct((D,), F32)
    shapes = (
        back, back, square, vector, square, square, vector, square, vector, vector, vector,
        jax.ShapeDtypeStruct((D, FF), F32), jax.ShapeDtypeStruct((FF,), F32), jax.ShapeDtypeStruct((FF, D), F32),
        vector, vector, vector,
    )
    return pl.pallas_call(
        widen_kernel,
        out_shape=shapes,
        in_specs=[vmem] * 4,
        out_specs=tuple(vmem if len(o.shape) == 1 else anyw for o in shapes),
        scratch_shapes=[
            pltpu.VMEM((4, 384, D), F32), pltpu.SemaphoreType.DMA((4,)), pltpu.SemaphoreType.DMA((2,)),
        ],
        compiler_params=pltpu.CompilerParams(vmem_limit_bytes=16 << 20),
        name="widen",
    )(sums, small, y, dx)


def on_device(dp_size, seq_size, *args):
    return widen(*whole_layer(args, dp_size, seq_size))


def solution(mesh):
    sizes = (mesh.shape["dp"], mesh.shape["seq"])
    tokens = P("dp", "seq", None)
    return jax.shard_map(
        functools.partial(on_device, *sizes),
        mesh=mesh,
        in_specs=(tokens, P("dp", "seq")) + (P(),) * 15 + (tokens,),
        out_specs=(tokens, tokens) + (P(),) * 15,
        check_vma=False,
    )
```

```python
import functools

import jax
import jax.numpy as jnp
from jax import lax
from jax.experimental import pallas as pl
from jax.experimental.pallas import tpu as pltpu
from jax.sharding import PartitionSpec as P

HD = 64
EPSILON = 1e-12
MASKED = -1000000000.0
INV_ROOT_TWO = 0.7071067811865476
DENSITY = 0.3989422804014327
MESH = pl.DeviceIdType.MESH
BF16 = jnp.bfloat16
F32 = jnp.float32


def product(left, right):
    return jnp.dot(left, right, preferred_element_type=F32)


def product_tn(left, right):
    return lax.dot_general(left, right, (((0,), (0,)), ((), ())), preferred_element_type=F32)


def product_nt(left, right):
    return lax.dot_general(left, right, (((1,), (1,)), ((), ())), preferred_element_type=F32)


def place(seq_size):
    dp, sq = lax.axis_index("dp"), lax.axis_index("seq")
    side = dp % 2
    return dp, sq, side, dp - side


GROUP = 1536
PIECE = 512
ORDERS = (("yxz", "yxz", "zxy"), ("zyx", "xyz", "xyz"), ("yxz", "xzy", "yxz"), ("zxy", "xyz", "xyz"), ("yzx", "xyz", "yxz"), ("yzx", "xyz", "yxz"))
SUBS = 1
LANES = "cxyz"


class Exchange:
    def __init__(self, dp_size, seq_size, groups):
        self.dp_size, self.seq_size, self.groups = dp_size, seq_size, groups
        self.extra = []
        bit = 8
        while bit < dp_size:
            self.extra.append(bit)
            bit *= 2
        self.sems = 0
        self.slots = 0
        self.pieces = []
        for g in range(groups):
            for cls in range(3):
                self.pieces.append(self.plan(g * GROUP + cls * PIECE, ORDERS[g % len(ORDERS)][cls]))

    def sem(self):
        self.sems += 1
        return self.sems - 1

    def slot(self, rows):
        self.slots += rows
        return self.slots - rows

    def plan(self, base, order):
        stages, rows, ends = [], PIECE, False
        for axis in "c" + order:
            half = rows // 2
            st = dict(axis=axis, rows=half, ends=ends)
            if axis == "z":
                n = half // SUBS
                st["down"] = [dict(rs=self.sem(), ag=self.sem(), slot=self.slot(n), rows=n, at=i * n) for i in range(SUBS)]
                st["up"] = [dict(rs=self.sem(), ag=self.sem(), slot=self.slot(n), rows=n, at=i * n) for i in range(SUBS)]
                ends = True
            else:
                st.update(rs=self.sem(), ag=self.sem(), slot=None if axis == "c" else self.slot(half))
            stages.append(st)
            rows = half
        more = [dict(bit=b, rs=self.sem(), slot=self.slot(rows)) for b in self.extra]
        return dict(base=base, stages=stages, more=more, rows=rows)

    def bind(self, total, slots, final, send_sem, recv_sem):
        self.total, self.landing, self.final = total, slots, final
        self.ss, self.rs = send_sem, recv_sem
        dp, sq = lax.axis_index("dp"), lax.axis_index("seq")
        self.dp, self.sq = dp, sq
        self.bits = {"c": (1, dp % 2), "x": (2, (dp // 2) % 2), "y": (4, (dp // 4) % 2)}
        self.last = self.seq_size - 1
        self.edge = jnp.logical_or(sq == 0, sq == self.last)
        self.side = sq // self.last
        self.rows_sent = {}
        for p in self.pieces:
            off = p["base"]
            for st in p["stages"]:
                half = st["rows"]
                st["off"] = off
                value = self.side if st["axis"] == "z" else self.bits[st["axis"]][1]
                st["keep"] = off + value * half
                st["give"] = off + (1 - value) * half
                off = st["keep"]
            p["own"] = off

    def view(self, off, rows):
        return self.total.at[pl.ds(pl.multiple_of(off, 16), rows)]

    def partner(self, axis):
        bit, value = self.bits[axis]
        return (self.dp + bit * (1 - 2 * value), self.sq)

    def copy(self, src, dst, lane, sem, tgt):
        return pltpu.make_async_remote_copy(src, dst, self.ss.at[lane], self.rs.at[sem], tgt, MESH)

    def send(self, copy, lane, rows, who):
        copy.start()
        for place_ in who:
            self.rows_sent[lane, place_] = self.rows_sent.get((lane, place_), 0) + rows

    def everyone(self, st):
        return (0, self.last) if st["ends"] else range(self.seq_size)

    def gated(self, when, f):
        if when is None:
            f()
        else:
            pl.when(when)(f)

    def done(self, off, rows):
        return self.final.at[pl.ds(pl.multiple_of(off, 16), rows)]

    def landed(self, st):
        if st["slot"] is None:
            return self.done(st["give"], st["rows"])
        return self.landing.at[pl.ds(st["slot"], st["rows"])]

    def add(self, off, slot, rows, into=None):
        into = self.total if into is None else into
        source = self.final if slot is None else self.landing
        slot = off if slot is None else slot
        step = 32 if rows % 32 == 0 else 16

        def body(i, _):
            at = pl.multiple_of(off + i * step, 16)
            frm = pl.multiple_of(slot + i * step, 16)
            into[pl.ds(at, step)] = self.total[pl.ds(at, step)] + source[pl.ds(frm, step)]
            return 0

        lax.fori_loop(0, rows // step, body, 0)


    def rs_start(self, p, i):
        st = p["stages"][i]
        if st["axis"] == "z":
            for way, at, to, base in (("down", self.last, -1, 0), ("up", 0, 1, st["rows"])):
                when = self.sq == at

                def f(way=way, at=at, to=to, base=base):
                    for s in st[way]:
                        self.send(self.rs_copy(st, s, base, to), LANES.index("z"), s["rows"], (at,))
                self.gated(when, f)
        else:
            when = self.edge if st["ends"] else None

            def f():
                self.send(self.rs_pair(st), LANES.index(st["axis"]), st["rows"], self.everyone(st))
            self.gated(when, f)

    def rs_pair(self, st):
        return self.copy(
            self.view(st["give"], st["rows"]), self.landed(st), LANES.index(st["axis"]), st["rs"], self.partner(st["axis"])
        )

    def rs_hyper(self, p, i):
        st = p["stages"][i]

        def f():
            self.rs_pair(st).wait_recv()
            self.add(st["keep"], st["slot"], st["rows"], self.final if i + 1 == len(p["stages"]) else None)
        self.gated(self.edge if st["ends"] else None, f)

    def rs_hop(self, p, i, hop):
        st = p["stages"][i]
        for way, at, to, base in (("down", self.last - hop, -1, 0), ("up", hop, 1, st["rows"])):
            when = self.sq == at

            def f(way=way, at=at, to=to, base=base):
                for s in st[way]:
                    self.rs_copy(st, s, base, -to).wait_recv()
                    ended = hop == self.last and i + 1 == len(p["stages"])
                    self.add(st["off"] + base + s["at"], s["slot"], s["rows"], self.final if ended else None)
                    if hop < self.last:
                        self.send(self.rs_copy(st, s, base, to), LANES.index("z"), s["rows"], (at,))
            self.gated(when, f)

    def rs_copy(self, st, s, base, to):
        return self.copy(
            self.view(st["off"] + base + s["at"], s["rows"]), self.landing.at[pl.ds(s["slot"], s["rows"])],
            LANES.index("z"), s["rs"], (self.dp, self.sq + to),
        )

    def more(self, p):
        for m in p["more"]:
            bit = m["bit"]
            value = (self.dp // bit) % 2
            tgt = (self.dp + bit * (1 - 2 * value), self.sq)

            def f():
                c = self.copy(
                    self.done(p["own"], p["rows"]), self.landing.at[pl.ds(m["slot"], p["rows"])], len(LANES) * 2, m["rs"], tgt
                )
                c.start()
                c.wait()
                part = pl.ds(pl.multiple_of(p["own"], 16), p["rows"])
                self.final[part] = self.final[part] + self.landing[pl.ds(m["slot"], p["rows"])]
            self.gated(self.edge, f)


    def ag_start(self, p, i):
        st = p["stages"][i]
        if st["axis"] == "z":
            for way, at, to, base in (("down", self.last, -1, st["rows"]), ("up", 0, 1, 0)):
                when = self.sq == at

                def f(way=way, at=at, to=to, base=base):
                    for s in st[way]:
                        self.send(self.ag_copy(st, s, base, to), len(LANES) + LANES.index("z"), s["rows"], (at,))
                self.gated(when, f)
        else:
            when = self.edge if st["ends"] else None

            def f():
                self.send(
                    self.ag_pair(st, st["keep"]), len(LANES) + LANES.index(st["axis"]), st["rows"], self.everyone(st)
                )
            self.gated(when, f)

    def ag_copy(self, st, s, base, to):
        part = self.done(st["off"] + base + s["at"], s["rows"])
        return self.copy(part, part, len(LANES) + LANES.index("z"), s["ag"], (self.dp, self.sq + to))

    def ag_pair(self, st, off):
        part = self.done(off, st["rows"])
        return self.copy(part, part, len(LANES) + LANES.index(st["axis"]), st["ag"], self.partner(st["axis"]))

    def ag_hyper(self, p, i):
        st = p["stages"][i]

        def f():
            self.ag_pair(st, st["give"]).wait_recv()
        self.gated(self.edge if st["ends"] else None, f)

    def ag_hop(self, p, i, hop):
        st = p["stages"][i]
        for way, at, to, base in (("down", self.last - hop, -1, st["rows"]), ("up", hop, 1, 0)):
            when = self.sq == at

            def f(way=way, at=at, to=to, base=base):
                for s in st[way]:
                    self.ag_copy(st, s, base, -to).wait_recv()
                    if hop < self.last:
                        self.send(self.ag_copy(st, s, base, to), len(LANES) + LANES.index("z"), s["rows"], (at,))
            self.gated(when, f)

    def script(self, p):
        steps, n = [], len(p["stages"])
        for i, st in enumerate(p["stages"]):
            after = (lambda i=i: self.rs_start(p, i + 1)) if i + 1 < n else (lambda: (self.more(p), self.ag_start(p, n - 1)))
            if st["axis"] == "z":
                for hop in range(1, self.last + 1):
                    def step(i=i, hop=hop, after=after):
                        self.rs_hop(p, i, hop)
                        if hop == self.last:
                            after()
                    steps.append((f"rz{hop}", step))
            else:
                def step(i=i, after=after):
                    self.rs_hyper(p, i)
                    after()
                steps.append(("r" + st["axis"], step))
        for i in reversed(range(n)):
            st = p["stages"][i]
            after = (lambda i=i: self.ag_start(p, i - 1)) if i > 0 else (lambda: None)
            if st["axis"] == "z":
                for hop in range(1, self.last + 1):
                    def step(i=i, hop=hop, after=after):
                        self.ag_hop(p, i, hop)
                        if hop == self.last:
                            after()
                    steps.append((f"gz{hop}", step))
            else:
                def step(i=i, after=after):
                    self.ag_hyper(p, i)
                    after()
                steps.append(("g" + st["axis"], step))
        return steps

    def finish(self):
        for lane in range(2 * len(LANES)):
            rows = [self.rows_sent[lane, p] for p in range(self.seq_size)]

            def f(n, lane=lane):
                self.copy(self.total.at[pl.ds(0, n)], self.total.at[pl.ds(0, n)], lane, 0, self.partner("c")).wait_send()

            if min(rows) == max(rows):
                f(rows[0])
            else:
                for p in range(self.seq_size):
                    pl.when(self.sq == p)(functools.partial(f, rows[p]))


def small_bits(dp_size, seq_size):
    out, bit = [], 1
    while bit < dp_size:
        out.append(("dp", bit))
        bit *= 2
    bit = 1
    while bit < seq_size:
        out.append(("seq", bit))
        bit *= 2
    return out


D = 768
FF = 3072
OUTER, INNER, PROJ = 0, 3072, 6144
ORDER = (
    -1, -2, -3, -4, 0, -5, -6, 1, -7, 3, 2, 4, -8, 6, 5, 0, -9, 7, 8, -10, 1, 3, 4, 9,
    -11, -12, 10, 11, -13, 6, 5, 2, 0, 12, -14, 3, 9, 8, -15, 4, 7, 0, -16, 1, 5, 2, -17, 13,
    4, 3, 14, -18, 7, 9, 15, 12, 16, 0, 1, 10, 17, 4, 5, -19, -20, 3, 2, 11, 7, 12, 1, 6,
    5, 9, 14, 0, 8, 4, 15, 13, 6, 10, 0, 8, 4, 16, 12, 7, -21, 17, 15, 6, 1, 3, 10, 0,
    5, 11, 8, 2, 4, 12, 13, 1, 6, 9, 5, 15, 0, 16, 11, 10, 8, 7, 13, 14, 1, 4, -22, 6,
    5, 2, 17, 16, 11, 15, 3, 8, 9, 13, 10, 7, 14, 12, 6, 1, 16, -23, 17, 4, 0, 8, 5, 15,
    10, 2, 14, 11, 12, 13, 3, 7, 6, 9, -24, 1, 17, 16, 10, 11, 8, 14, 12, 7, 17, 4, 0, 13,
    11, 10, 15, 4, 5, 0, 2, 12, 7, 3, 13, 11, 6, 16, 1, 14, 9, 17, 12, 1, 10, 13, 8, 15,
    11, 3, 16, 14, 5, 2, 17, 6, 5, 15, 6, 3, 7, 9, 16, 3, 12, 14, 7, 17, 2, 12, 13, 10,
    15, 10, 9, 8, 11, 2, 8, 16, 11, 14, 2, 17, 9, 15, 9, 15, 13, 14, 13, 14, 16, 17, 16, 17,
)


SMALL_PARTS = 5


class Row:
    def __init__(self, ref):
        self.ref = ref

    def __getitem__(self, at):
        return (self.ref[...] if at is Ellipsis else self.ref[at[1]]).reshape(1, -1)


def fold(values):
    return jnp.sum(values.reshape(values.shape[0] // 8, 8, values.shape[1]), axis=0)


def layer_kernel(plan, seq_size, *refs):
    x_ref, cot_ref, seg_ref, wq_hbm, wk_hbm, wv_hbm, wo_hbm, win_hbm, wout_hbm = refs[:9]
    vectors_hbm, vectors = refs[9:18], refs[-9:]
    final, small_out, y_out, dx_out = refs[18:22]
    (total, landing, wproj, xf, qs, key, val, probs, attn, normed, inv1, hid, hid_t, active, slope, cot, ybuf, gout, acc,
     mask, sg, dx_far, small, ss, rs, gs_, gr, gl, ws, ms, mr, ys, yr, xs) = refs[22:-9]
    plan.bind(total, landing, final, ss, rs)
    bq, bv, bo, g1, s1, bi, b2, g2, s2 = (Row(v) for v in vectors)
    dp, sq, side, pair = place(seq_size)
    sibling = (dp + 1 - 2 * side, sq)
    rows, length = x_ref.shape[0], x_ref.shape[1]
    spread = seq_size // 2
    tokens = spread * length
    own, far = side * tokens, (1 - side) * tokens

    barrier = pltpu.get_barrier_semaphore()
    column = [(pair + c, p) for p in range(seq_size) for c in range(2)]
    for to in column:
        pl.when(jnp.logical_not(jnp.logical_and(to[0] == dp, to[1] == sq)))(
            lambda to=to: pl.semaphore_signal(barrier, inc=1, device_id=to, device_id_type=MESH)
        )
    across = [bit for axis, bit in small_bits(plan.dp_size, seq_size) if axis == "dp" and bit > 1]
    for bit in across:
        to = (dp + bit * (1 - 2 * ((dp // bit) % 2)), sq)
        pl.semaphore_signal(barrier, inc=1, device_id=to, device_id_type=MESH)

    loads = {}

    def load(name, src, dst, i):
        loads.setdefault(name, []).append(pltpu.make_async_copy(src, dst, ws.at[i]))
        loads[name][-1].start()

    for i, (name, src) in enumerate((("q", wq_hbm), ("k", wk_hbm), ("v", wv_hbm), ("o", wo_hbm))):
        load(name, src, wproj.at[i], i)
    for i, (src, dst) in enumerate(zip(vectors_hbm, vectors)):
        load("vectors", src, dst, 9 + i)
    for j in range(4):
        load("in", win_hbm.at[:, pl.ds(j * D, D)], total.at[pl.ds(INNER + j * D, D)], 4 + j)
    load("out", wout_hbm, total.at[pl.ds(PROJ, FF)], 8)

    def loaded(name):
        for c in loads[name]:
            c.wait()

    pl.semaphore_wait(barrier, len(column) - 1 + len(across))

    half, spot = sq % 2, sq // 2
    near = sq // 2

    def block(i):
        return pl.ds(pl.multiple_of(i * length, length), length)

    def x_copy(r, b, tgt, at):
        return pltpu.make_async_remote_copy(x_ref.at[r], xf.at[block(at)], gs_.at[0, r], gr.at[0, b], tgt, MESH)

    def c_copy(r, b, tgt):
        return pltpu.make_async_remote_copy(cot_ref.at[r], cot.at[block(b)], gs_.at[1, r], gr.at[1, b], tgt, MESH)

    def s_copy(r, c, at, tgt):
        return pltpu.make_async_remote_copy(seg_ref.at[r], sg.at[at], gs_.at[2 + c, r], gr.at[2, at], tgt, MESH)

    def forward(b, base):
        part = xf.at[block(base + b)]
        return pltpu.make_async_remote_copy(part, part, gs_.at[4, b], gr.at[3, b], sibling, MESH)

    def split(local, near, remote):
        pl.when(local)(near)
        pl.when(jnp.logical_not(local))(remote)

    stays = [jnp.logical_and(half == side, sq == rows * side + r) for r in range(rows)]
    comes = [jnp.logical_and(sq // rows == side, 2 * b + side == sq) for b in range(spread)]

    def x_local(r, at):
        return pltpu.make_async_copy(x_ref.at[r], xf.at[block(at)], gl.at[0])

    def c_local(r, at):
        return pltpu.make_async_copy(cot_ref.at[r], cot.at[block(at)], gl.at[1])

    def s_local(r):
        return pltpu.make_async_copy(seg_ref.at[r], sg.at[sq], gl.at[2])

    mine = [[jnp.logical_and(side == c, sq == rows * side + r) for c in range(2)] for r in range(rows)]
    for r in range(rows):
        for c in range(2):
            split(
                mine[r][c],
                lambda r=r: s_local(r).start(),
                lambda r=r, c=c: s_copy(r, c, sq, (pair + c, rows * side + r)).start(),
            )
    for r in range(rows):
        at = half * spread + spot
        split(
            stays[r],
            lambda r=r, at=at: x_local(r, at).start(),
            lambda r=r, at=at: x_copy(r, spot, (pair + half, rows * side + r), at).start(),
        )

    def token_block(which):
        return pl.ds(pl.multiple_of(which, tokens), tokens)

    def cols(i, n=256):
        return pl.ds(pl.multiple_of(i * n, 128), n)

    def arrive(b):
        split(
            jnp.logical_and(sq // rows == side, 2 * b + side == sq),
            lambda: x_local(0, side * spread + b).wait(),
            lambda: x_copy(0, b, sibling, side * spread + b).wait_recv(),
        )
        forward(b, side * spread).start()

    def project(b, of, also_query):
        at = block(of * spread + b)

        def body(i, _):
            xb = xf[at]
            c = cols(i)
            if also_query:
                qs[block(b), c] = (product(xb, wproj[0, :, c]) + bq[:, c]).astype(BF16) * BF16(0.125)
            key[at, c] = product(xb, wproj[1, :, c]).astype(BF16)
            val[at, c] = (product(xb, wproj[2, :, c]) + bv[:, c]).astype(BF16)
            return 0

        lax.fori_loop(0, D // 256, body, 0, unroll=3)

    arrive(near)
    for name in ("vectors", "q", "k", "v"):
        loaded(name)
    project(near, side, True)
    forward(near, (1 - side) * spread).wait_recv()
    project(near, 1 - side, False)

    for p in range(seq_size):
        split(
            jnp.logical_and(sq // rows == side, p == sq),
            lambda: s_local(0).wait(),
            lambda p=p: s_copy(0, 0, p, sibling).wait_recv(),
        )
    diagonal = lax.broadcasted_iota(jnp.int32, (length, length), 0) == lax.broadcasted_iota(
        jnp.int32, (length, length), 1
    )
    for b in range(spread):
        mine_seg = jnp.broadcast_to(sg[2 * b + side], (length, length))
        column = jnp.sum(jnp.where(diagonal, mine_seg, 0), axis=1, keepdims=True)
        for p in range(seq_size):
            at = (p % 2) * spread + p // 2
            seen = jnp.broadcast_to(column, (length, length)) == jnp.broadcast_to(sg[p], (length, length))
            mask[b * length : (b + 1) * length, at * length : (at + 1) * length] = jnp.where(seen, 0.0, MASKED)

    arrive(1 - near)
    for r in range(rows):
        split(
            stays[r],
            lambda r=r: c_local(r, spot).start(),
            lambda r=r: c_copy(r, spot, (pair + half, rows * side + r)).start(),
        )
    project(1 - near, side, True)
    forward(1 - near, (1 - side) * spread).wait_recv()
    project(1 - near, 1 - side, False)

    lane = lax.broadcasted_iota(jnp.int32, (1, 128), 1)
    first = (lane < HD).astype(BF16)
    picks = (first, BF16(1.0) - first)
    low_lanes = lane < HD

    def attend(i, _):
        c = cols(i, 128)
        qp, kp, vp = qs[:, c], key[:, c], val[:, c]
        both = jnp.concatenate([qp * picks[0], qp * picks[1]], axis=0)
        s = product_nt(both, kp)
        for n in range(2):
            t = s[n * tokens : (n + 1) * tokens] + mask[...]
            e = jnp.exp(t - jnp.max(t, axis=-1, keepdims=True))
            probs[pl.ds(pl.multiple_of((2 * i + n) * tokens, tokens), tokens)] = (
                e * (1.0 / jnp.sum(e, axis=-1, keepdims=True))
            ).astype(BF16)
        out = product(probs[pl.ds(pl.multiple_of(2 * i * tokens, 2 * tokens), 2 * tokens)], vp)
        attn[:, c] = jnp.where(low_lanes, out[:tokens], out[tokens:]).astype(BF16)
        return 0

    lax.fori_loop(0, D // 128, attend, 0, unroll=6)

    loaded("o")

    def branch(i, _):
        c = cols(i)
        acc[:, c] = product(attn[...], wproj[3, :, c]) + bo[:, c] + xf[token_block(own), c].astype(F32)
        return 0

    lax.fori_loop(0, D // 256, branch, 0, unroll=3)
    step = 32

    def chunk(i):
        return pl.ds(pl.multiple_of(i * step, step), step)

    def norm_one(i, _):
        r = chunk(i)
        v = acc[r]
        centre = v - jnp.mean(v, axis=-1, keepdims=True)
        inv = lax.rsqrt(jnp.mean(centre * centre, axis=-1, keepdims=True) + EPSILON)
        n = centre * inv
        normed[r] = n
        inv1[r] = jnp.broadcast_to(inv, (step, 128))
        hid[r] = (n * g1[...] + s1[...]).astype(BF16)
        return 0

    lax.fori_loop(0, tokens // step, norm_one, 0, unroll=4)

    loaded("in")
    loaded("out")

    def inner_cols(j, i):
        return total.at[pl.ds(INNER + j * D, D), cols(i)]

    for j in range(4):

        def expand(i, _, j=j):
            c = cols(j * 3 + i)
            v = product(hid[...], inner_cols(j, i)[...]) + bi[:, c]
            cdf = 0.5 * (1.0 + lax.erf(v * INV_ROOT_TWO))
            active[:, c] = (v * cdf).astype(BF16)
            slope[:, c] = v
            return 0

        lax.fori_loop(0, 3, expand, 0, unroll=3)

    def contract(i, _):
        c = cols(i)
        acc[:, c] = product(active[...], total[pl.ds(PROJ, FF), c]) + b2[:, c]
        return 0

    lax.fori_loop(0, D // 256, contract, 0, unroll=3)
    for b in range(spread):
        split(comes[b], lambda b=b: c_local(b, b).wait(), lambda b=b: c_copy(0, b, sibling).wait_recv())

    small[0] = jnp.zeros((16, D), F32)

    def norm_two(i, carry):
        d_gain, d_shift, d_bias = carry
        r = chunk(i)
        v = normed[r] * g1[...] + s1[...] + acc[r]
        centre = v - jnp.mean(v, axis=-1, keepdims=True)
        inv = lax.rsqrt(jnp.mean(centre * centre, axis=-1, keepdims=True) + EPSILON)
        n = centre * inv
        ybuf[r] = (n * g2[...] + s2[...]).astype(BF16)
        g = cot[r].astype(F32)
        scaled = g * g2[...]
        grad = inv * (
            scaled - jnp.mean(scaled, axis=-1, keepdims=True) - n * jnp.mean(scaled * n, axis=-1, keepdims=True)
        )
        grad_low = grad.astype(BF16)
        gout[r] = grad_low
        acc[r] = grad
        return d_gain + fold(g * n), d_shift + fold(g), d_bias + fold(grad_low.astype(F32))

    zero = jnp.zeros((8, D), F32)
    sums = lax.fori_loop(0, tokens // step, norm_two, (zero, zero, zero), unroll=4)
    for at, v in zip((6, 7, 5), sums):
        small[0, at : at + 1] = jnp.sum(v, axis=0, keepdims=True)

    homes = [(pair + sq // rows, 2 * b + side) for b in range(spread)]
    at_home = [jnp.logical_and(h[0] == dp, h[1] == sq) for h in homes]

    def back(src, dst, b, lane_, to, slot):
        return pltpu.make_async_remote_copy(
            src.at[pl.ds(b * length, length)], dst.at[slot], ys.at[lane_, b], yr.at[lane_, slot], to, MESH
        )

    def home_local(src, dst, b, lane_):
        return pltpu.make_async_copy(src.at[pl.ds(b * length, length)], dst.at[sq % rows], xs.at[2 + lane_])

    def send_home(src, dst, lane_):
        for b in range(spread):
            split(
                at_home[b],
                lambda b=b: home_local(src, dst, b, lane_).start(),
                lambda b=b: back(src, dst, b, lane_, homes[b], sq % rows).start(),
            )

    def sent_home(src, dst, lane_):
        for b in range(spread):
            split(
                at_home[b],
                lambda b=b: home_local(src, dst, b, lane_).wait(),
                lambda b=b: back(src, dst, b, lane_, homes[b], sq % rows).wait_send(),
            )
        for r in range(rows):
            pl.when(jnp.logical_not(jnp.logical_and(half == side, sq == rows * side + r)))(
                lambda r=r: back(src, dst, 0, lane_, sibling, r).wait_recv()
            )

    send_home(ybuf, y_out, 0)


    bits = small_bits(plan.dp_size, seq_size)

    def small_copy(i):
        axis, bit = bits[i]
        if axis == "dp":
            tgt = (dp + bit * (1 - 2 * ((dp // bit) % 2)), sq)
        else:
            tgt = (dp, sq + bit * (1 - 2 * ((sq // bit) % 2)))
        return pltpu.make_async_remote_copy(small.at[i], small.at[len(bits) + 1 + i], ms.at[i], mr.at[i], tgt, MESH)

    def outer_part(n):
        def body(i, _):
            t = n * 2 + i
            total[pl.ds(pl.multiple_of(OUTER + t * 256, 256), 256)] = product(
                active[:, cols(t)].T, gout[...]
            ).astype(BF16)
            return 0

        lax.fori_loop(0, 2, body, 0, unroll=2)

    def inner_part(j):
        if j == 0:
            for i in range(3):
                hid_t[i * 256 : (i + 1) * 256] = hid[:, i * 256 : (i + 1) * 256].T

        def body(i, _):
            t = j * 3 + i
            up = product_nt(gout[...], total[pl.ds(pl.multiple_of(PROJ + t * 256, 256), 256)])
            v = slope[:, cols(t)]
            cdf = 0.5 * (1.0 + lax.erf(v * INV_ROOT_TWO))
            gi = (up * (cdf + v * DENSITY * jnp.exp(-0.5 * v * v))).astype(BF16)
            small[0, 8 + j : 9 + j, cols(i)] = jnp.sum(fold(gi.astype(F32)), axis=0, keepdims=True)
            view = inner_cols(j, i)
            acc[...] += product_nt(gi, view[...])
            view[...] = product(hid_t[...], gi).astype(BF16)
            return 0

        lax.fori_loop(0, 3, body, 0, unroll=3)

    def norm_one_part():
        def body(i, carry):
            d_gain, d_shift, d_bias = carry
            r = chunk(i)
            g, n = acc[r], normed[r]
            scaled = g * g1[...]
            grad = inv1[r][:, :1] * (
                scaled - jnp.mean(scaled, axis=-1, keepdims=True) - n * jnp.mean(scaled * n, axis=-1, keepdims=True)
            )
            grad_low = grad.astype(BF16)
            gout[r] = grad_low
            acc[r] = grad
            return d_gain + fold(g * n), d_shift + fold(g), d_bias + fold(grad_low.astype(F32))

        out = lax.fori_loop(0, tokens // step, body, (zero, zero, zero), unroll=2)
        for at, v in zip((3, 4, 2), out):
            small[0, at : at + 1] = jnp.sum(v, axis=0, keepdims=True)

    def branch_part():
        def body(i, _):
            total[pl.ds(pl.multiple_of(PROJ + i * 256, 256), 256)] = product(attn[:, cols(i)].T, gout[...]).astype(BF16)
            cot[:, cols(i)] = product_nt(gout[...], wproj[3, pl.ds(pl.multiple_of(i * 256, 256), 256)]).astype(BF16)
            return 0

        lax.fori_loop(0, D // 256, body, 0, unroll=3)

    def attention_part(n):
        def body(m, _):
            i = n * 2 + m
            c = cols(i, 128)
            qp, kp, vp, gp = qs[:, c], key[:, c], val[:, c], cot[:, c]
            queries = jnp.concatenate([qp * picks[0], qp * picks[1]], axis=0)
            grads = jnp.concatenate([gp * picks[0], gp * picks[1]], axis=0)
            p = probs[pl.ds(pl.multiple_of(2 * i * tokens, 2 * tokens), 2 * tokens)]
            pf = p.astype(F32)
            weighted = pf * product_nt(grads, vp)
            gs = (weighted - pf * jnp.sum(weighted, axis=-1, keepdims=True)).astype(BF16)
            dq = product(gs, kp)
            gq = (jnp.where(low_lanes, dq[:tokens], dq[tokens:]) * 0.125).astype(BF16)
            gk = product_tn(gs, queries).astype(BF16)
            gv = product_tn(p, grads).astype(BF16)
            qs[:, c] = gq
            small[0, 0:1, c] = jnp.sum(fold(gq.astype(F32)), axis=0, keepdims=True)
            small[0, 1:2, c] = jnp.sum(fold(gv.astype(F32)), axis=0, keepdims=True)
            for b in range(2):
                active[:, cols(b * 6 + i, 128)] = gk[b * tokens : (b + 1) * tokens]
                active[:, cols(12 + b * 6 + i, 128)] = gv[b * tokens : (b + 1) * tokens]
            return 0

        lax.fori_loop(0, 2, body, 0, unroll=2)
        if n == 2:
            small_copy(0).start()

    def query_part():
        def body(i, _):
            total[pl.ds(pl.multiple_of(PROJ + D + i * 256, 256), 256)] = product(
                xf[token_block(own), cols(i)].T, qs[...]
            ).astype(BF16)
            return 0

        lax.fori_loop(0, D // 256, body, 0, unroll=3)

    def key_part():
        def body(i, _):
            left = xf[pl.ds(0, tokens), cols(i)].T
            right = xf[pl.ds(tokens, tokens), cols(i)].T
            for n in range(2):
                base = n * 2 * D
                total[pl.ds(pl.multiple_of(PROJ + (2 + n) * D + i * 256, 256), 256)] = (
                    product(left, active[:, base : base + D]) + product(right, active[:, base + D : base + 2 * D])
                ).astype(BF16)
            return 0

        lax.fori_loop(0, D // 256, body, 0, unroll=3)

    dx_send = pltpu.make_async_remote_copy(hid, dx_far, xs.at[0], xs.at[1], sibling, MESH)

    def input_part():
        def both(s, w):
            return product_nt(active[:, pl.ds(pl.multiple_of(s * D, 128), D)], wproj[1, w]) + product_nt(
                active[:, pl.ds(pl.multiple_of((2 + s) * D, 128), D)], wproj[2, w]
            )

        def body(i, _):
            w = pl.ds(pl.multiple_of(i * 256, 256), 256)
            hid[:, cols(i)] = both(1 - side, w).astype(BF16)
            acc[:, cols(i)] += product_nt(qs[...], wproj[0, w]) + both(side, w)
            return 0

        lax.fori_loop(0, D // 256, body, 0, unroll=3)
        dx_send.start()

    def input_end():
        dx_send.wait_recv()

        def body(i, _):
            r = chunk(i)
            gout[r] = (acc[r] + dx_far[r].astype(F32)).astype(BF16)
            return 0

        lax.fori_loop(0, tokens // step, body, 0)
        send_home(gout, dx_out, 1)

    def small_part(n):
        for i in range(n, n + 1 if n < SMALL_PARTS - 1 else len(bits)):
            small_copy(i).wait_recv()
            small[i + 1] = small[i] + small[len(bits) + 1 + i]
            if i + 1 < len(bits):
                small_copy(i + 1).start()

    parts = (
        [functools.partial(outer_part, n) for n in range(6)]
        + [functools.partial(inner_part, j) for j in range(4)]
        + [norm_one_part, branch_part]
        + [functools.partial(attention_part, n) for n in range(3)]
        + [query_part, key_part, input_part, input_end]
        + [functools.partial(small_part, n) for n in range(SMALL_PARTS)]
    )
    ready = {n: (n,) for n in range(6)}
    ready.update({6: (6,), 7: (7, 8), 8: (9,), 9: (10, 11), 11: (12,), 15: (13, 14), 16: (15, 16, 17)})
    scripts = [iter(plan.script(p)) for p in plan.pieces]
    for entry in ORDER:
        if entry >= 0:
            next(scripts[entry])[1]()
            continue
        parts[-entry - 1]()
        for n in ready.get(-entry - 1, ()):
            plan.rs_start(plan.pieces[n], 0)
    small_out[...] = small[len(bits)]
    for i in range(len(bits)):
        small_copy(i).wait_send()
    dx_send.wait_send()
    sent_home(ybuf, y_out, 0)
    sent_home(gout, dx_out, 1)
    for r in range(rows):
        for c in range(2):
            pl.when(jnp.logical_not(mine[r][c]))(lambda r=r, c=c: s_copy(r, c, sq, sibling).wait_send())
        pl.when(jnp.logical_not(stays[r]))(lambda r=r: x_copy(r, spot, sibling, 0).wait_send())
        pl.when(jnp.logical_not(stays[r]))(lambda r=r: c_copy(r, spot, sibling).wait_send())
    for b in range(spread):
        forward(b, side * spread).wait_send()
    plan.finish()


def whole_layer(args, dp_size, seq_size):
    (layer_input, segment_ids, w_query, b_query, w_key, w_value, b_value, w_out, b_out, gain_one, shift_one,
     w_inner, b_inner, w_outer, b_outer, gain_two, shift_two, cotangent) = args
    plan = Exchange(dp_size, seq_size, 6)
    rows, length, width = layer_input.shape
    tokens = seq_size * length // 2
    vmem, anyw = pl.BlockSpec(memory_space=pltpu.VMEM), pl.BlockSpec(memory_space=pl.ANY)
    nbits = len(small_bits(dp_size, seq_size))
    back = pltpu.VMEM((rows, length, width), BF16)
    dma = pltpu.SemaphoreType.DMA
    vectors = (b_query, b_value, b_out, gain_one, shift_one, b_inner, b_outer, gain_two, shift_two)
    return pl.pallas_call(
        functools.partial(layer_kernel, plan, seq_size),
        out_shape=(pltpu.VMEM((3 * FF, D), BF16), pltpu.VMEM((16, D), F32), back, back),
        in_specs=[anyw] * 18,
        out_specs=(vmem,) * 4,
        scratch_shapes=[
            pltpu.VMEM((3 * FF, D), BF16),
            pltpu.VMEM((plan.slots, D), BF16),
            pltpu.VMEM((4, D, D), BF16),
            pltpu.VMEM((2 * tokens, D), BF16),
            pltpu.VMEM((tokens, D), BF16),
            pltpu.VMEM((2 * tokens, D), BF16),
            pltpu.VMEM((2 * tokens, D), BF16),
            pltpu.VMEM((D // HD * tokens, 2 * tokens), BF16),
            pltpu.VMEM((tokens, D), BF16),
            pltpu.VMEM((tokens, D), F32),
            pltpu.VMEM((tokens, 128), F32),
            pltpu.VMEM((tokens, D), BF16),
            pltpu.VMEM((D, tokens), BF16),
            pltpu.VMEM((tokens, FF), BF16),
            pltpu.VMEM((tokens, FF), F32),
            pltpu.VMEM((tokens, D), BF16),
            pltpu.VMEM((tokens, D), BF16),
            pltpu.VMEM((tokens, D), BF16),
            pltpu.VMEM((tokens, D), F32),
            pltpu.VMEM((tokens, 2 * tokens), F32),
            pltpu.VMEM((seq_size, 1, length), jnp.int32),
            pltpu.VMEM((tokens, D), BF16),
            pltpu.VMEM((2 * nbits + 1, 16, D), F32),
            dma((2 * len(LANES) + 1,)), dma((plan.sems,)),
            dma((5, 2)), dma((4, seq_size)), dma((3,)), dma((18,)),
            dma((nbits,)), dma((nbits,)), dma((2, 2)), dma((2, 2)), dma((4,)),
        ]
        + [pltpu.VMEM(v.shape, F32) for v in vectors],
        compiler_params=pltpu.CompilerParams(collective_id=1, has_side_effects=True, vmem_limit_bytes=VMEM_LIMIT),
        name="layer",
    )(
        layer_input, cotangent, segment_ids.reshape(rows, 1, length), w_query, w_key, w_value, w_out, w_inner, w_outer,
        *vectors,
    )


VMEM_LIMIT = 46 << 20


def widen_kernel(sums, small, y_in, dx_in, *refs):
    outs, (wide, sem, far) = refs[:17], refs[17:]
    (y, dx, d_query, d_b_query, d_key, d_value, d_b_value, d_out, d_b_out, d_gain_one, d_shift_one, d_inner,
     d_b_inner, d_outer, d_b_outer, d_gain_two, d_shift_two) = outs
    rows = [pltpu.make_async_copy(y_in, y, far.at[0]), pltpu.make_async_copy(dx_in, dx, far.at[1])]
    for c in rows:
        c.start()
    for i, o in enumerate((d_b_query, d_b_value, d_b_out, d_gain_one, d_shift_one, d_b_outer, d_gain_two, d_shift_two)):
        o[...] = small[i]
    for j in range(4):
        d_b_inner[j * D : (j + 1) * D] = small[8 + j]
    step = 384
    copies = []
    for n in range(3 * FF // step):
        at = n * step
        if at < INNER:
            view = d_outer.at[pl.ds(at, step)]
        elif at < PROJ:
            j, row = (at - INNER) // D, (at - INNER) % D
            view = d_inner.at[pl.ds(row, step), pl.ds(j * D, D)]
        else:
            j, row = (at - PROJ) // D, (at - PROJ) % D
            view = (d_out, d_query, d_key, d_value)[j].at[pl.ds(row, step)]
        slot = n % 4
        if n >= 4:
            copies[n - 4].wait()

        def body(i, _, at=at, slot=slot):
            wide[slot, pl.ds(pl.multiple_of(i * 32, 32), 32)] = sums[pl.ds(pl.multiple_of(at + i * 32, 32), 32)].astype(F32)
            return 0

        lax.fori_loop(0, step // 32, body, 0, unroll=4)
        copies.append(pltpu.make_async_copy(wide.at[slot], view, sem.at[slot]))
        copies[-1].start()
    for c in copies[-4:] + rows:
        c.wait()


def widen(sums, small, y, dx):
    vmem, anyw = pl.BlockSpec(memory_space=pltpu.VMEM), pl.BlockSpec(memory_space=pl.ANY)
    back = jax.ShapeDtypeStruct(y.shape, BF16)
    square, vector = jax.ShapeDtypeStruct((D, D), F32), jax.ShapeDtypeStruct((D,), F32)
    shapes = (
        back, back, square, vector, square, square, vector, square, vector, vector, vector,
        jax.ShapeDtypeStruct((D, FF), F32), jax.ShapeDtypeStruct((FF,), F32), jax.ShapeDtypeStruct((FF, D), F32),
        vector, vector, vector,
    )
    return pl.pallas_call(
        widen_kernel,
        out_shape=shapes,
        in_specs=[vmem] * 4,
        out_specs=tuple(vmem if len(o.shape) == 1 else anyw for o in shapes),
        scratch_shapes=[
            pltpu.VMEM((4, 384, D), F32), pltpu.SemaphoreType.DMA((4,)), pltpu.SemaphoreType.DMA((2,)),
        ],
        compiler_params=pltpu.CompilerParams(vmem_limit_bytes=16 << 20),
        name="widen",
    )(sums, small, y, dx)


def on_device(dp_size, seq_size, *args):
    return widen(*whole_layer(args, dp_size, seq_size))


def solution(mesh):
    sizes = (mesh.shape["dp"], mesh.shape["seq"])
    tokens = P("dp", "seq", None)
    return jax.shard_map(
        functools.partial(on_device, *sizes),
        mesh=mesh,
        in_specs=(tokens, P("dp", "seq")) + (P(),) * 15 + (tokens,),
        out_specs=(tokens, tokens) + (P(),) * 15,
        check_vma=False,
    )
```
